32 devices in a mesh: group: 8 (over y, x, core), seq: 4 (over z).
Axes of the slice: x: 2, y: 2, z: 4, core: 2. Of those that a mesh axis runs over, the one named last changes fastest.
Arguments:
- latent: float32 [16, 1024, 64], P('group', 'seq'), may hold values from -6 to 6
- margin_len: int32 [15], replicated, may hold values from 1 to 512, 5760 in all
- in_weight: bfloat16 [64, 1536], replicated, may hold values from -0.75 to 0.75
- norm_gain: float32 [1536], replicated, may hold values from 0.1 to 1.9
- qkv_weight: bfloat16 [3, 1536, 1024], P(None, None, 'seq'), may hold values from -0.15625 to 0.15625
- out_weight: bfloat16 [1024, 1536], P('seq'), may hold values from -0.1875 to 0.1875
- final_gain: float32 [1536], replicated, may hold values from 0.1 to 1.9
- head_out: bfloat16 [1536, 64], replicated, may hold values from -0.15625 to 0.15625
Outputs:
- next_latent: float32 [16, 1024, 64], P('group', 'seq')
The draws below stay inside these ranges and needn't reach their ends.
Inputs may be any that keep to these rules, and one draw needn't show every extreme that they name: `margin_len`: the lengths sum to 15 * (384) and the largest is exactly 512.
All inputs are finite; a program needn't handle non-finite values.
Results may differ from the reference program's by a relative error of at most 0.0024.
Values may be sent and summed in bfloat16 or wider, within the bound.
No kernel may reach another device: no remote copies, remote signals or barrier semaphores. Data moves between devices by JAX's collectives and lax.ppermute only.
A program may use at most 128 MiB of HBM per device.

```python
import math
import jax
import jax.numpy as jnp
import numpy as np
from jax import lax

D = 1536
C = 64
HEADS = 16
HDIM = 64
CH = 1024
OVMAX = 512
NCH = 16
NOV = 15


def block_scale(rng, extent, cuts, least, largest):
    def one(axis_at, shards_of):
        heights = jax.random.uniform(jax.random.fold_in(jax.random.fold_in(rng, 6), axis_at), (shards_of,), jnp.float32, least / len(cuts), largest / len(cuts))
        return jnp.repeat(jnp.exp(heights), extent[axis_at] // shards_of).reshape((-1,) + (1,) * (len(extent) - axis_at - 1))

    level = one(*cuts[0])
    for cut in cuts[1:]:
        level = level * one(*cut)
    return level


def profile(count, total, limit, slope):
    loads = [(1 << 20) // math.isqrt(grade ** slope) + 1 for grade in range(2, count + 1)]
    spare, counts = total - limit - (count - 1), [1] * (count - 1)
    while spare > 0:
        candidates = [i for i in range(count - 1) if counts[i] < limit]
        pool, left = sum([loads[i] for i in candidates]), spare
        for i in candidates:
            addition = min(limit - counts[i], max(1, left * loads[i] // pool), spare)
            counts[i] = counts[i] + addition
            spare = spare - addition
    return np.array([limit] + counts)


def ragged_sizes(own_key, amount, total, limit, lean):
    if amount == 2:
        one = jax.random.randint(own_key, (), max(1, total - limit), min(limit, total - 1) + 1)
        return jnp.stack([one, total - one])
    tallies = jnp.asarray(profile(amount, total, limit, lean), jnp.int32)
    couples = (amount - 1) // 2
    donor, sink = tallies[1:1 + 2 * couples:2], tallies[2:2 + 2 * couples:2]
    margin = jnp.minimum(donor - 1, limit - sink)
    passed = jax.random.randint(jax.random.fold_in(own_key, 1), (couples,), 0, 1 << 20) % (margin + 1)
    tallies = tallies.at[1:1 + 2 * couples:2].set(donor - passed).at[2:2 + 2 * couples:2].set(sink + passed)
    return tallies[jax.random.permutation(jax.random.fold_in(own_key, 2), amount)]


def noise(rng, dims, scale, limit, cuts=(), kind=jnp.bfloat16):
    array = scale * jax.random.normal(rng, dims, jnp.float32)
    if cuts:
        array = array * block_scale(rng, dims, cuts, -0.22, 0.18)
    return jnp.clip(array, -limit, limit).astype(kind)


def setup_inputs(seed: int = 0) -> dict:
    keys = jax.random.split(jax.random.key(seed), 9)
    latent = noise(keys[0], (NCH, CH, C), 1.0, 6.0, ((0, 8), (1, 4)), jnp.float32)
    margin_len = ragged_sizes(keys[1], NOV, NOV * (3 * OVMAX // 4), OVMAX, 1).astype(jnp.int32)
    in_weight = noise(keys[2], (C, D), C ** -0.5, 0.75)
    norm_gain = jnp.clip(1.0 + 0.18 * jax.random.normal(keys[3], (D,), jnp.float32), 0.1, 1.9)
    qkv_weight = noise(keys[4], (3, D, HEADS * HDIM), D ** -0.5, 0.15625, ((2, 4),))
    out_weight = noise(keys[5], (HEADS * HDIM, D), (HEADS * HDIM) ** -0.5, 0.1875, ((0, 4),))
    final_gain = jnp.clip(1.0 + 0.18 * jax.random.normal(keys[6], (D,), jnp.float32), 0.1, 1.9)
    head_out = noise(keys[7], (D, C), D ** -0.5, 0.15625)
    return dict(latent=latent, margin_len=margin_len, in_weight=in_weight, norm_gain=norm_gain, qkv_weight=qkv_weight, out_weight=out_weight, final_gain=final_gain, head_out=head_out)


STEP = -0.5

def layer_norm(values_in, gain):
    row_mean = lax.optimization_barrier(jnp.mean(values_in, axis=-1, keepdims=True))
    centered = values_in - row_mean
    variance = lax.optimization_barrier(jnp.mean(centered * centered, axis=-1, keepdims=True))
    return centered / jnp.sqrt(variance + 1e-05) * gain.astype(jnp.float32)

def rms_heads(values_in):
    return values_in / jnp.sqrt(lax.optimization_barrier(jnp.mean(values_in * values_in, axis=-1, keepdims=True)) + 1e-06)

def node_block(window, key_count, in_weight, norm_gain, qkv_weight, out_weight, final_gain, head_out):
    tokens = window.shape[0]
    inputs = jnp.dot(window.astype(jnp.bfloat16), in_weight, preferred_element_type=jnp.float32)
    normed = layer_norm(inputs, norm_gain).astype(jnp.bfloat16)
    queries = jnp.dot(normed, qkv_weight[0], preferred_element_type=jnp.float32).reshape(tokens, HEADS, HDIM)
    keys_all = jnp.dot(normed, qkv_weight[1], preferred_element_type=jnp.float32).reshape(tokens, HEADS, HDIM)
    values = jnp.dot(normed, qkv_weight[2], preferred_element_type=jnp.float32).reshape(tokens, HEADS, HDIM)
    queries = rms_heads(queries).astype(jnp.bfloat16)
    keys_all = rms_heads(keys_all).astype(jnp.bfloat16)
    values = values.astype(jnp.bfloat16)
    scores = jnp.einsum('qhd,khd->hqk', queries.astype(jnp.float32), keys_all.astype(jnp.float32))
    key_mask = (jnp.arange(tokens) < key_count).astype(jnp.float32)
    exp_scores = jnp.exp(scores * HDIM ** (-0.5)) * key_mask[None, None, :]
    weights = (exp_scores / lax.optimization_barrier(jnp.sum(exp_scores, axis=-1, keepdims=True))).astype(jnp.bfloat16)
    attention = jnp.einsum('hqk,khd->qhd', weights.astype(jnp.float32), values.astype(jnp.float32))
    attention = attention.astype(jnp.bfloat16).reshape(tokens, HEADS * HDIM)
    mixed = inputs + jnp.dot(attention, out_weight, preferred_element_type=jnp.float32)
    final_norm = layer_norm(mixed, final_gain).astype(jnp.bfloat16)
    return jnp.dot(final_norm, head_out, preferred_element_type=jnp.float32)

def reference(latent, margin_len, in_weight, norm_gain, qkv_weight, out_weight, final_gain, head_out):
    flat_latent = latent.reshape(NCH * CH, C)
    padded_len = jnp.concatenate([margin_len.astype(jnp.int32), jnp.zeros((1,), jnp.int32)])
    own_len = (CH - padded_len).astype(jnp.int32)
    positions = jnp.arange(CH, dtype=jnp.int32)
    group_ids = jnp.arange(NCH, dtype=jnp.int32)
    group_rows = jnp.where(positions[None, :] < own_len[:, None], group_ids[:, None] * CH + positions[None, :], (group_ids[:, None] + 1) * CH + positions[None, :] - own_len[:, None]).astype(jnp.int32)
    over_ids = jnp.arange(NOV, dtype=jnp.int32)
    spots = jnp.arange(OVMAX, dtype=jnp.int32)
    over_rows = ((over_ids[:, None] + 1) * CH + spots[None, :]).astype(jnp.int32)

    def run_group(rows_here):
        return node_block(jnp.take(flat_latent, rows_here, axis=0), CH, in_weight, norm_gain, qkv_weight, out_weight, final_gain, head_out)

    def run_margin(pair):
        return node_block(jnp.take(flat_latent, pair[0], axis=0), pair[1], in_weight, norm_gain, qkv_weight, out_weight, final_gain, head_out)
    group_scores = lax.map(run_group, group_rows)
    over_scores = lax.map(run_margin, (over_rows, margin_len.astype(jnp.int32)))
    counted = (spots[None, :] < margin_len[:, None]).astype(jnp.float32)
    signed = -over_scores * counted[:, :, None]
    assembled = jnp.zeros((NCH * CH, C), jnp.float32)
    assembled = assembled.at[group_rows.reshape(-1)].add(group_scores.reshape(-1, C))
    assembled = assembled.at[over_rows.reshape(-1)].add(signed.reshape(-1, C))
    keep_rows = positions[None, :] < own_len[:, None]
    return jnp.where(keep_rows[:, :, None], latent + STEP * assembled.reshape(NCH, CH, C), jnp.float32(0.0))
```

```python
import functools

import jax
import jax.numpy as jnp
from jax import lax
from jax.experimental import pallas as pl
from jax.experimental.pallas import tpu as pltpu
from jax.sharding import PartitionSpec as P

HDIM = 64
OVMAX = 512
LANES = 128
STEP = -0.5
ROWS = 256
F32 = jnp.float32
BF16 = jnp.bfloat16


def iota(shape, dim):
    return lax.broadcasted_iota(jnp.int32, shape, dim)


def layer_norm(values_in, gain):
    row_mean = jnp.mean(values_in, axis=-1, keepdims=True)
    centered = values_in - row_mean
    variance = jnp.mean(centered * centered, axis=-1, keepdims=True)
    return centered * lax.rsqrt(variance + 1e-05) * gain


def matmul(lhs, rhs):
    return jnp.dot(lhs, rhs, preferred_element_type=F32)


def attend_kernel(count, slot_at, next_at, meta, *refs):
    slot_refs, refs = refs[:count], refs[count:]
    next_refs, refs = refs[:count], refs[count:]
    in_ref, gain_ref, qkv_ref, win_ref, att_ref, next_scr, q_scr, k_scr, v_scr = refs
    total, channels = win_ref.shape
    width = q_scr.shape[1]
    pairs = width // LANES
    share = total // count
    over_share = OVMAX // count
    low = total - OVMAX
    seq_pos = meta[0]
    over_len = meta[1]
    own = total - over_len

    for k in range(count):
        source = lax.rem(seq_pos + (count - k), count)
        at = pl.ds(pl.multiple_of(source * share, share), share)
        win_ref[at, :] = slot_refs[k][slot_at] if slot_at is not None else slot_refs[k][...]
        next_scr[at, :] = next_refs[k][next_at] if next_at is not None else next_refs[k][...]

    spot = iota((OVMAX, OVMAX), 0)
    column = iota((OVMAX, OVMAX), 1)
    is_own = spot + low < own
    pick_slot = jnp.where(is_own & (column == spot), 1.0, 0.0).astype(BF16)
    pick_next = jnp.where((~is_own) & (column == spot + low - own), 1.0, 0.0).astype(BF16)
    tail = matmul(pick_slot, win_ref[low:, :]) + matmul(pick_next, next_scr[:OVMAX, :])
    win_ref[low:, :] = tail.astype(BF16)

    one_head = iota((width, width), 0) // HDIM == iota((width, width), 1) // HDIM
    spread = jnp.where(one_head, 1.0 / HDIM, 0.0).astype(BF16)

    def rms(values_in):
        squares = values_in * values_in
        high = squares.astype(BF16)
        rest = (squares - high.astype(F32)).astype(BF16)
        return values_in * lax.rsqrt(matmul(high, spread) + matmul(rest, spread) + 1e-06)

    def project(step, carry):
        at = pl.ds(pl.multiple_of(step * ROWS, ROWS), ROWS)
        normed = layer_norm(matmul(win_ref[at, :], in_ref[...]), gain_ref[...]).astype(BF16)
        q_scr[at, :] = rms(matmul(normed, qkv_ref[0])).astype(BF16)
        k_scr[at, :] = rms(matmul(normed, qkv_ref[1])).astype(BF16)
        values = matmul(normed, qkv_ref[2])
        position = iota((ROWS, LANES), 0) + step * ROWS
        counted = (position >= jnp.minimum(own, total - 1)).astype(F32)
        left = iota((ROWS, LANES), 1) < HDIM
        weights_even = jnp.where(left, 1.0, counted)
        weights_odd = jnp.where(left, counted, 1.0)
        for pair in range(pairs):
            both = values[:, pair * LANES : (pair + 1) * LANES]
            turned = pltpu.roll(both, HDIM, 1) * counted
            v_scr[2 * pair, at, :LANES] = jnp.where(left, both, turned).astype(BF16)
            v_scr[2 * pair, at, LANES:] = weights_even.astype(BF16)
            v_scr[2 * pair + 1, at, :LANES] = jnp.where(left, turned, both).astype(BF16)
            v_scr[2 * pair + 1, at, LANES:] = weights_odd.astype(BF16)
        return carry

    lax.fori_loop(0, total // ROWS, project, 0)

    left = iota((ROWS, LANES), 1) < HDIM
    head_of = iota((ROWS, width), 1) // HDIM

    def one(queries, head):
        mine = jnp.where(head_of == head, queries, jnp.zeros_like(queries))
        scores = lax.dot_general(mine, k_scr[...], (((1,), (1,)), ((), ())), preferred_element_type=F32)
        weights = jnp.exp(scores * HDIM ** (-0.5)).astype(BF16)
        summed = matmul(weights, v_scr[head])
        return summed[:, :LANES] / summed[:, LANES:]

    for start in range(0, total, ROWS):
        queries = q_scr[start : start + ROWS, :]
        for pair in range(pairs):
            even = one(queries, 2 * pair)
            odd = one(queries, 2 * pair + 1)
            lanes = slice(pair * LANES, (pair + 1) * LANES)
            group_att = jnp.where(left, even, odd).astype(BF16)
            for part in range(0, ROWS, min(share, ROWS)):
                target, row = divmod(start + part, share)
                size = min(share, ROWS)
                k = lax.rem(target + count - seq_pos, count)
                att_ref[k, row : row + size, lanes] = group_att[part : part + size]
            if start >= low:
                over_att = pltpu.roll(jnp.where(left, odd, even), HDIM, 1).astype(BF16)
                for part in range(0, ROWS, min(over_share, ROWS)):
                    target, row = divmod(start - low + part, over_share)
                    size = min(over_share, ROWS)
                    k = lax.rem(target + count - seq_pos, count)
                    att_ref[k, share + row : share + row + size, lanes] = over_att[part : part + size]


def attend(count, meta, slot_pieces, slot_at, next_pieces, next_at, in_weight, gain, qkv):
    channels = in_weight.shape[0]
    share = slot_pieces[0].shape[-2]
    total = share * count
    width = qkv.shape[2]
    vmem = pl.BlockSpec(memory_space=pltpu.VMEM)
    flops = 2 * total * (in_weight.size + qkv.size) + 4 * total * total * width
    return pl.pallas_call(
        functools.partial(attend_kernel, count, slot_at, next_at),
        out_shape=(
            jax.ShapeDtypeStruct((total, channels), BF16),
            jax.ShapeDtypeStruct((count, share + OVMAX // count, width), BF16),
        ),
        in_specs=[pl.BlockSpec(memory_space=pltpu.SMEM)] + [vmem] * (2 * count + 3),
        out_specs=(vmem, vmem),
        scratch_shapes=[
            pltpu.VMEM((total, channels), BF16),
            pltpu.VMEM((total, width), BF16),
            pltpu.VMEM((total, width), BF16),
            pltpu.VMEM((width // HDIM, total, 2 * LANES), BF16),
        ],
        cost_estimate=pl.CostEstimate(
            flops=flops, bytes_accessed=2 * qkv.size, transcendentals=total * total * width // HDIM
        ),
        name="attend",
    )(meta, *slot_pieces, *next_pieces, in_weight, gain, qkv)


def finish_kernel(count, meta, *refs):
    att_refs, refs = refs[:count], refs[count:]
    win_ref, in_ref, out_ref, gain_ref, head_ref, score_ref = refs
    total = win_ref.shape[0]
    share = total // count
    over_share = OVMAX // count
    seq_pos = meta[0]
    own = total - meta[1]
    first_over = total - OVMAX + seq_pos * over_share
    group_at = pl.ds(pl.multiple_of(seq_pos * share, share), share)
    over_at = pl.ds(pl.multiple_of(first_over, over_share), over_share)
    for rows, at in (((0, share), group_at), ((share, share + over_share), over_at)):
        mixed = matmul(win_ref[at, :], in_ref[...])
        for k in range(count):
            mixed += matmul(att_refs[k][rows[0] : rows[1], :], out_ref[k])
        final = layer_norm(mixed, gain_ref[...]).astype(BF16)
        score = matmul(final, head_ref[...])
        if rows[0]:
            position = iota(score.shape, 0) + first_over
            score = jnp.where(position >= own, -score, 0.0)
        score_ref[rows[0] : rows[1], :] = score


def finish(count, meta, att_pieces, window, in_weight, full_out, gain, head_out):
    rows = att_pieces[0].shape[0]
    channels = in_weight.shape[0]
    vmem = pl.BlockSpec(memory_space=pltpu.VMEM)
    return pl.pallas_call(
        functools.partial(finish_kernel, count),
        out_shape=jax.ShapeDtypeStruct((rows, channels), F32),
        in_specs=[pl.BlockSpec(memory_space=pltpu.SMEM)] + [vmem] * (count + 5),
        out_specs=vmem,
        cost_estimate=pl.CostEstimate(
            flops=2 * rows * (full_out.size + 2 * in_weight.size), bytes_accessed=2 * full_out.size, transcendentals=0
        ),
        name="finish",
    )(meta, *att_pieces, window, in_weight, full_out, gain, head_out)


def combine_kernel(count, over_deltas, group_deltas, meta, latent_ref, first_ref, second_ref, *refs):
    lists = []
    for _ in range(2):
        lists.append((refs[: len(over_deltas)], refs[len(over_deltas) : len(over_deltas) + len(group_deltas)]))
        refs = refs[len(over_deltas) + len(group_deltas) :]
    out_ref, tail_scr = refs
    share = latent_ref.shape[1]
    over_share = OVMAX // count
    total = share * count
    seq_pos = meta[0]
    for slot, head_ref in enumerate((first_ref, second_ref)):
        own = total - meta[1 + slot]
        own_own = total - meta[2 + slot]
        over_refs, group_refs = lists[slot]
        tail_scr[...] = jnp.zeros_like(tail_scr)
        for delta, ref in zip(group_deltas, group_refs):
            row = (seq_pos + delta) * share - (total - OVMAX)
            tail_scr[pl.ds(pl.multiple_of(row, share), share), :] = ref[...]
        for delta, ref in zip(over_deltas, over_refs):
            at = pl.ds(pl.multiple_of((seq_pos + delta) * over_share, over_share), over_share)
            tail_scr[at, :] = tail_scr[at, :] + ref[...]
        moved = tail_scr[pl.ds(own - (total - OVMAX) + seq_pos * share, share), :]
        score = head_ref[:share, :] + moved
        keep = iota(score.shape, 0) + seq_pos * share < own_own
        out_ref[slot] = jnp.where(keep, latent_ref[slot] + STEP * score, 0.0)


def body(latent, margin_len, in_weight, norm_gain, qkv_weight, out_weight, final_gain, head_out):
    count = lax.axis_size("seq")
    groups = lax.axis_size("group")
    group_pos = lax.axis_index("group")
    seq_pos = lax.axis_index("seq")
    share = latent.shape[1]
    total = share * count
    over_share = OVMAX // count
    width = qkv_weight.shape[2]
    depth = out_weight.shape[1]

    def shift(value, by):
        return lax.ppermute(value, "seq", [(i, (i + by) % count) for i in range(count)])

    def across(value, group_by, pairs):
        moves = [
            (g * count + i, (g + group_by) * count + j)
            for g in range(groups)
            for i, j in pairs
            if 0 <= g + group_by < groups
        ]
        return lax.ppermute(value, ("group", "seq"), moves)

    edge = jnp.zeros((1,), jnp.int32)
    lengths = lax.dynamic_slice(jnp.concatenate([edge, margin_len, edge]), (2 * group_pos,), (3,))
    here = seq_pos.astype(jnp.int32)[None]
    rows16 = latent.astype(BF16)
    own_pieces = [rows16] + [shift(rows16, k) for k in range(1, count)]
    readers = OVMAX // share
    next_pieces = [
        across(rows16[0], -1, [(i, (i + k) % count) for i in range(readers)]) for k in range(count)
    ]
    gain = norm_gain[None, :]
    qkv = jnp.concatenate([qkv_weight] * max(1, LANES // width), axis=2)

    block = width // groups
    part = lax.dynamic_slice_in_dim(out_weight, group_pos * block, block, 0)
    gathered = jnp.stack([part] + [shift(part, k) for k in range(1, count)])[None]
    bits = groups.bit_length() - 1
    for bit in list(range(1, bits)) + [0]:
        other = lax.ppermute(gathered, "group", [(g, g ^ (1 << bit)) for g in range(groups)])
        gathered = jnp.concatenate([gathered, other])
    members = [0]
    for bit in list(range(1, bits)) + [0]:
        members = members + [m ^ (1 << bit) for m in members]
    place = [members.index(m) for m in range(groups)]
    order = jnp.asarray(place, jnp.int32)[jnp.arange(groups, dtype=jnp.int32) ^ group_pos]
    full_out = jnp.take(gathered, order, axis=0).transpose(1, 0, 2, 3).reshape(count, width, depth)

    scores = []
    for slot in range(2):
        meta = jnp.concatenate([here, lengths[1 + slot : 2 + slot]])
        following, next_at = (own_pieces, 1) if slot == 0 else (next_pieces, None)
        window, att = attend(count, meta, own_pieces, slot, following, next_at, in_weight, gain, qkv)
        att = att[:, :, :width]
        pieces = [att[0]] + [shift(att[k], k) for k in range(1, count)]
        scores.append(finish(count, meta, pieces, window, in_weight, full_out, final_gain[None, :], head_out))

    half = count - readers
    over_deltas = list(range(count))
    group_deltas = list(range(half, count))
    tails = []
    for slot, group_by in ((1, 1), (0, 0)):
        score = scores[slot]
        over_part = score[share:]
        overs, wholes = [], []
        for delta in over_deltas:
            pairs = [(i, i - delta) for i in range(delta, count) if i - delta <= (i * over_share + over_share - 1) // share]
            if delta in group_deltas:
                pairs = sorted(set(pairs) | {(i, i - delta) for i in range(delta, count)})
                moved = across(score, group_by, pairs)
                overs.append(moved[share:])
                wholes.append(moved[:share])
            elif delta == 0 and group_by == 0:
                overs.append(over_part)
            else:
                overs.append(across(over_part, group_by, pairs))
        tails += overs + wholes
    vmem = pl.BlockSpec(memory_space=pltpu.VMEM)
    return pl.pallas_call(
        functools.partial(combine_kernel, count, over_deltas, group_deltas),
        out_shape=jax.ShapeDtypeStruct(latent.shape, F32),
        in_specs=[pl.BlockSpec(memory_space=pltpu.SMEM)] + [vmem] * (3 + len(tails)),
        out_specs=vmem,
        scratch_shapes=[pltpu.VMEM((OVMAX + total + share, latent.shape[2]), F32)],
        name="combine",
    )(jnp.concatenate([here, lengths]), latent, scores[0], scores[1], *tails)


def solution(mesh):
    in_specs = (
        P("group", "seq", None),
        P(),
        P(),
        P(),
        P(None, None, "seq"),
        P("seq", None),
        P(),
        P(),
    )
    out_specs = P("group", "seq", None)
    return jax.shard_map(body, mesh=mesh, in_specs=in_specs, out_specs=out_specs, check_vma=False)
```

```python
import functools
import math

import jax
import jax.numpy as jnp
from jax import lax
from jax.experimental import pallas as pl
from jax.experimental.pallas import tpu as pltpu
from jax.sharding import PartitionSpec as P

HDIM = 64
OVMAX = 512
LANES = 128
QUAD = 4 * HDIM
STEP = -0.5
F32 = jnp.float32
BF16 = jnp.bfloat16
VMEM = pl.BlockSpec(memory_space=pltpu.VMEM)
SMEM = pl.BlockSpec(memory_space=pltpu.SMEM)


def iota(shape, dim):
    return lax.broadcasted_iota(jnp.int32, shape, dim)


def matmul(lhs, rhs):
    return jnp.dot(lhs, rhs, preferred_element_type=F32)


def matmul_nt(lhs, rhs, precision=None):
    return lax.dot_general(lhs, rhs, (((1,), (1,)), ((), ())), precision=precision, preferred_element_type=F32)


def split(value):
    high = value.astype(BF16)
    return high, (value - high.astype(F32)).astype(BF16)


def margin_at(margin_ref, index):
    last = margin_ref.shape[0]
    length = margin_ref[jnp.clip(index, 0, last - 1)]
    return jnp.where((index >= 0) & (index < last), length, 0)


def fold_kernel(shares, in_ref, gain_ref, qkv_ref, out_ref, map_ref, back_ref, part_ref, gram_ref):
    weight = in_ref[...].astype(F32)
    channels, depth = weight.shape
    width = out_ref.shape[0]
    centered = weight - jnp.mean(weight, axis=-1, keepdims=True)
    high, low = split(centered * gain_ref[...])
    both = jnp.concatenate([high, low], axis=0)

    def folded(which):
        product = matmul(both, qkv_ref[which])
        return product[:channels] + product[channels:]

    map_ref[...] = jnp.concatenate([folded(0), folded(1)], axis=0).T.astype(BF16)
    values = folded(2)
    tiled = jnp.concatenate([values] * (width // HDIM), axis=0)
    same = iota((width, width), 0) // channels == iota((width, width), 1) // HDIM
    high, low = split(jnp.where(same, tiled, 0.0))
    back_ref[...] = (matmul(high, out_ref[...]) + matmul(low, out_ref[...])).astype(BF16)
    rows = width // shares
    sub = lax.rem(lax.axis_index("group"), shares)
    part_ref[...] = back_ref[pl.ds(pl.multiple_of(sub * rows, rows), rows), :]
    gram = matmul_nt(centered, centered, lax.Precision.HIGHEST) * (1.0 / depth)
    for i in range(3):
        piece = gram.astype(BF16)
        gram_ref[i] = piece
        gram = gram - piece.astype(F32)


def attend_kernel(count, window, margin_ref, *refs):
    piece_refs, refs = refs[:count], refs[count:]
    next_refs = piece_refs
    if window:
        next_refs, refs = [refs[0].at[k] for k in range(count)], refs[1:]
    map_refs, refs = refs[:count], refs[count:]
    gram_ref, sum_ref, own_ref, slot_scr, next_scr, win_scr, map_scr, key_scr, query_scr, p_scr, even_scr, odd_scr = refs
    total = win_scr.shape[0]
    channels = gram_ref.shape[-1]
    share = total // count
    width = map_refs[0].shape[0]
    low = total - OVMAX
    group_pos = lax.axis_index("group")
    seq_pos = lax.axis_index("seq")
    over_len = margin_at(margin_ref, 2 * group_pos + window)
    own = total - over_len

    next_scr[:OVMAX, :] = jnp.zeros((OVMAX, LANES), F32)
    for k in range(count):
        source = lax.rem(seq_pos + (count - k), count) * share
        at = pl.ds(pl.multiple_of(source, share), share)
        after = pl.ds(pl.multiple_of(source + OVMAX, share), share)
        slot = piece_refs[k][...].astype(F32)
        slot_scr[at, :] = pltpu.roll(slot, channels, 1) if window else slot
        following = next_refs[k][...].astype(F32)
        next_scr[after, :] = following if window else pltpu.roll(following, channels, 1)
        map_scr[k * width : (k + 1) * width, :] = map_refs[k][...]
    left = iota((OVMAX, LANES), 1) < channels
    for start in range(0, total, OVMAX):
        rows = slot_scr[start : start + OVMAX, :]
        if start >= low:
            tail = next_scr[pl.ds(over_len + (start - low), OVMAX), :]
            rows = jnp.where(iota(rows.shape, 0) + start < own, rows, tail)
        win_scr[start : start + OVMAX, :] = jnp.where(left, rows, 0.0).astype(BF16)

    win = win_scr[...]
    mine = win_scr[pl.ds(pl.multiple_of(seq_pos * share, share), share), :]
    own_ref[...] = mine

    def variance(tokens):
        bent = sum(matmul(tokens[:, :channels], gram_ref[i]) for i in range(3))
        return jnp.sum(bent * tokens[:, :channels].astype(F32), axis=-1, keepdims=True) + 1e-05

    scaled = win.astype(F32) * lax.rsqrt(variance(win))
    turned = pltpu.roll(scaled, channels, 1)
    position = iota((total, LANES), 0)
    counted = (position >= jnp.minimum(own, total - 1)).astype(F32)
    left = iota((total, LANES), 1) < channels
    even_scr[:, :LANES] = jnp.where(left, scaled, turned * counted).astype(BF16)
    even_scr[:, LANES:] = jnp.where(left, 1.0, counted).astype(BF16)
    odd_scr[:, :LANES] = jnp.where(left, scaled * counted, turned).astype(BF16)
    odd_scr[:, LANES:] = jnp.where(left, counted, 1.0).astype(BF16)

    identity = jnp.where(iota((channels, channels), 0) == iota((channels, channels), 1), 1.0, 0.0).astype(BF16)
    forms = jnp.concatenate([gram_ref[0], gram_ref[1], gram_ref[2], identity], axis=0)
    bent = matmul_nt(forms, win[:, :channels])
    sides = [bent[i * channels : (i + 1) * channels] for i in range(4)]
    key_eps = (jnp.sum((sides[0] + sides[1] + sides[2]) * sides[3], axis=0, keepdims=True) + 1e-05) * 1e-06
    query_eps = variance(mine) * 1e-06

    win_right = pltpu.roll(win.astype(F32), channels, 1).astype(BF16)
    one_head = iota((QUAD, QUAD), 0) // HDIM == iota((QUAD, QUAD), 1) // HDIM
    spread = jnp.where(one_head, 1.0 / HDIM, 0.0).astype(BF16)
    head_of = iota((share, QUAD), 1) // HDIM
    quads = map_scr.shape[0] // QUAD
    scale = HDIM ** (-0.5) * math.log2(math.e)
    tile = min(total, 256)
    left = iota((share, LANES), 1) < channels
    for quad in range(quads):
        maps = map_scr[quad * QUAD : (quad + 1) * QUAD, :]
        keys = matmul_nt(maps, win_right).reshape(4, HDIM, total)
        norm = jnp.mean(keys * keys, axis=1, keepdims=True)
        keys = keys * lax.rsqrt(norm + key_eps[None])
        key_scr[quad % 2] = keys.reshape(QUAD, total).astype(BF16)
        queries = matmul_nt(mine, maps)
        high, rest = split(queries * queries)
        queries = (queries * lax.rsqrt(matmul(high, spread) + matmul(rest, spread) + query_eps)).astype(BF16)
        for i, head in enumerate((0, 2, 1, 3)):
            query_scr[quad % 2, i * share : (i + 1) * share, :] = jnp.where(
                head_of == head, queries, jnp.zeros_like(queries)
            )
        for start in range(0, total, tile):
            scores = matmul(query_scr[quad % 2], key_scr[quad % 2, :, start : start + tile])
            p_scr[quad % 2, :, start : start + tile] = jnp.exp2(scores * scale).astype(BF16)
        even = matmul(p_scr[quad % 2, : 2 * share, :], even_scr[...])
        odd = matmul(p_scr[quad % 2, 2 * share :, :], odd_scr[...])
        even = even[:, :LANES] / even[:, LANES:]
        odd = odd[:, :LANES] / odd[:, LANES:]
        for pair in range(2):
            rows = slice(pair * share, (pair + 1) * share)
            at = slice(quad * QUAD + pair * LANES, quad * QUAD + (pair + 1) * LANES)
            sum_ref[:share, at] = jnp.where(left, even[rows], odd[rows]).astype(BF16)
            sum_ref[share:, at] = pltpu.roll(jnp.where(left, odd[rows], even[rows]), HDIM, 1).astype(BF16)


def finish_kernel(count, shares, high, margin_ref, *refs):
    sum_refs, own_refs = refs[:2], refs[2:4]
    in_ref, gain_ref, head_ref, back_ref, far_ref, near_ref, rows_ref, packed_ref, all_scr, mixed_scr, final_scr, head_scr = refs[4:]
    width, depth = back_ref.shape
    share = own_refs[0].shape[0]
    channels = in_ref.shape[0]
    total = share * count
    part = width // shares
    group_pos = lax.axis_index("group")
    seq_pos = lax.axis_index("seq")
    sub = lax.rem(group_pos, shares)
    all_scr[:width, :] = back_ref[...]
    for i, m in enumerate(high):
        for near, ref in ((0, far_ref), (1, near_ref)):
            place = jnp.bitwise_xor(sub, m ^ near) * part
            for k in range(1, count):
                all_scr[pl.ds(pl.multiple_of(place + k * width, part), part), :] = ref[i, k - 1]
    head_scr[...] = jnp.zeros_like(head_scr)
    head_scr[:, :channels] = head_ref[...]
    tile = 256
    chunk = min(128, share)
    for window in range(2):
        for start in range(0, depth, tile):
            at = slice(start, start + tile)
            inputs = matmul(own_refs[window][:, :channels], in_ref[:, at])
            added = matmul(sum_refs[window][...], all_scr[:, at])
            mixed_scr[window, :share, at] = added[:share] + inputs
            mixed_scr[window, share:, at] = added[share:] + inputs
        for start in range(0, 2 * share, chunk):
            at = slice(start, start + chunk)
            mixed = mixed_scr[window, at, :]
            centered = mixed - jnp.mean(mixed, axis=-1, keepdims=True)
            variance = jnp.mean(centered * centered, axis=-1, keepdims=True)
            final_scr[window, at, :] = (centered * lax.rsqrt(variance + 1e-05) * gain_ref[...]).astype(BF16)
        score = matmul(final_scr[window], head_scr[...])
        own = total - margin_at(margin_ref, 2 * group_pos + window)
        position = iota((share, LANES), 0) + seq_pos * share
        score = score[:share] - jnp.where(position >= own, score[share:], 0.0)
        rows_ref[window] = score[:, :channels]
        packed_ref[window] = score[: share // 2] + pltpu.roll(score[share // 2 :], channels, 1)


def combine_kernel(count, deltas, margin_ref, latent_ref, rows_ref, *refs):
    out_ref, tail_scr = refs[2 * len(deltas) :]
    share, channels = latent_ref.shape[1:]
    total = share * count
    group_pos = lax.axis_index("group")
    seq_pos = lax.axis_index("seq")
    for slot in range(2):
        before = margin_at(margin_ref, 2 * group_pos + slot - 1)
        own = total - margin_at(margin_ref, 2 * group_pos + slot)
        tail_scr[...] = jnp.zeros_like(tail_scr)
        for delta, ref in zip(deltas, refs[slot * len(deltas) : (slot + 1) * len(deltas)]):
            row = (seq_pos + delta) * share - (total - OVMAX)
            for half in range(2):
                value = ref[...] if half == 0 else pltpu.roll(ref[...], channels, 1)
                at = pl.ds(pl.multiple_of(row + half * (share // 2), share // 2), share // 2)
                tail_scr[at, :] = value
        moved = tail_scr[pl.ds(OVMAX - before + seq_pos * share, share), :]
        score = rows_ref[slot] + moved[:, :channels]
        keep = iota(score.shape, 0) + seq_pos * share < own
        out_ref[slot] = jnp.where(keep, latent_ref[slot] + STEP * score, 0.0)


def body(latent, margin_len, in_weight, norm_gain, qkv_weight, out_weight, final_gain, head_out):
    count = lax.axis_size("seq")
    groups = lax.axis_size("group")
    share, channels = latent.shape[1:]
    total = share * count
    width, depth = out_weight.shape
    full = width * count
    shares = min(groups, width // 16)
    high = range(0, shares, 2)

    def shift(value, by):
        return lax.ppermute(value, "seq", [(i, (i + by) % count) for i in range(count)])

    def across(value, group_by, pairs):
        moves = [
            (g * count + i, (g + group_by) * count + j)
            for g in range(groups)
            for i, j in pairs
            if 0 <= g + group_by < groups
        ]
        return lax.ppermute(value, ("group", "seq"), moves)

    def swap(value, bits):
        return lax.ppermute(value, "group", [(g, g ^ bits) for g in range(groups)])

    def gathered(value):
        return [value] + [shift(value, k) for k in range(1, count)]

    packed = jnp.concatenate([latent[0], latent[1]], axis=1).astype(BF16)
    pieces = gathered(packed)
    following = across(jnp.stack(pieces), -1, [(i, i) for i in range(count)])

    maps, back, part, gram = pl.pallas_call(
        functools.partial(fold_kernel, shares),
        out_shape=(
            jax.ShapeDtypeStruct((width, 2 * channels), BF16),
            jax.ShapeDtypeStruct((width, depth), BF16),
            jax.ShapeDtypeStruct((width // shares, depth), BF16),
            jax.ShapeDtypeStruct((3, channels, channels), BF16),
        ),
        in_specs=[VMEM] * 4,
        out_specs=(VMEM,) * 4,
        cost_estimate=pl.CostEstimate(flops=width * depth * 1200, bytes_accessed=8 * width * depth, transcendentals=0),
        name="fold",
    )(in_weight, norm_gain[None, :], qkv_weight, out_weight)
    map_pieces = gathered(maps)
    own_part = jnp.stack([shift(part, k) for k in range(1, count)])

    def attend(window):
        rows = 4 * share
        extra = [following] if window else []
        return pl.pallas_call(
            functools.partial(attend_kernel, count, window),
            out_shape=(
                jax.ShapeDtypeStruct((2 * share, full), BF16),
                jax.ShapeDtypeStruct((share, LANES), BF16),
            ),
            in_specs=[SMEM] + [VMEM] * (2 * count + len(extra) + 1),
            out_specs=(VMEM, VMEM),
            scratch_shapes=[
                pltpu.VMEM((total, LANES), F32),
                pltpu.VMEM((OVMAX + total, LANES), F32),
                pltpu.VMEM((total, LANES), BF16),
                pltpu.VMEM((full, LANES), BF16),
                pltpu.VMEM((2, QUAD, total), BF16),
                pltpu.VMEM((2, rows, QUAD), BF16),
                pltpu.VMEM((2, rows, total), BF16),
                pltpu.VMEM((total, QUAD), BF16),
                pltpu.VMEM((total, QUAD), BF16),
            ],
            cost_estimate=pl.CostEstimate(
                flops=16 * share * total * full, bytes_accessed=4 * full * share, transcendentals=share * total * full // HDIM
            ),
            name="attend",
        )(margin_len, *pieces, *extra, *map_pieces, gram)

    sums, owns = zip(*[attend(window) for window in range(2)])
    far = jnp.stack([own_part] + [swap(own_part, bits) for bits in high[1:]])
    near = swap(far, 1)
    rows, tails = pl.pallas_call(
        functools.partial(finish_kernel, count, shares, list(high)),
        out_shape=(
            jax.ShapeDtypeStruct((2, share, channels), F32),
            jax.ShapeDtypeStruct((2, share // 2, LANES), F32),
        ),
        in_specs=[SMEM] + [VMEM] * 10,
        out_specs=(VMEM, VMEM),
        scratch_shapes=[
            pltpu.VMEM((full, depth), BF16),
            pltpu.VMEM((2, 2 * share, depth), F32),
            pltpu.VMEM((2, 2 * share, depth), BF16),
            pltpu.VMEM((depth, LANES), BF16),
        ],
        cost_estimate=pl.CostEstimate(flops=8 * share * full * depth, bytes_accessed=2 * full * depth, transcendentals=0),
        name="finish",
    )(margin_len, *sums, *owns, in_weight, final_gain[None, :], head_out, back, far, near)

    deltas = list(range((total - OVMAX) // share, count))
    received = []
    for window, group_by in ((1, 1), (0, 0)):
        received += [across(tails[window], group_by, [(i, i - d) for i in range(d, count)]) for d in deltas]
    return pl.pallas_call(
        functools.partial(combine_kernel, count, deltas),
        out_shape=jax.ShapeDtypeStruct(latent.shape, F32),
        in_specs=[SMEM] + [VMEM] * (2 + len(received)),
        out_specs=VMEM,
        scratch_shapes=[pltpu.VMEM((OVMAX + total + share, LANES), F32)],
        name="combine",
    )(margin_len, latent, rows, *received)


def solution(mesh):
    in_specs = (
        P("group", "seq", None),
        P(),
        P(),
        P(),
        P(None, None, "seq"),
        P("seq", None),
        P(),
        P(),
    )
    out_specs = P("group", "seq", None)
    return jax.shard_map(body, mesh=mesh, in_specs=in_specs, out_specs=out_specs, check_vma=False)
```

```python
import functools
import math

import jax
import jax.numpy as jnp
from jax import lax
from jax.experimental import pallas as pl
from jax.experimental.pallas import tpu as pltpu
from jax.sharding import PartitionSpec as P

HDIM = 64
OVMAX = 512
LANES = 128
QUAD = 4 * HDIM
STEP = -0.5
F32 = jnp.float32
BF16 = jnp.bfloat16
VMEM = pl.BlockSpec(memory_space=pltpu.VMEM)
SMEM = pl.BlockSpec(memory_space=pltpu.SMEM)


def iota(shape, dim):
    return lax.broadcasted_iota(jnp.int32, shape, dim)


def matmul(lhs, rhs):
    return jnp.dot(lhs, rhs, preferred_element_type=F32)


def matmul_nt(lhs, rhs, precision=None):
    return lax.dot_general(lhs, rhs, (((1,), (1,)), ((), ())), precision=precision, preferred_element_type=F32)


def split(value):
    high = value.astype(BF16)
    return high, (value - high.astype(F32)).astype(BF16)


def margin_at(margin_ref, index):
    last = margin_ref.shape[0]
    length = margin_ref[jnp.clip(index, 0, last - 1)]
    return jnp.where((index >= 0) & (index < last), length, 0)


def fold_kernel(shares, in_ref, gain_ref, qkv_ref, out_ref, map_ref, back_ref, part_ref, gram_ref):
    weight = in_ref[...].astype(F32)
    channels, depth = weight.shape
    width = out_ref.shape[0]
    centered = weight - jnp.mean(weight, axis=-1, keepdims=True)
    high, low = split(centered * gain_ref[...])
    both = jnp.concatenate([high, low], axis=0)

    def folded(which):
        product = matmul(both, qkv_ref[which])
        return product[:channels] + product[channels:]

    map_ref[...] = jnp.concatenate([folded(0), folded(1)], axis=0).T.astype(BF16)
    values = folded(2)
    tiled = jnp.concatenate([values] * (width // HDIM), axis=0)
    same = iota((width, width), 0) // channels == iota((width, width), 1) // HDIM
    high, low = split(jnp.where(same, tiled, 0.0))
    back_ref[...] = (matmul(high, out_ref[...]) + matmul(low, out_ref[...])).astype(BF16)
    rows = width // shares
    sub = lax.rem(lax.axis_index("group"), shares)
    part_ref[...] = back_ref[pl.ds(pl.multiple_of(sub * rows, rows), rows), :]
    gram = matmul_nt(centered, centered, lax.Precision.HIGHEST) * (1.0 / depth)
    for i in range(3):
        piece = gram.astype(BF16)
        gram_ref[i] = piece
        gram = gram - piece.astype(F32)


def attend_kernel(count, window, margin_ref, *refs):
    piece_refs, refs = refs[:count], refs[count:]
    next_refs = piece_refs
    if window:
        next_refs, refs = [refs[0].at[k] for k in range(count)], refs[1:]
    map_refs, refs = refs[:count], refs[count:]
    gram_ref, sum_ref, own_ref, slot_scr, next_scr, win_scr, map_scr, key_scr, query_scr, p_scr, even_scr, odd_scr = refs
    total = win_scr.shape[0]
    channels = gram_ref.shape[-1]
    share = total // count
    width = map_refs[0].shape[0]
    low = total - OVMAX
    group_pos = lax.axis_index("group")
    seq_pos = lax.axis_index("seq")
    over_len = margin_at(margin_ref, 2 * group_pos + window)
    own = total - over_len

    next_scr[:OVMAX, :] = jnp.zeros((OVMAX, LANES), F32)
    for k in range(count):
        source = lax.rem(seq_pos + (count - k), count) * share
        at = pl.ds(pl.multiple_of(source, share), share)
        after = pl.ds(pl.multiple_of(source + OVMAX, share), share)
        slot = piece_refs[k][...].astype(F32)
        slot_scr[at, :] = pltpu.roll(slot, channels, 1) if window else slot
        following = next_refs[k][...].astype(F32)
        next_scr[after, :] = following if window else pltpu.roll(following, channels, 1)
        map_scr[k * width : (k + 1) * width, :] = map_refs[k][...]
    left = iota((OVMAX, LANES), 1) < channels
    for start in range(0, total, OVMAX):
        rows = slot_scr[start : start + OVMAX, :]
        if start >= low:
            tail = next_scr[pl.ds(over_len + (start - low), OVMAX), :]
            rows = jnp.where(iota(rows.shape, 0) + start < own, rows, tail)
        win_scr[start : start + OVMAX, :] = jnp.where(left, rows, 0.0).astype(BF16)

    win = win_scr[...]
    mine = win_scr[pl.ds(pl.multiple_of(seq_pos * share, share), share), :]
    own_ref[...] = mine

    def variance(tokens):
        bent = sum(matmul(tokens[:, :channels], gram_ref[i]) for i in range(3))
        return jnp.sum(bent * tokens[:, :channels].astype(F32), axis=-1, keepdims=True) + 1e-05

    scaled = win.astype(F32) * lax.rsqrt(variance(win))
    turned = pltpu.roll(scaled, channels, 1)
    position = iota((total, LANES), 0)
    counted = (position >= jnp.minimum(own, total - 1)).astype(F32)
    left = iota((total, LANES), 1) < channels
    even_scr[:, :LANES] = jnp.where(left, scaled, turned * counted).astype(BF16)
    even_scr[:, LANES:] = jnp.where(left, 1.0, counted).astype(BF16)
    odd_scr[:, :LANES] = jnp.where(left, scaled * counted, turned).astype(BF16)
    odd_scr[:, LANES:] = jnp.where(left, counted, 1.0).astype(BF16)

    identity = jnp.where(iota((channels, channels), 0) == iota((channels, channels), 1), 1.0, 0.0).astype(BF16)
    forms = jnp.concatenate([gram_ref[0], gram_ref[1], gram_ref[2], identity], axis=0)
    bent = matmul_nt(forms, win[:, :channels])
    sides = [bent[i * channels : (i + 1) * channels] for i in range(4)]
    key_eps = (jnp.sum((sides[0] + sides[1] + sides[2]) * sides[3], axis=0, keepdims=True) + 1e-05) * 1e-06
    query_eps = variance(mine) * 1e-06

    win_right = pltpu.roll(win.astype(F32), channels, 1).astype(BF16)
    one_head = iota((QUAD, QUAD), 0) // HDIM == iota((QUAD, QUAD), 1) // HDIM
    spread = jnp.where(one_head, 1.0 / HDIM, 0.0).astype(BF16)
    head_of = iota((share, QUAD), 1) // HDIM
    quads = map_scr.shape[0] // QUAD
    scale = HDIM ** (-0.5) * math.log2(math.e)
    tile = min(total, 256)
    left = iota((share, LANES), 1) < channels
    for quad in range(quads):
        maps = map_scr[quad * QUAD : (quad + 1) * QUAD, :]
        keys = matmul_nt(maps, win_right).reshape(4, HDIM, total)
        norm = jnp.mean(keys * keys, axis=1, keepdims=True)
        keys = keys * lax.rsqrt(norm + key_eps[None])
        key_scr[quad % 2] = keys.reshape(QUAD, total).astype(BF16)
        queries = matmul_nt(mine, maps)
        high, rest = split(queries * queries)
        queries = (queries * lax.rsqrt(matmul(high, spread) + matmul(rest, spread) + query_eps)).astype(BF16)
        for i, head in enumerate((0, 2, 1, 3)):
            query_scr[quad % 2, i * share : (i + 1) * share, :] = jnp.where(
                head_of == head, queries, jnp.zeros_like(queries)
            )
        for start in range(0, total, tile):
            scores = matmul(query_scr[quad % 2], key_scr[quad % 2, :, start : start + tile])
            p_scr[quad % 2, :, start : start + tile] = jnp.exp2(scores * scale).astype(BF16)
        even = matmul(p_scr[quad % 2, : 2 * share, :], even_scr[...])
        odd = matmul(p_scr[quad % 2, 2 * share :, :], odd_scr[...])
        even = even[:, :LANES] / even[:, LANES:]
        odd = odd[:, :LANES] / odd[:, LANES:]
        for pair in range(2):
            rows = slice(pair * share, (pair + 1) * share)
            at = slice(quad * QUAD + pair * LANES, quad * QUAD + (pair + 1) * LANES)
            sum_ref[:share, at] = jnp.where(left, even[rows], odd[rows]).astype(BF16)
            sum_ref[share:, at] = pltpu.roll(jnp.where(left, odd[rows], even[rows]), HDIM, 1).astype(BF16)


def finish_kernel(count, shares, high, margin_ref, *refs):
    sum_refs, own_refs = refs[:2], refs[2:4]
    in_ref, gain_ref, head_ref, back_ref, far_ref, near_ref, rows_ref, packed_first, packed_second, all_scr, mixed_scr, final_scr, head_scr = refs[4:]
    width, depth = back_ref.shape
    share = own_refs[0].shape[0]
    channels = in_ref.shape[0]
    total = share * count
    part = width // shares
    group_pos = lax.axis_index("group")
    seq_pos = lax.axis_index("seq")
    sub = lax.rem(group_pos, shares)
    all_scr[:width, :] = back_ref[...]
    for i, m in enumerate(high):
        for near, ref in ((0, far_ref), (1, near_ref)):
            place = jnp.bitwise_xor(sub, m ^ near) * part
            for k in range(1, count):
                all_scr[pl.ds(pl.multiple_of(place + k * width, part), part), :] = ref[i, k - 1]
    head_scr[...] = jnp.zeros_like(head_scr)
    head_scr[:, :channels] = head_ref[...]
    tile = 256
    chunk = min(128, share)
    for window in range(2):
        for start in range(0, depth, tile):
            at = slice(start, start + tile)
            inputs = matmul(own_refs[window][:, :channels], in_ref[:, at])
            added = matmul(sum_refs[window][...], all_scr[:, at])
            mixed_scr[window, :share, at] = added[:share] + inputs
            mixed_scr[window, share:, at] = added[share:] + inputs
        for start in range(0, 2 * share, chunk):
            at = slice(start, start + chunk)
            mixed = mixed_scr[window, at, :]
            centered = mixed - jnp.mean(mixed, axis=-1, keepdims=True)
            variance = jnp.mean(centered * centered, axis=-1, keepdims=True)
            final_scr[window, at, :] = (centered * lax.rsqrt(variance + 1e-05) * gain_ref[...]).astype(BF16)
        score = matmul(final_scr[window], head_scr[...])
        own = total - margin_at(margin_ref, 2 * group_pos + window)
        position = iota((share, LANES), 0) + seq_pos * share
        score = score[:share] - jnp.where(position >= own, score[share:], 0.0)
        rows_ref[window] = score[:, :channels]
        packed_ref = packed_second if window else packed_first
        packed_ref[...] = (score[: share // 2] + pltpu.roll(score[share // 2 :], channels, 1)).astype(BF16)


def combine_kernel(count, deltas, margin_ref, latent_ref, rows_ref, *refs):
    out_ref, tail_scr = refs[2 * len(deltas) :]
    share, channels = latent_ref.shape[1:]
    total = share * count
    group_pos = lax.axis_index("group")
    seq_pos = lax.axis_index("seq")
    for slot in range(2):
        before = margin_at(margin_ref, 2 * group_pos + slot - 1)
        own = total - margin_at(margin_ref, 2 * group_pos + slot)
        tail_scr[...] = jnp.zeros_like(tail_scr)
        for delta, ref in zip(deltas, refs[slot * len(deltas) : (slot + 1) * len(deltas)]):
            row = (seq_pos + delta) * share - (total - OVMAX)
            for half in range(2):
                value = ref[...].astype(F32)
                value = pltpu.roll(value, channels, 1) if half else value
                at = pl.ds(pl.multiple_of(row + half * (share // 2), share // 2), share // 2)
                tail_scr[at, :] = value
        moved = tail_scr[pl.ds(OVMAX - before + seq_pos * share, share), :]
        score = rows_ref[slot] + moved[:, :channels]
        keep = iota(score.shape, 0) + seq_pos * share < own
        out_ref[slot] = jnp.where(keep, latent_ref[slot] + STEP * score, 0.0)


def body(latent, margin_len, in_weight, norm_gain, qkv_weight, out_weight, final_gain, head_out):
    count = lax.axis_size("seq")
    groups = lax.axis_size("group")
    share, channels = latent.shape[1:]
    total = share * count
    width, depth = out_weight.shape
    full = width * count
    shares = min(groups, width // 16)
    high = range(0, shares, 2)

    def shift(value, by):
        return lax.ppermute(value, "seq", [(i, (i + by) % count) for i in range(count)])

    def across(value, group_by, pairs):
        moves = [
            (g * count + i, (g + group_by) * count + j)
            for g in range(groups)
            for i, j in pairs
            if 0 <= g + group_by < groups
        ]
        return lax.ppermute(value, ("group", "seq"), moves)

    def swap(value, bits):
        return lax.ppermute(value, "group", [(g, g ^ bits) for g in range(groups)])

    def gathered(value):
        return [value] + [shift(value, k) for k in range(1, count)]

    packed = jnp.concatenate([latent[0], latent[1]], axis=1).astype(BF16)
    pieces = gathered(packed)
    stacked = jnp.stack(pieces)
    following = across(stacked, -1, [(i, i) for i in range(count)])

    maps, back, part, gram = pl.pallas_call(
        functools.partial(fold_kernel, shares),
        out_shape=(
            jax.ShapeDtypeStruct((width, 2 * channels), BF16),
            jax.ShapeDtypeStruct((width, depth), BF16),
            jax.ShapeDtypeStruct((width // shares, depth), BF16),
            jax.ShapeDtypeStruct((3, channels, channels), BF16),
        ),
        in_specs=[VMEM] * 4,
        out_specs=(VMEM,) * 4,
        cost_estimate=pl.CostEstimate(flops=width * depth * 1200, bytes_accessed=8 * width * depth, transcendentals=0),
        name="fold",
    )(in_weight, norm_gain[None, :], qkv_weight, out_weight)
    map_pieces = gathered(maps)
    own_part = jnp.stack(gathered(part)[1:])

    def attend(window):
        rows = 4 * share
        extra = [following] if window else []
        return pl.pallas_call(
            functools.partial(attend_kernel, count, window),
            out_shape=(
                jax.ShapeDtypeStruct((2 * share, full), BF16),
                jax.ShapeDtypeStruct((share, LANES), BF16),
            ),
            in_specs=[SMEM] + [VMEM] * (2 * count + len(extra) + 1),
            out_specs=(VMEM, VMEM),
            scratch_shapes=[
                pltpu.VMEM((total, LANES), F32),
                pltpu.VMEM((OVMAX + total, LANES), F32),
                pltpu.VMEM((total, LANES), BF16),
                pltpu.VMEM((full, LANES), BF16),
                pltpu.VMEM((2, QUAD, total), BF16),
                pltpu.VMEM((2, rows, QUAD), BF16),
                pltpu.VMEM((2, rows, total), BF16),
                pltpu.VMEM((total, QUAD), BF16),
                pltpu.VMEM((total, QUAD), BF16),
            ],
            cost_estimate=pl.CostEstimate(
                flops=16 * share * total * full, bytes_accessed=4 * full * share, transcendentals=share * total * full // HDIM
            ),
            name="attend",
        )(margin_len, *pieces, *extra, *map_pieces, gram)

    first = attend(0)
    second = attend(1)
    sums, owns = zip(first, second)
    planes = [swap(own_part, bits) for bits in high[1:]]
    far = jnp.stack([own_part] + planes)
    near = swap(far, 1)
    rows, *tails = pl.pallas_call(
        functools.partial(finish_kernel, count, shares, list(high)),
        out_shape=(
            jax.ShapeDtypeStruct((2, share, channels), F32),
            jax.ShapeDtypeStruct((share // 2, LANES), BF16),
            jax.ShapeDtypeStruct((share // 2, LANES), BF16),
        ),
        in_specs=[SMEM] + [VMEM] * 10,
        out_specs=(VMEM, VMEM, VMEM),
        scratch_shapes=[
            pltpu.VMEM((full, depth), BF16),
            pltpu.VMEM((2, 2 * share, depth), F32),
            pltpu.VMEM((2, 2 * share, depth), BF16),
            pltpu.VMEM((depth, LANES), BF16),
        ],
        cost_estimate=pl.CostEstimate(flops=8 * share * full * depth, bytes_accessed=2 * full * depth, transcendentals=0),
        name="finish",
    )(margin_len, *sums, *owns, in_weight, final_gain[None, :], head_out, back, far, near)

    deltas = list(range((total - OVMAX) // share, count))
    received = []
    for window, group_by in ((1, 1), (0, 0)):
        received += [across(tails[window], group_by, [(i, i - d) for i in range(d, count)]) for d in deltas]
    return pl.pallas_call(
        functools.partial(combine_kernel, count, deltas),
        out_shape=jax.ShapeDtypeStruct(latent.shape, F32),
        in_specs=[SMEM] + [VMEM] * (2 + len(received)),
        out_specs=VMEM,
        scratch_shapes=[pltpu.VMEM((OVMAX + total + share, LANES), F32)],
        name="combine",
    )(margin_len, latent, rows, *received)


def solution(mesh):
    in_specs = (
        P("group", "seq", None),
        P(),
        P(),
        P(),
        P(None, None, "seq"),
        P("seq", None),
        P(),
        P(),
    )
    out_specs = P("group", "seq", None)

    return jax.shard_map(body, mesh=mesh, in_specs=in_specs, out_specs=out_specs, check_vma=False)
```

```python
import functools
import math

import jax
import jax.numpy as jnp
from jax import lax
from jax.experimental import pallas as pl
from jax.experimental.pallas import tpu as pltpu
from jax.sharding import PartitionSpec as P

HDIM = 64
OVMAX = 512
LANES = 128
QUAD = 4 * HDIM
STEP = -0.5
F32 = jnp.float32
BF16 = jnp.bfloat16
VMEM = pl.BlockSpec(memory_space=pltpu.VMEM)
SMEM = pl.BlockSpec(memory_space=pltpu.SMEM)


def iota(shape, dim):
    return lax.broadcasted_iota(jnp.int32, shape, dim)


def matmul(lhs, rhs):
    return jnp.dot(lhs, rhs, preferred_element_type=F32)


def matmul_nt(lhs, rhs, precision=None):
    return lax.dot_general(lhs, rhs, (((1,), (1,)), ((), ())), precision=precision, preferred_element_type=F32)


def split(value):
    high = value.astype(BF16)
    return high, (value - high.astype(F32)).astype(BF16)


def margin_at(margin_ref, index):
    last = margin_ref.shape[0]
    length = margin_ref[jnp.clip(index, 0, last - 1)]
    return jnp.where((index >= 0) & (index < last), length, 0)


def fold_kernel(shares, latent_ref, in_ref, gain_ref, qkv_ref, out_ref, final_ref, head_ref, *refs):
    send_ref, back_ref, part_ref, direct_ref, gram_ref = refs
    weight = in_ref[...].astype(F32)
    channels, depth = weight.shape
    width = out_ref.shape[0]
    share = latent_ref.shape[2]
    centered = weight - jnp.mean(weight, axis=-1, keepdims=True)
    both = jnp.concatenate(split(centered * gain_ref[...]), axis=0)

    def folded(which):
        product = matmul(both, qkv_ref[which])
        return product[:channels] + product[channels:]

    values = folded(2)
    tiled = jnp.concatenate([values] * (width // HDIM), axis=0)
    same = iota((width, width), 0) // channels == iota((width, width), 1) // HDIM
    high, low = split(jnp.where(same, tiled, 0.0))
    back = matmul(high, out_ref[...]) + matmul(low, out_ref[...])
    back = back - jnp.mean(back, axis=-1, keepdims=True)
    back_ref[:, :depth] = back.astype(BF16)

    pieces = split(back * final_ref[...]) + split(centered * final_ref[...])
    scores = matmul_nt(jnp.concatenate(pieces, axis=0), head_ref[...])
    left = iota((width, LANES), 1) < channels

    def halves(value):
        value = jnp.concatenate([value, value], axis=1)
        high, low = split(value)
        return jnp.where(left[: value.shape[0]], high.astype(F32), low.astype(F32)).astype(BF16)

    back_ref[:, depth:] = halves(scores[:width] + scores[width : 2 * width])
    rows = width // shares
    sub = lax.rem(lax.axis_index("group"), shares)
    part_ref[...] = back_ref[pl.ds(pl.multiple_of(sub * rows, rows), rows), :]

    send_ref[:width, :] = jnp.concatenate([folded(0), folded(1)], axis=0).T.astype(BF16)
    send_ref[width:, :] = latent_ref[...].reshape(2 * channels, share).T.astype(BF16)

    high, low = split(centered)
    direct_ref[:channels, :depth] = high
    direct_ref[channels:, :depth] = low
    direct_ref[:channels, depth:] = halves(scores[2 * width : 2 * width + channels] + scores[2 * width + channels :])
    direct_ref[channels:, depth:] = jnp.zeros((channels, LANES), BF16)

    gram = matmul_nt(jnp.concatenate([high, low], axis=0), jnp.concatenate([high, low], axis=0))
    gram = (gram[:channels] + gram[channels:]) * (1.0 / depth)
    gram = gram + pltpu.roll(gram, channels, 1)
    first, rest = split(gram)
    rest = gram - first.astype(F32)
    second, third = split(rest)
    left = left[:channels]
    gram_ref[:, :LANES] = jnp.where(left, first.astype(F32), second.astype(F32)).astype(BF16)
    gram_ref[:, LANES:] = jnp.where(left, third.astype(F32), 0.0).astype(BF16)


def attend_kernel(count, window, margin_ref, *refs):
    piece_refs, refs = refs[:count], refs[count:]
    gram_ref, refs = refs[0], refs[1:]
    if window:
        next_ref, refs = refs[0], refs[1:]
    sum_ref, slot_scr, next_scr, win_scr, map_scr, key_scr, query_scr, p_scr, ext_scr = refs
    total = win_scr.shape[0]
    channels = gram_ref.shape[0]
    share = total // count
    full = map_scr.shape[0]
    width = full // count
    low = total - OVMAX
    group_pos = lax.axis_index("group")
    seq_pos = lax.axis_index("seq")
    over_len = margin_at(margin_ref, 2 * group_pos + window)
    own = total - over_len

    next_scr[:OVMAX, :] = jnp.zeros((OVMAX, LANES), F32)
    for k in range(count):
        source = lax.rem(seq_pos + (count - k), count) * share
        at = pl.ds(pl.multiple_of(source, share), share)
        after = pl.ds(pl.multiple_of(source + OVMAX, share), share)
        slot = piece_refs[k][width:, :].astype(F32)
        slot_scr[at, :] = pltpu.roll(slot, channels, 1) if window else slot
        next_scr[after, :] = next_ref[k].astype(F32) if window else pltpu.roll(slot, channels, 1)
        map_scr[k * width : (k + 1) * width, :] = piece_refs[k][:width, :]
    left = iota((OVMAX, LANES), 1) < channels
    for start in range(0, total, OVMAX):
        rows = slot_scr[start : start + OVMAX, :]
        if start >= low:
            tail = next_scr[pl.ds(over_len + (start - low), OVMAX), :]
            rows = jnp.where(iota(rows.shape, 0) + start < own, rows, tail)
        win_scr[start : start + OVMAX, :] = jnp.where(left, rows, 0.0).astype(BF16)

    def twice(tokens):
        tokens = tokens.astype(F32)
        return tokens + pltpu.roll(tokens, channels, 1)

    def bend(tokens, doubled):
        bent = matmul(tokens[:, :channels], gram_ref[...])
        return (bent[:, :LANES] + bent[:, LANES:]) * doubled

    def variance(bent):
        return jnp.maximum(jnp.sum(bent, axis=-1, keepdims=True), 0.0) + 1e-05

    win = win_scr[...]
    mine = win_scr[pl.ds(pl.multiple_of(seq_pos * share, share), share), :]
    mine_twice = twice(mine)
    sum_ref[:share, full:] = mine_twice.astype(BF16)
    sum_ref[share:, full:] = mine_twice.astype(BF16)
    query_eps = variance(bend(mine, mine_twice)) * 1e-06
    doubled = twice(win)
    bent = bend(win, doubled)
    ones = jnp.ones((16, LANES), BF16)
    key_eps = (jnp.maximum(matmul_nt(ones, bent.astype(BF16))[:1], 0.0) + 1e-05) * 1e-06

    scaled = doubled * lax.rsqrt(variance(bent))
    counted = (iota((total, LANES), 0) >= jnp.minimum(own, total - 1)).astype(F32)
    left = iota((total, LANES), 1) < channels
    ext_scr[:, :LANES] = jnp.where(left, scaled, scaled * counted).astype(BF16)
    ext_scr[:, LANES:] = jnp.where(left, 1.0, counted).astype(BF16)

    tile = min(total, 256)
    win_right = jnp.where(left, 0.0, doubled).astype(BF16)
    for start in range(0, total, tile):
        keys = matmul_nt(map_scr[...], win_right[start : start + tile]).reshape(full // HDIM, HDIM, tile)
        norm = jnp.mean(keys * keys, axis=1, keepdims=True)
        keys = keys * lax.rsqrt(norm + key_eps[None, :, start : start + tile])
        key_scr[:, start : start + tile] = keys.reshape(full, tile).astype(BF16)

    one_head = iota((QUAD, QUAD), 0) // HDIM == iota((QUAD, QUAD), 1) // HDIM
    spread = jnp.where(one_head, 1.0 / HDIM, 0.0).astype(BF16)
    head_of = iota((share, QUAD), 1) // HDIM
    scale = HDIM ** (-0.5) * math.log2(math.e)
    left = iota((share, LANES), 1) < channels
    for quad in range(full // QUAD):
        span = slice(quad * QUAD, (quad + 1) * QUAD)
        queries = matmul_nt(mine, map_scr[span, :])
        norm = matmul((queries * queries).astype(BF16), spread)
        queries = (queries * lax.rsqrt(norm + query_eps)).astype(BF16)
        for head in range(4):
            query_scr[quad % 2, head * share : (head + 1) * share, :] = jnp.where(
                head_of == head, queries, jnp.zeros_like(queries)
            )
        for start in range(0, total, tile):
            scores = matmul(query_scr[quad % 2], key_scr[span, start : start + tile])
            p_scr[quad % 2, :, start : start + tile] = jnp.exp2(scores * scale).astype(BF16)
        summed = matmul(p_scr[quad % 2], ext_scr[...])
        summed = summed[:, :LANES] / summed[:, LANES:]
        for pair in range(2):
            even = summed[2 * pair * share : (2 * pair + 1) * share]
            odd = summed[(2 * pair + 1) * share : (2 * pair + 2) * share]
            at = slice(quad * QUAD + pair * LANES, quad * QUAD + (pair + 1) * LANES)
            sum_ref[:share, at] = jnp.where(left, even, pltpu.roll(odd, HDIM, 1)).astype(BF16)
            sum_ref[share:, at] = jnp.where(left, pltpu.roll(even, HDIM, 1), odd).astype(BF16)


def finish_kernel(count, shares, high, margin_ref, *refs):
    first_ref, second_ref, direct_ref, back_ref, far_ref, near_ref = refs[:6]
    rows_ref, packed_first, packed_second, all_scr, square_scr = refs[6:]
    width = back_ref.shape[0]
    depth = back_ref.shape[1] - LANES
    share = first_ref.shape[0] // 2
    full = width * count
    total = share * count
    part = width // shares
    channels = direct_ref.shape[0] // 2
    group_pos = lax.axis_index("group")
    seq_pos = lax.axis_index("seq")
    sub = lax.rem(group_pos, shares)
    all_scr[:width, :] = back_ref[...]
    all_scr[full:, :] = direct_ref[...]
    for i, m in enumerate(high):
        for near, ref in ((0, far_ref), (1, near_ref)):
            place = jnp.bitwise_xor(sub, m ^ near) * part
            for k in range(1, count):
                all_scr[pl.ds(pl.multiple_of(place + k * width, part), part), :] = ref[i, k - 1]
    tile = 2 * LANES
    known = jnp.concatenate([first_ref[...], second_ref[...]], axis=0)
    for start in range(0, depth, tile):
        mixed = matmul(known, all_scr[:, start : start + tile])
        squares = mixed * mixed
        squares = squares[:, :LANES] + squares[:, LANES:]
        square_scr[...] = squares if start == 0 else square_scr[...] + squares
    score = matmul(known, all_scr[:, depth:])
    variance = jnp.sum(square_scr[...], axis=-1, keepdims=True) * (1.0 / depth)
    score = (score + pltpu.roll(score, channels, 1)) * lax.rsqrt(variance + 1e-05)
    position = iota((share, LANES), 0) + seq_pos * share
    left = iota((share // 2, LANES), 1) < channels
    for window, packed_ref in enumerate((packed_first, packed_second)):
        at = 2 * share * window
        own = total - margin_at(margin_ref, 2 * group_pos + window)
        margin = jnp.where(position >= own, score[at + share : at + 2 * share], 0.0)
        signed = score[at : at + share] - margin
        rows_ref[window] = signed
        packed_ref[...] = jnp.where(left, signed[: share // 2], signed[share // 2 :]).astype(BF16)


def combine_kernel(count, deltas, margin_ref, latent_ref, rows_ref, *refs):
    out_ref, tail_scr = refs[2 * len(deltas) :]
    channels, share = latent_ref.shape[1:]
    total = share * count
    group_pos = lax.axis_index("group")
    seq_pos = lax.axis_index("seq")
    for slot in range(2):
        before = margin_at(margin_ref, 2 * group_pos + slot - 1)
        own = total - margin_at(margin_ref, 2 * group_pos + slot)
        tail_scr[...] = jnp.zeros_like(tail_scr)
        for delta, ref in zip(deltas, refs[slot * len(deltas) : (slot + 1) * len(deltas)]):
            row = (seq_pos + delta) * share - (total - OVMAX)
            for half in range(2):
                value = ref[...].astype(F32)
                value = pltpu.roll(value, channels, 1) if half else value
                at = pl.ds(pl.multiple_of(row + half * (share // 2), share // 2), share // 2)
                tail_scr[at, :] = value
        moved = tail_scr[pl.ds(OVMAX - before + seq_pos * share, share), :]
        score = (rows_ref[slot] + moved).T[:channels]
        keep = iota(score.shape, 1) + seq_pos * share < own
        out_ref[slot] = jnp.where(keep, latent_ref[slot] + STEP * score, 0.0)


def body(latent, margin_len, in_weight, norm_gain, qkv_weight, out_weight, final_gain, head_out):
    count = lax.axis_size("seq")
    groups = lax.axis_size("group")
    share, channels = latent.shape[1:]
    total = share * count
    width, depth = out_weight.shape
    full = width * count
    shares = min(groups, width // 16)
    high = range(0, shares, 2)

    def across(value, group_by, pairs):
        moves = [
            (g * count + i, (g + group_by) * count + j)
            for g in range(groups)
            for i, j in pairs
            if 0 <= g + group_by < groups
        ]
        return lax.ppermute(value, ("group", "seq"), moves)

    def swap(value, bits):
        return lax.ppermute(value, "group", [(g, g ^ bits) for g in range(groups)])

    def gathered(value):
        return [lax.ppermute(value, "seq", [(i, (i + k) % count) for i in range(count)]) for k in range(1, count)]

    turned = latent.transpose(0, 2, 1)
    send, back, part, direct, gram = pl.pallas_call(
        functools.partial(fold_kernel, shares),
        out_shape=(
            jax.ShapeDtypeStruct((width + share, LANES), BF16),
            jax.ShapeDtypeStruct((width, depth + LANES), BF16),
            jax.ShapeDtypeStruct((width // shares, depth + LANES), BF16),
            jax.ShapeDtypeStruct((2 * channels, depth + LANES), BF16),
            jax.ShapeDtypeStruct((channels, 2 * LANES), BF16),
        ),
        in_specs=[VMEM] * 7,
        out_specs=(VMEM,) * 5,
        cost_estimate=pl.CostEstimate(flops=width * depth * 1200, bytes_accessed=8 * width * depth, transcendentals=0),
        name="fold",
    )(turned, in_weight, norm_gain[None, :], qkv_weight, out_weight, final_gain[None, :], head_out.T)
    own_part = jnp.stack(gathered(part))
    pieces = [send] + gathered(send)
    stacked = jnp.stack([piece[width:] for piece in pieces])
    following = across(stacked, -1, [(i, i) for i in range(count)])

    def attend(window):
        rows = 4 * share
        extra = [following] if window else []
        return pl.pallas_call(
            functools.partial(attend_kernel, count, window),
            out_shape=jax.ShapeDtypeStruct((2 * share, full + LANES), BF16),
            in_specs=[SMEM] + [VMEM] * (count + len(extra) + 1),
            out_specs=VMEM,
            scratch_shapes=[
                pltpu.VMEM((total, LANES), F32),
                pltpu.VMEM((OVMAX + total, LANES), F32),
                pltpu.VMEM((total, LANES), BF16),
                pltpu.VMEM((full, LANES), BF16),
                pltpu.VMEM((full, total), BF16),
                pltpu.VMEM((2, rows, QUAD), BF16),
                pltpu.VMEM((2, rows, total), BF16),
                pltpu.VMEM((total, QUAD), BF16),
            ],
            cost_estimate=pl.CostEstimate(
                flops=16 * share * total * full,
                bytes_accessed=4 * full * share,
                transcendentals=share * total * full // HDIM,
            ),
            name="attend",
        )(margin_len, *pieces, gram, *extra)

    first = attend(0)
    second = attend(1)
    planes = [swap(own_part, bits) for bits in high[1:]]
    far = jnp.stack([own_part] + planes)
    near = swap(far, 1)
    rows, *tails = pl.pallas_call(
        functools.partial(finish_kernel, count, shares, list(high)),
        out_shape=(
            jax.ShapeDtypeStruct((2, share, LANES), F32),
            jax.ShapeDtypeStruct((share // 2, LANES), BF16),
            jax.ShapeDtypeStruct((share // 2, LANES), BF16),
        ),
        in_specs=[SMEM] + [VMEM] * 6,
        out_specs=(VMEM, VMEM, VMEM),
        scratch_shapes=[
            pltpu.VMEM((full + 2 * channels, depth + LANES), BF16),
            pltpu.VMEM((4 * share, LANES), F32),
        ],
        cost_estimate=pl.CostEstimate(
            flops=8 * share * full * depth, bytes_accessed=2 * full * depth, transcendentals=0
        ),
        name="finish",
    )(margin_len, first, second, direct, back, far, near)

    deltas = list(range((total - OVMAX) // share, count))
    received = []
    for window, group_by in ((1, 1), (0, 0)):
        received += [across(tails[window], group_by, [(i, i - d) for i in range(d, count)]) for d in deltas]
    turned = pl.pallas_call(
        functools.partial(combine_kernel, count, deltas),
        out_shape=jax.ShapeDtypeStruct(turned.shape, F32),
        in_specs=[SMEM] + [VMEM] * (2 + len(received)),
        out_specs=VMEM,
        scratch_shapes=[pltpu.VMEM((OVMAX + total + share, LANES), F32)],
        name="combine",
    )(margin_len, turned, rows, *received)
    return turned.transpose(0, 2, 1)


def solution(mesh):
    in_specs = (
        P("group", "seq", None),
        P(),
        P(),
        P(),
        P(None, None, "seq"),
        P("seq", None),
        P(),
        P(),
    )
    out_specs = P("group", "seq", None)

    return jax.shard_map(body, mesh=mesh, in_specs=in_specs, out_specs=out_specs, check_vma=False)
```

```python
import functools
import math

import jax
import jax.numpy as jnp
from jax import lax
from jax.experimental import pallas as pl
from jax.experimental.pallas import tpu as pltpu
from jax.sharding import PartitionSpec as P

HDIM = 64
OVMAX = 512
LANES = 128
QUAD = 4 * HDIM
STEP = -0.5
F32 = jnp.float32
BF16 = jnp.bfloat16
VMEM = pl.BlockSpec(memory_space=pltpu.VMEM)
SMEM = pl.BlockSpec(memory_space=pltpu.SMEM)


def limit(mebibytes):
    return pltpu.CompilerParams(vmem_limit_bytes=mebibytes << 20)


def iota(shape, dim):
    return lax.broadcasted_iota(jnp.int32, shape, dim)


def matmul(lhs, rhs):
    return jnp.dot(lhs, rhs, preferred_element_type=F32)


def matmul_nt(lhs, rhs, precision=None):
    return lax.dot_general(lhs, rhs, (((1,), (1,)), ((), ())), precision=precision, preferred_element_type=F32)


def split(value):
    high = value.astype(BF16)
    return high, (value - high.astype(F32)).astype(BF16)


def margin_at(margin_ref, index):
    last = margin_ref.shape[0]
    length = margin_ref[jnp.clip(index, 0, last - 1)]
    return jnp.where((index >= 0) & (index < last), length, 0)


def fold_kernel(shares, in_ref, gain_ref, qkv_ref, out_ref, final_ref, head_ref, *refs):
    map_ref, back_ref, part_ref, direct_ref, gram_ref = refs
    weight = in_ref[...].astype(F32)
    channels, depth = weight.shape
    width = out_ref.shape[0]
    centered = weight - jnp.mean(weight, axis=-1, keepdims=True)
    both = jnp.concatenate(split(centered * gain_ref[...][None, :]), axis=0)

    def folded(which):
        product = matmul(both, qkv_ref[which])
        return product[:channels] + product[channels:]

    values = folded(2)
    tiled = jnp.concatenate([values] * (width // HDIM), axis=0)
    same = iota((width, width), 0) // channels == iota((width, width), 1) // HDIM
    high, low = split(jnp.where(same, tiled, 0.0))
    back = matmul(high, out_ref[...]) + matmul(low, out_ref[...])
    back = back - jnp.mean(back, axis=-1, keepdims=True)
    back_ref[:, :depth] = back.astype(BF16)

    pieces = split(back * final_ref[...][None, :]) + split(centered * final_ref[...][None, :])
    scores = matmul_nt(jnp.concatenate(pieces, axis=0), head_ref[...])
    left = iota((width, LANES), 1) < channels

    def halves(value):
        value = jnp.concatenate([value, value], axis=1)
        high, low = split(value)
        return jnp.where(left[: value.shape[0]], high.astype(F32), low.astype(F32)).astype(BF16)

    back_ref[:, depth:] = halves(scores[:width] + scores[width : 2 * width])
    rows = width // shares
    sub = lax.rem(lax.axis_index("group"), shares)
    part_ref[...] = back_ref[pl.ds(pl.multiple_of(sub * rows, rows), rows), :]

    map_ref[...] = jnp.concatenate([folded(0), folded(1)], axis=0).T.astype(BF16)

    high, low = split(centered)
    direct_ref[:channels, :depth] = high
    direct_ref[channels:, :depth] = low
    direct_ref[:channels, depth:] = halves(scores[2 * width : 2 * width + channels] + scores[2 * width + channels :])
    direct_ref[channels:, depth:] = jnp.zeros((channels, LANES), BF16)

    gram = matmul_nt(jnp.concatenate([high, low], axis=0), jnp.concatenate([high, low], axis=0))
    gram = (gram[:channels] + gram[channels:]) * (1.0 / depth)
    gram = gram + pltpu.roll(gram, channels, 1)
    first, rest = split(gram)
    rest = gram - first.astype(F32)
    second, third = split(rest)
    left = left[:channels]
    gram_ref[:, :LANES] = jnp.where(left, first.astype(F32), second.astype(F32)).astype(BF16)
    gram_ref[:, LANES:] = jnp.where(left, third.astype(F32), 0.0).astype(BF16)


def attend_kernel(count, window, margin_ref, *refs):
    piece_refs, refs = refs[:count], refs[count:]
    map_refs, refs = refs[:count], refs[count:]
    gram_ref, refs = refs[0], refs[1:]
    if window:
        next_ref, refs = refs[0], refs[1:]
    sum_ref, slot_scr, next_scr, win_scr, map_scr, key_scr, query_scr, p_scr, ext_scr = refs
    total = win_scr.shape[0]
    channels = gram_ref.shape[0]
    share = total // count
    full = map_scr.shape[0]
    width = full // count
    low = total - OVMAX
    group_pos = lax.axis_index("group")
    seq_pos = lax.axis_index("seq")
    over_len = margin_at(margin_ref, 2 * group_pos + window)
    own = total - over_len

    next_scr[:OVMAX, :] = jnp.zeros((OVMAX, LANES), F32)
    for k in range(count):
        source = jnp.bitwise_xor(seq_pos, k) * share
        at = pl.ds(pl.multiple_of(source, share), share)
        after = pl.ds(pl.multiple_of(source + OVMAX, share), share)
        slot = piece_refs[k][...].astype(F32)
        slot_scr[at, :] = pltpu.roll(slot, channels, 1) if window else slot
        next_scr[after, :] = next_ref[k].astype(F32) if window else pltpu.roll(slot, channels, 1)
        map_scr[k * width : (k + 1) * width, :] = map_refs[k][...]
    left = iota((OVMAX, LANES), 1) < channels
    for start in range(0, total, OVMAX):
        rows = slot_scr[start : start + OVMAX, :]
        if start >= low:
            tail = next_scr[pl.ds(over_len + (start - low), OVMAX), :]
            rows = jnp.where(iota(rows.shape, 0) + start < own, rows, tail)
        win_scr[start : start + OVMAX, :] = jnp.where(left, rows, 0.0).astype(BF16)

    def twice(tokens):
        tokens = tokens.astype(F32)
        return tokens + pltpu.roll(tokens, channels, 1)

    def bend(tokens, doubled):
        bent = matmul(tokens[:, :channels], gram_ref[...])
        return (bent[:, :LANES] + bent[:, LANES:]) * doubled

    def variance(bent):
        return jnp.maximum(jnp.sum(bent, axis=-1, keepdims=True), 0.0) + 1e-05

    win = win_scr[...]
    mine = win_scr[pl.ds(pl.multiple_of(seq_pos * share, share), share), :]
    mine_twice = twice(mine)
    sum_ref[:share, full:] = mine_twice.astype(BF16)
    sum_ref[share:, full:] = mine_twice.astype(BF16)
    query_eps = variance(bend(mine, mine_twice)) * 1e-06
    doubled = twice(win)
    bent = bend(win, doubled)
    ones = jnp.ones((16, LANES), BF16)
    key_eps = (jnp.maximum(matmul_nt(ones, bent.astype(BF16))[:1], 0.0) + 1e-05) * 1e-06

    scaled = doubled * lax.rsqrt(variance(bent))
    counted = (iota((total, LANES), 0) >= jnp.minimum(own, total - 1)).astype(F32)
    left = iota((total, LANES), 1) < channels
    ext_scr[:, :LANES] = jnp.where(left, scaled, scaled * counted).astype(BF16)
    ext_scr[:, LANES:] = jnp.where(left, 1.0, counted).astype(BF16)

    tile = min(total, 256)
    win_right = jnp.where(left, 0.0, doubled).astype(BF16)
    for start in range(0, total, tile):
        keys = matmul_nt(map_scr[...], win_right[start : start + tile]).reshape(full // HDIM, HDIM, tile)
        norm = jnp.mean(keys * keys, axis=1, keepdims=True)
        keys = keys * lax.rsqrt(norm + key_eps[None, :, start : start + tile])
        key_scr[:, start : start + tile] = keys.reshape(full, tile).astype(BF16)

    one_head = iota((QUAD, QUAD), 0) // HDIM == iota((QUAD, QUAD), 1) // HDIM
    spread = jnp.where(one_head, 1.0 / HDIM, 0.0).astype(BF16)
    head_of = iota((share, QUAD), 1) // HDIM
    scale = HDIM ** (-0.5) * math.log2(math.e)
    left = iota((share, LANES), 1) < channels
    for quad in range(full // QUAD):
        span = slice(quad * QUAD, (quad + 1) * QUAD)
        queries = matmul_nt(mine, map_scr[span, :])
        norm = matmul((queries * queries).astype(BF16), spread)
        queries = (queries * lax.rsqrt(norm + query_eps)).astype(BF16)
        for head in range(4):
            query_scr[quad % 2, head * share : (head + 1) * share, :] = jnp.where(
                head_of == head, queries, jnp.zeros_like(queries)
            )
        for start in range(0, total, tile):
            scores = matmul(query_scr[quad % 2], key_scr[span, start : start + tile])
            p_scr[quad % 2, :, start : start + tile] = jnp.exp2(scores * scale).astype(BF16)
        summed = matmul(p_scr[quad % 2], ext_scr[...])
        summed = summed[:, :LANES] / summed[:, LANES:]
        for pair in range(2):
            even = summed[2 * pair * share : (2 * pair + 1) * share]
            odd = summed[(2 * pair + 1) * share : (2 * pair + 2) * share]
            at = slice(quad * QUAD + pair * LANES, quad * QUAD + (pair + 1) * LANES)
            sum_ref[:share, at] = jnp.where(left, even, pltpu.roll(odd, HDIM, 1)).astype(BF16)
            sum_ref[share:, at] = jnp.where(left, pltpu.roll(even, HDIM, 1), odd).astype(BF16)


def finish_kernel(count, shares, high, margin_ref, *refs):
    first_ref, second_ref, direct_ref, back_ref, far_ref, near_ref = refs[:6]
    rows_ref, packed_first, packed_second, all_scr, square_scr = refs[6:]
    width = back_ref.shape[0]
    depth = back_ref.shape[1] - LANES
    share = first_ref.shape[0] // 2
    full = width * count
    total = share * count
    part = width // shares
    channels = direct_ref.shape[0] // 2
    group_pos = lax.axis_index("group")
    seq_pos = lax.axis_index("seq")
    sub = lax.rem(group_pos, shares)
    all_scr[:width, :] = back_ref[...]
    all_scr[full:, :] = direct_ref[...]
    for i, m in enumerate(high):
        for near, ref in ((0, far_ref), (1, near_ref)):
            place = jnp.bitwise_xor(sub, m ^ near) * part
            for k in range(1, count):
                all_scr[pl.ds(pl.multiple_of(place + k * width, part), part), :] = ref[i, k - 1]
    tile = 2 * LANES
    known = jnp.concatenate([first_ref[...], second_ref[...]], axis=0)
    for start in range(0, depth, tile):
        mixed = matmul(known, all_scr[:, start : start + tile])
        squares = mixed * mixed
        squares = squares[:, :LANES] + squares[:, LANES:]
        square_scr[...] = squares if start == 0 else square_scr[...] + squares
    score = matmul(known, all_scr[:, depth:])
    variance = jnp.sum(square_scr[...], axis=-1, keepdims=True) * (1.0 / depth)
    score = (score + pltpu.roll(score, channels, 1)) * lax.rsqrt(variance + 1e-05)
    position = iota((share, LANES), 0) + seq_pos * share
    left = iota((share // 2, LANES), 1) < channels
    for window, packed_ref in enumerate((packed_first, packed_second)):
        at = 2 * share * window
        own = total - margin_at(margin_ref, 2 * group_pos + window)
        margin = jnp.where(position >= own, score[at + share : at + 2 * share], 0.0)
        signed = score[at : at + share] - margin
        rows_ref[window] = signed
        packed_ref[...] = jnp.where(left, signed[: share // 2], signed[share // 2 :]).astype(BF16)


def combine_kernel(count, deltas, margin_ref, latent_ref, rows_ref, *refs):
    out_ref, tail_scr = refs[2 * len(deltas) :]
    channels, share = latent_ref.shape[1:]
    total = share * count
    group_pos = lax.axis_index("group")
    seq_pos = lax.axis_index("seq")
    for slot in range(2):
        before = margin_at(margin_ref, 2 * group_pos + slot - 1)
        own = total - margin_at(margin_ref, 2 * group_pos + slot)
        tail_scr[...] = jnp.zeros_like(tail_scr)
        for delta, ref in zip(deltas, refs[slot * len(deltas) : (slot + 1) * len(deltas)]):
            row = (seq_pos + delta) * share - (total - OVMAX)
            for half in range(2):
                value = ref[...].astype(F32)
                value = pltpu.roll(value, channels, 1) if half else value
                at = pl.ds(pl.multiple_of(row + half * (share // 2), share // 2), share // 2)
                tail_scr[at, :] = value
        moved = tail_scr[pl.ds(OVMAX - before + seq_pos * share, share), :]
        score = (rows_ref[slot] + moved).T[:channels]
        keep = iota(score.shape, 1) + seq_pos * share < own
        out_ref[slot] = jnp.where(keep, latent_ref[slot] + STEP * score, 0.0)


def body(latent, margin_len, in_weight, norm_gain, qkv_weight, out_weight, final_gain, head_out):
    count = lax.axis_size("seq")
    groups = lax.axis_size("group")
    share, channels = latent.shape[1:]
    total = share * count
    width, depth = out_weight.shape
    full = width * count
    shares = min(groups, width // 16)
    high = range(0, shares, 2)

    def across(value, group_by, pairs):
        moves = [
            (g * count + i, (g + group_by) * count + j)
            for g in range(groups)
            for i, j in pairs
            if 0 <= g + group_by < groups
        ]
        return lax.ppermute(value, ("group", "seq"), moves)

    def swap(value, bits):
        return lax.ppermute(value, "group", [(g, g ^ bits) for g in range(groups)])

    def gathered(value):
        return [lax.ppermute(value, "seq", [(i, i ^ k) for i in range(count)]) for k in range(1, count)]

    turned = latent.transpose(0, 2, 1)
    packed = jnp.concatenate([latent[0], latent[1]], axis=1).astype(BF16)
    pieces = [packed] + gathered(packed)
    stacked = jnp.stack(pieces)
    following = across(stacked, -1, [(i, i) for i in range(count)])
    maps, back, part, direct, gram = pl.pallas_call(
        functools.partial(fold_kernel, shares),
        out_shape=(
            jax.ShapeDtypeStruct((width, LANES), BF16),
            jax.ShapeDtypeStruct((width, depth + LANES), BF16),
            jax.ShapeDtypeStruct((width // shares, depth + LANES), BF16),
            jax.ShapeDtypeStruct((2 * channels, depth + LANES), BF16),
            jax.ShapeDtypeStruct((channels, 2 * LANES), BF16),
        ),
        in_specs=[VMEM] * 6,
        compiler_params=limit(20),
        out_specs=(VMEM,) * 5,
        cost_estimate=pl.CostEstimate(flops=width * depth * 1200, bytes_accessed=8 * width * depth, transcendentals=0),
        name="fold",
    )(in_weight, norm_gain, qkv_weight, out_weight, final_gain, head_out.T)
    own_part = jnp.stack(gathered(part))
    map_pieces = [maps] + gathered(maps)

    def attend(window):
        rows = 4 * share
        extra = [following] if window else []
        return pl.pallas_call(
            functools.partial(attend_kernel, count, window),
            out_shape=jax.ShapeDtypeStruct((2 * share, full + LANES), BF16),
            in_specs=[SMEM] + [VMEM] * (2 * count + len(extra) + 1),
            compiler_params=limit(32),
            out_specs=VMEM,
            scratch_shapes=[
                pltpu.VMEM((total, LANES), F32),
                pltpu.VMEM((OVMAX + total, LANES), F32),
                pltpu.VMEM((total, LANES), BF16),
                pltpu.VMEM((full, LANES), BF16),
                pltpu.VMEM((full, total), BF16),
                pltpu.VMEM((2, rows, QUAD), BF16),
                pltpu.VMEM((2, rows, total), BF16),
                pltpu.VMEM((total, QUAD), BF16),
            ],
            cost_estimate=pl.CostEstimate(
                flops=16 * share * total * full,
                bytes_accessed=4 * full * share,
                transcendentals=share * total * full // HDIM,
            ),
            name="attend",
        )(margin_len, *pieces, *map_pieces, gram, *extra)

    first = attend(0)
    second = attend(1)
    planes = [swap(own_part, bits) for bits in high[1:]]
    far = jnp.stack([own_part] + planes)
    near = swap(far, 1)
    rows, *tails = pl.pallas_call(
        functools.partial(finish_kernel, count, shares, list(high)),
        out_shape=(
            jax.ShapeDtypeStruct((2, share, LANES), F32),
            jax.ShapeDtypeStruct((share // 2, LANES), BF16),
            jax.ShapeDtypeStruct((share // 2, LANES), BF16),
        ),
        in_specs=[SMEM] + [VMEM] * 6,
        compiler_params=limit(24),
        out_specs=(VMEM, VMEM, VMEM),
        scratch_shapes=[
            pltpu.VMEM((full + 2 * channels, depth + LANES), BF16),
            pltpu.VMEM((4 * share, LANES), F32),
        ],
        cost_estimate=pl.CostEstimate(
            flops=8 * share * full * depth, bytes_accessed=2 * full * depth, transcendentals=0
        ),
        name="finish",
    )(margin_len, first, second, direct, back, far, near)

    deltas = list(range((total - OVMAX) // share, count))
    received = []
    for window, group_by in ((1, 1), (0, 0)):
        received += [across(tails[window], group_by, [(i, i - d) for i in range(d, count)]) for d in deltas]
    turned = pl.pallas_call(
        functools.partial(combine_kernel, count, deltas),
        out_shape=jax.ShapeDtypeStruct(turned.shape, F32),
        in_specs=[SMEM] + [VMEM] * (2 + len(received)),
        compiler_params=limit(8),
        out_specs=VMEM,
        scratch_shapes=[pltpu.VMEM((OVMAX + total + share, LANES), F32)],
        name="combine",
    )(margin_len, turned, rows, *received)
    return turned.transpose(0, 2, 1)


def solution(mesh):
    in_specs = (
        P("group", "seq", None),
        P(),
        P(),
        P(),
        P(None, None, "seq"),
        P("seq", None),
        P(),
        P(),
    )
    out_specs = P("group", "seq", None)

    return jax.shard_map(body, mesh=mesh, in_specs=in_specs, out_specs=out_specs, check_vma=False)
```

```python
import functools
import math

import jax
import jax.numpy as jnp
from jax import lax
from jax.experimental import pallas as pl
from jax.experimental.pallas import tpu as pltpu
from jax.sharding import PartitionSpec as P

HDIM = 64
OVMAX = 512
LANES = 128
QUAD = 4 * HDIM
STEP = -0.5
F32 = jnp.float32
BF16 = jnp.bfloat16
VMEM = pl.BlockSpec(memory_space=pltpu.VMEM)
SMEM = pl.BlockSpec(memory_space=pltpu.SMEM)


def limit(mebibytes):
    return pltpu.CompilerParams(vmem_limit_bytes=mebibytes << 20)


def iota(shape, dim):
    return lax.broadcasted_iota(jnp.int32, shape, dim)


def matmul(lhs, rhs):
    return jnp.dot(lhs, rhs, preferred_element_type=F32)


def matmul_nt(lhs, rhs, precision=None):
    return lax.dot_general(lhs, rhs, (((1,), (1,)), ((), ())), precision=precision, preferred_element_type=F32)


def split(value):
    high = value.astype(BF16)
    return high, (value - high.astype(F32)).astype(BF16)


def margin_at(margin_ref, index):
    last = margin_ref.shape[0]
    length = margin_ref[jnp.clip(index, 0, last - 1)]
    return jnp.where((index >= 0) & (index < last), length, 0)


def fold_kernel(shares, in_hbm, gain_hbm, qkv_hbm, out_hbm, final_hbm, head_hbm, *refs):
    map_ref, back_ref, part_ref, direct_ref, gram_ref = refs[:5]
    in_ref, gain_ref, qkv_ref, out_ref, final_ref, head_ref, sem = refs[5:]
    pairs = [(in_hbm, in_ref), (gain_hbm, gain_ref), (qkv_hbm.at[2], qkv_ref.at[2]), (out_hbm, out_ref)]
    pairs += [(final_hbm, final_ref), (head_hbm, head_ref)]
    pairs += [(qkv_hbm.at[0], qkv_ref.at[0]), (qkv_hbm.at[1], qkv_ref.at[1])]
    copies = [pltpu.make_async_copy(source, target, sem.at[i]) for i, (source, target) in enumerate(pairs)]
    for copy in copies:
        copy.start()
    copies[0].wait()
    copies[1].wait()
    weight = in_ref[...].astype(F32)
    channels, depth = weight.shape
    width = out_ref.shape[0]
    centered = weight - jnp.mean(weight, axis=-1, keepdims=True)
    both = jnp.concatenate(split(centered * gain_ref[...][None, :]), axis=0)

    def folded(which):
        product = matmul(both, qkv_ref[which])
        return product[:channels] + product[channels:]

    copies[2].wait()
    values = folded(2)
    copies[3].wait()
    tiled = jnp.concatenate([values] * (width // HDIM), axis=0)
    same = iota((width, width), 0) // channels == iota((width, width), 1) // HDIM
    high, low = split(jnp.where(same, tiled, 0.0))
    back = matmul(high, out_ref[...]) + matmul(low, out_ref[...])
    back = back - jnp.mean(back, axis=-1, keepdims=True)
    back_ref[:, :depth] = back.astype(BF16)

    copies[4].wait()
    copies[5].wait()
    pieces = split(back * final_ref[...][None, :]) + split(centered * final_ref[...][None, :])
    scores = matmul_nt(jnp.concatenate(pieces, axis=0), head_ref[...])
    left = iota((width, LANES), 1) < channels

    def halves(value):
        value = jnp.concatenate([value, value], axis=1)
        high, low = split(value)
        return jnp.where(left[: value.shape[0]], high.astype(F32), low.astype(F32)).astype(BF16)

    back_ref[:, depth:] = halves(scores[:width] + scores[width : 2 * width])
    rows = width // shares
    sub = lax.rem(lax.axis_index("group"), shares)
    part_ref[...] = back_ref[pl.ds(pl.multiple_of(sub * rows, rows), rows), :]

    copies[6].wait()
    copies[7].wait()
    map_ref[...] = jnp.concatenate([folded(0), folded(1)], axis=0).T.astype(BF16)

    high, low = split(centered)
    direct_ref[:channels, :depth] = high
    direct_ref[channels:, :depth] = low
    direct_ref[:channels, depth:] = halves(scores[2 * width : 2 * width + channels] + scores[2 * width + channels :])
    direct_ref[channels:, depth:] = jnp.zeros((channels, LANES), BF16)

    gram = matmul_nt(jnp.concatenate([high, low], axis=0), jnp.concatenate([high, low], axis=0))
    gram = (gram[:channels] + gram[channels:]) * (1.0 / depth)
    gram = gram + pltpu.roll(gram, channels, 1)
    first, rest = split(gram)
    rest = gram - first.astype(F32)
    second, third = split(rest)
    left = left[:channels]
    gram_ref[:, :LANES] = jnp.where(left, first.astype(F32), second.astype(F32)).astype(BF16)
    gram_ref[:, LANES:] = jnp.where(left, third.astype(F32), 0.0).astype(BF16)


def attend_kernel(count, window, margin_ref, *refs):
    piece_refs, refs = refs[:count], refs[count:]
    map_refs, refs = refs[:count], refs[count:]
    gram_ref, refs = refs[0], refs[1:]
    if window:
        next_ref, refs = refs[0], refs[1:]
    sum_ref, slot_scr, next_scr, win_scr, map_scr, key_scr, query_scr, p_scr, ext_scr = refs
    total = win_scr.shape[0]
    channels = gram_ref.shape[0]
    share = total // count
    full = map_scr.shape[0]
    width = full // count
    low = total - OVMAX
    group_pos = lax.axis_index("group")
    seq_pos = lax.axis_index("seq")
    over_len = margin_at(margin_ref, 2 * group_pos + window)
    own = total - over_len

    next_scr[:OVMAX, :] = jnp.zeros((OVMAX, LANES), F32)
    for k in range(count):
        source = jnp.bitwise_xor(seq_pos, k) * share
        at = pl.ds(pl.multiple_of(source, share), share)
        after = pl.ds(pl.multiple_of(source + OVMAX, share), share)
        slot = piece_refs[k][...].astype(F32)
        slot_scr[at, :] = pltpu.roll(slot, channels, 1) if window else slot
        next_scr[after, :] = next_ref[k].astype(F32) if window else pltpu.roll(slot, channels, 1)
        map_scr[k * width : (k + 1) * width, :] = map_refs[k][...]
    left = iota((OVMAX, LANES), 1) < channels
    for start in range(0, total, OVMAX):
        rows = slot_scr[start : start + OVMAX, :]
        if start >= low:
            tail = next_scr[pl.ds(over_len + (start - low), OVMAX), :]
            rows = jnp.where(iota(rows.shape, 0) + start < own, rows, tail)
        win_scr[start : start + OVMAX, :] = jnp.where(left, rows, 0.0).astype(BF16)

    def twice(tokens):
        tokens = tokens.astype(F32)
        return tokens + pltpu.roll(tokens, channels, 1)

    def bend(tokens, doubled):
        bent = matmul(tokens[:, :channels], gram_ref[...])
        return (bent[:, :LANES] + bent[:, LANES:]) * doubled

    def variance(bent):
        return jnp.maximum(jnp.sum(bent, axis=-1, keepdims=True), 0.0) + 1e-05

    win = win_scr[...]
    mine = win_scr[pl.ds(pl.multiple_of(seq_pos * share, share), share), :]
    mine_twice = twice(mine)
    sum_ref[:share, full:] = mine_twice.astype(BF16)
    sum_ref[share:, full:] = mine_twice.astype(BF16)
    query_eps = variance(bend(mine, mine_twice)) * 1e-06
    doubled = twice(win)
    bent = bend(win, doubled)
    ones = jnp.ones((16, LANES), BF16)
    key_eps = (jnp.maximum(matmul_nt(ones, bent.astype(BF16))[:1], 0.0) + 1e-05) * 1e-06

    scaled = doubled * lax.rsqrt(variance(bent))
    counted = (iota((total, LANES), 0) >= jnp.minimum(own, total - 1)).astype(F32)
    left = iota((total, LANES), 1) < channels
    ext_scr[:, :LANES] = jnp.where(left, scaled, scaled * counted).astype(BF16)
    ext_scr[:, LANES:] = jnp.where(left, 1.0, counted).astype(BF16)

    tile = min(total, 256)
    win_right = jnp.where(left, 0.0, doubled).astype(BF16)
    for start in range(0, total, tile):
        keys = matmul_nt(map_scr[...], win_right[start : start + tile]).reshape(full // HDIM, HDIM, tile)
        norm = jnp.mean(keys * keys, axis=1, keepdims=True)
        keys = keys * lax.rsqrt(norm + key_eps[None, :, start : start + tile])
        key_scr[:, start : start + tile] = keys.reshape(full, tile).astype(BF16)

    one_head = iota((QUAD, QUAD), 0) // HDIM == iota((QUAD, QUAD), 1) // HDIM
    spread = jnp.where(one_head, 1.0 / HDIM, 0.0).astype(BF16)
    head_of = iota((share, QUAD), 1) // HDIM
    scale = HDIM ** (-0.5) * math.log2(math.e)
    left = iota((share, LANES), 1) < channels
    for quad in range(full // QUAD):
        span = slice(quad * QUAD, (quad + 1) * QUAD)
        queries = matmul_nt(mine, map_scr[span, :])
        norm = matmul((queries * queries).astype(BF16), spread)
        queries = (queries * lax.rsqrt(norm + query_eps)).astype(BF16)
        for head in range(4):
            query_scr[quad % 2, head * share : (head + 1) * share, :] = jnp.where(
                head_of == head, queries, jnp.zeros_like(queries)
            )
        for start in range(0, total, tile):
            scores = matmul(query_scr[quad % 2], key_scr[span, start : start + tile])
            p_scr[quad % 2, :, start : start + tile] = jnp.exp2(scores * scale).astype(BF16)
        summed = matmul(p_scr[quad % 2], ext_scr[...])
        summed = summed[:, :LANES] / summed[:, LANES:]
        for pair in range(2):
            even = summed[2 * pair * share : (2 * pair + 1) * share]
            odd = summed[(2 * pair + 1) * share : (2 * pair + 2) * share]
            at = slice(quad * QUAD + pair * LANES, quad * QUAD + (pair + 1) * LANES)
            sum_ref[:share, at] = jnp.where(left, even, pltpu.roll(odd, HDIM, 1)).astype(BF16)
            sum_ref[share:, at] = jnp.where(left, pltpu.roll(even, HDIM, 1), odd).astype(BF16)


def score_window(count, window, known, all_ref, square_scr, margin_ref, rows_ref, packed_ref):
    depth = all_ref.shape[1] - LANES
    share = rows_ref.shape[0]
    total = share * count
    channels = LANES // 2
    tile = 2 * LANES
    for start in range(0, depth, tile):
        mixed = matmul(known, all_ref[:, start : start + tile])
        squares = mixed * mixed
        squares = squares[:, :LANES] + squares[:, LANES:]
        square_scr[...] = squares if start == 0 else square_scr[...] + squares
    score = matmul(known, all_ref[:, depth:])
    variance = jnp.sum(square_scr[...], axis=-1, keepdims=True) * (1.0 / depth)
    score = (score + pltpu.roll(score, channels, 1)) * lax.rsqrt(variance + 1e-05)
    position = iota((share, LANES), 0) + lax.axis_index("seq") * share
    left = iota((share // 2, LANES), 1) < channels
    own = total - margin_at(margin_ref, 2 * lax.axis_index("group") + window)
    signed = score[:share] - jnp.where(position >= own, score[share:], 0.0)
    rows_ref[...] = signed
    packed_ref[...] = jnp.where(left, signed[: share // 2], signed[share // 2 :]).astype(BF16)


def finish_second_kernel(count, shares, high, margin_ref, known_ref, direct_ref, back_ref, far_ref, near_ref, *refs):
    rows_ref, packed_ref, all_ref, square_scr = refs
    width = back_ref.shape[0]
    part = width // shares
    sub = lax.rem(lax.axis_index("group"), shares)
    all_ref[:width, :] = back_ref[...]
    all_ref[width * count :, :] = direct_ref[...]
    for i, m in enumerate(high):
        for near, ref in ((0, far_ref), (1, near_ref)):
            place = jnp.bitwise_xor(sub, m ^ near) * part
            for k in range(1, count):
                all_ref[pl.ds(pl.multiple_of(place + k * width, part), part), :] = ref[i, k - 1]
    score_window(count, 1, known_ref[...], all_ref, square_scr, margin_ref, rows_ref, packed_ref)


def finish_first_kernel(count, margin_ref, known_ref, all_ref, rows_ref, packed_ref, square_scr):
    score_window(count, 0, known_ref[...], all_ref, square_scr, margin_ref, rows_ref, packed_ref)


def combine_kernel(count, deltas, margin_ref, latent_ref, first_ref, second_ref, *refs):
    out_ref, tail_scr = refs[2 * len(deltas) :]
    channels, share = latent_ref.shape[1:]
    total = share * count
    group_pos = lax.axis_index("group")
    seq_pos = lax.axis_index("seq")
    for slot, rows_ref in enumerate((first_ref, second_ref)):
        before = margin_at(margin_ref, 2 * group_pos + slot - 1)
        own = total - margin_at(margin_ref, 2 * group_pos + slot)
        tail_scr[...] = jnp.zeros_like(tail_scr)
        for delta, ref in zip(deltas, refs[slot * len(deltas) : (slot + 1) * len(deltas)]):
            row = (seq_pos + delta) * share - (total - OVMAX)
            for half in range(2):
                value = ref[...].astype(F32)
                value = pltpu.roll(value, channels, 1) if half else value
                at = pl.ds(pl.multiple_of(row + half * (share // 2), share // 2), share // 2)
                tail_scr[at, :] = value
        moved = tail_scr[pl.ds(OVMAX - before + seq_pos * share, share), :]
        score = (rows_ref[...] + moved).T[:channels]
        keep = iota(score.shape, 1) + seq_pos * share < own
        out_ref[slot] = jnp.where(keep, latent_ref[slot] + STEP * score, 0.0)


def body(latent, margin_len, in_weight, norm_gain, qkv_weight, out_weight, final_gain, head_out):
    count = lax.axis_size("seq")
    groups = lax.axis_size("group")
    share, channels = latent.shape[1:]
    total = share * count
    width, depth = out_weight.shape
    full = width * count
    shares = min(groups, width // 16)
    high = range(0, shares, 2)

    def across(value, group_by, pairs):
        moves = [
            (g * count + i, (g + group_by) * count + j)
            for g in range(groups)
            for i, j in pairs
            if 0 <= g + group_by < groups
        ]
        return lax.ppermute(value, ("group", "seq"), moves)

    def swap(value, bits):
        return lax.ppermute(value, "group", [(g, g ^ bits) for g in range(groups)])

    def gathered(value):
        return [lax.ppermute(value, "seq", [(i, i ^ k) for i in range(count)]) for k in range(1, count)]

    turned = latent.transpose(0, 2, 1)
    packed = jnp.concatenate([latent[0], latent[1]], axis=1).astype(BF16)
    pieces = [packed] + gathered(packed)
    stacked = jnp.stack(pieces)
    following = across(stacked, -1, [(i, i) for i in range(count)])
    maps, back, part, direct, gram = pl.pallas_call(
        functools.partial(fold_kernel, shares),
        out_shape=(
            jax.ShapeDtypeStruct((width, LANES), BF16),
            jax.ShapeDtypeStruct((width, depth + LANES), BF16),
            jax.ShapeDtypeStruct((width // shares, depth + LANES), BF16),
            jax.ShapeDtypeStruct((2 * channels, depth + LANES), BF16),
            jax.ShapeDtypeStruct((channels, 2 * LANES), BF16),
        ),
        in_specs=[pl.BlockSpec(memory_space=pltpu.HBM)] * 6,
        compiler_params=limit(20),
        out_specs=(VMEM,) * 5,
        scratch_shapes=[
            pltpu.VMEM(in_weight.shape, BF16),
            pltpu.VMEM(norm_gain.shape, F32),
            pltpu.VMEM(qkv_weight.shape, BF16),
            pltpu.VMEM(out_weight.shape, BF16),
            pltpu.VMEM(final_gain.shape, F32),
            pltpu.VMEM(head_out.shape[::-1], BF16),
            pltpu.SemaphoreType.DMA((8,)),
        ],
        cost_estimate=pl.CostEstimate(flops=width * depth * 1200, bytes_accessed=8 * width * depth, transcendentals=0),
        name="fold",
    )(in_weight, norm_gain, qkv_weight, out_weight, final_gain, head_out.T)
    own_part = jnp.stack(gathered(part))
    map_pieces = [maps] + gathered(maps)

    def attend(window):
        rows = 4 * share
        extra = [following] if window else []
        return pl.pallas_call(
            functools.partial(attend_kernel, count, window),
            out_shape=jax.ShapeDtypeStruct((2 * share, full + LANES), BF16),
            in_specs=[SMEM] + [VMEM] * (2 * count + len(extra) + 1),
            compiler_params=limit(32),
            out_specs=VMEM,
            scratch_shapes=[
                pltpu.VMEM((total, LANES), F32),
                pltpu.VMEM((OVMAX + total, LANES), F32),
                pltpu.VMEM((total, LANES), BF16),
                pltpu.VMEM((full, LANES), BF16),
                pltpu.VMEM((full, total), BF16),
                pltpu.VMEM((2, rows, QUAD), BF16),
                pltpu.VMEM((2, rows, total), BF16),
                pltpu.VMEM((total, QUAD), BF16),
            ],
            cost_estimate=pl.CostEstimate(
                flops=16 * share * total * full,
                bytes_accessed=4 * full * share,
                transcendentals=share * total * full // HDIM,
            ),
            name="attend",
        )(margin_len, *pieces, *map_pieces, gram, *extra)

    first = attend(0)
    second = attend(1)
    planes = [swap(own_part, bits) for bits in high[1:]]
    far = jnp.stack([own_part] + planes)
    near = swap(far, 1)
    scored = (
        jax.ShapeDtypeStruct((share, LANES), F32),
        jax.ShapeDtypeStruct((share // 2, LANES), BF16),
    )
    squares = pltpu.VMEM((2 * share, LANES), F32)
    cost = pl.CostEstimate(flops=4 * share * full * depth, bytes_accessed=2 * full * depth, transcendentals=0)
    rows_second, tail_second, all_maps = pl.pallas_call(
        functools.partial(finish_second_kernel, count, shares, list(high)),
        out_shape=scored + (jax.ShapeDtypeStruct((full + 2 * channels, depth + LANES), BF16),),
        in_specs=[SMEM] + [VMEM] * 5,
        compiler_params=limit(20),
        out_specs=(VMEM,) * 3,
        scratch_shapes=[squares],
        cost_estimate=cost,
        name="finish_second",
    )(margin_len, second, direct, back, far, near)
    deltas = list(range((total - OVMAX) // share, count))

    def tails(value, group_by):
        return [across(value, group_by, [(i, i - d) for i in range(d, count)]) for d in deltas]

    received = tails(tail_second, 1)
    rows_first, tail_first = pl.pallas_call(
        functools.partial(finish_first_kernel, count),
        out_shape=scored,
        in_specs=[SMEM] + [VMEM] * 2,
        compiler_params=limit(20),
        out_specs=(VMEM,) * 2,
        scratch_shapes=[squares],
        cost_estimate=cost,
        name="finish_first",
    )(margin_len, first, all_maps)
    received += tails(tail_first, 0)
    turned = pl.pallas_call(
        functools.partial(combine_kernel, count, deltas),
        out_shape=jax.ShapeDtypeStruct(turned.shape, F32),
        in_specs=[SMEM] + [VMEM] * (3 + len(received)),
        compiler_params=limit(8),
        out_specs=VMEM,
        scratch_shapes=[pltpu.VMEM((OVMAX + total + share, LANES), F32)],
        name="combine",
    )(margin_len, turned, rows_first, rows_second, *received)
    return turned.transpose(0, 2, 1)


def solution(mesh):
    in_specs = (
        P("group", "seq", None),
        P(),
        P(),
        P(),
        P(None, None, "seq"),
        P("seq", None),
        P(),
        P(),
    )
    out_specs = P("group", "seq", None)

    return jax.shard_map(body, mesh=mesh, in_specs=in_specs, out_specs=out_specs, check_vma=False)
```

```python
import functools
import math

import jax
import jax.numpy as jnp
from jax import lax
from jax.experimental import pallas as pl
from jax.experimental.pallas import tpu as pltpu
from jax.sharding import PartitionSpec as P

HDIM = 64
OVMAX = 512
LANES = 128
QUAD = 4 * HDIM
STEP = -0.5
F32 = jnp.float32
BF16 = jnp.bfloat16
VMEM = pl.BlockSpec(memory_space=pltpu.VMEM)
SMEM = pl.BlockSpec(memory_space=pltpu.SMEM)


def limit(mebibytes):
    return pltpu.CompilerParams(vmem_limit_bytes=mebibytes << 20)


def iota(shape, dim):
    return lax.broadcasted_iota(jnp.int32, shape, dim)


def matmul(lhs, rhs):
    return jnp.dot(lhs, rhs, preferred_element_type=F32)


def matmul_nt(lhs, rhs, precision=None):
    return lax.dot_general(lhs, rhs, (((1,), (1,)), ((), ())), precision=precision, preferred_element_type=F32)


def split(value):
    high = value.astype(BF16)
    return high, (value - high.astype(F32)).astype(BF16)


def margin_at(margin_ref, index):
    last = margin_ref.shape[0]
    length = margin_ref[jnp.clip(index, 0, last - 1)]
    return jnp.where((index >= 0) & (index < last), length, 0)


def fold_kernel(shares, in_hbm, gain_hbm, qkv_hbm, out_hbm, final_hbm, head_hbm, *refs):
    map_ref, back_ref, part_ref, direct_ref, gram_ref = refs[:5]
    in_ref, gain_ref, qkv_ref, out_ref, final_ref, head_ref, sem = refs[5:]
    pairs = [(in_hbm, in_ref), (gain_hbm, gain_ref), (qkv_hbm.at[2], qkv_ref.at[2]), (out_hbm, out_ref)]
    pairs += [(final_hbm, final_ref), (head_hbm, head_ref)]
    pairs += [(qkv_hbm.at[0], qkv_ref.at[0]), (qkv_hbm.at[1], qkv_ref.at[1])]
    copies = [pltpu.make_async_copy(source, target, sem.at[i]) for i, (source, target) in enumerate(pairs)]
    for copy in copies:
        copy.start()
    copies[0].wait()
    copies[1].wait()
    weight = in_ref[...].astype(F32)
    channels, depth = weight.shape
    width = out_ref.shape[0]
    centered = weight - jnp.mean(weight, axis=-1, keepdims=True)
    both = jnp.concatenate(split(centered * gain_ref[...][None, :]), axis=0)

    def folded(which):
        product = matmul(both, qkv_ref[which])
        return product[:channels] + product[channels:]

    copies[2].wait()
    values = folded(2)
    copies[3].wait()
    tiled = jnp.concatenate([values] * (width // HDIM), axis=0)
    same = iota((width, width), 0) // channels == iota((width, width), 1) // HDIM
    high, low = split(jnp.where(same, tiled, 0.0))
    back = matmul(high, out_ref[...]) + matmul(low, out_ref[...])
    back = back - jnp.mean(back, axis=-1, keepdims=True)
    back_ref[:, :depth] = back.astype(BF16)

    copies[4].wait()
    copies[5].wait()
    pieces = split(back * final_ref[...][None, :]) + split(centered * final_ref[...][None, :])
    scores = matmul_nt(jnp.concatenate(pieces, axis=0), head_ref[...])
    left = iota((width, LANES), 1) < channels

    def halves(value):
        value = jnp.concatenate([value, value], axis=1)
        high, low = split(value)
        return jnp.where(left[: value.shape[0]], high.astype(F32), low.astype(F32)).astype(BF16)

    back_ref[:, depth:] = halves(scores[:width] + scores[width : 2 * width])
    rows = width // shares
    sub = lax.rem(lax.axis_index("group"), shares)
    part_ref[...] = back_ref[pl.ds(pl.multiple_of(sub * rows, rows), rows), :]

    copies[6].wait()
    copies[7].wait()
    map_ref[...] = jnp.concatenate([folded(0), folded(1)], axis=0).T.astype(BF16)

    high, low = split(centered)
    direct_ref[:channels, :depth] = high
    direct_ref[channels:, :depth] = low
    direct_ref[:channels, depth:] = halves(scores[2 * width : 2 * width + channels] + scores[2 * width + channels :])
    direct_ref[channels:, depth:] = jnp.zeros((channels, LANES), BF16)

    gram = matmul_nt(jnp.concatenate([high, low], axis=0), jnp.concatenate([high, low], axis=0))
    gram = (gram[:channels] + gram[channels:]) * (1.0 / depth)
    gram = gram + pltpu.roll(gram, channels, 1)
    first, rest = split(gram)
    rest = gram - first.astype(F32)
    second, third = split(rest)
    left = left[:channels]
    gram_ref[:, :LANES] = jnp.where(left, first.astype(F32), second.astype(F32)).astype(BF16)
    gram_ref[:, LANES:] = jnp.where(left, third.astype(F32), 0.0).astype(BF16)


def attend_kernel(count, window, margin_ref, *refs):
    piece_refs, refs = refs[:count], refs[count:]
    map_refs, refs = refs[:count], refs[count:]
    gram_ref, refs = refs[0], refs[1:]
    if window:
        next_ref, refs = refs[0], refs[1:]
    sum_ref, slot_scr, next_scr, win_scr, map_scr, key_scr, query_scr, p_scr, ext_scr = refs
    total = win_scr.shape[0]
    channels = gram_ref.shape[0]
    share = total // count
    full = map_scr.shape[0]
    width = full // count
    low = total - OVMAX
    group_pos = lax.axis_index("group")
    seq_pos = lax.axis_index("seq")
    over_len = margin_at(margin_ref, 2 * group_pos + window)
    own = total - over_len

    next_scr[:OVMAX, :] = jnp.zeros((OVMAX, LANES), F32)
    for k in range(count):
        source = jnp.bitwise_xor(seq_pos, k) * share
        at = pl.ds(pl.multiple_of(source, share), share)
        after = pl.ds(pl.multiple_of(source + OVMAX, share), share)
        slot = piece_refs[k][...].astype(F32)
        slot_scr[at, :] = pltpu.roll(slot, channels, 1) if window else slot
        next_scr[after, :] = next_ref[k].astype(F32) if window else pltpu.roll(slot, channels, 1)
        map_scr[k * width : (k + 1) * width, :] = map_refs[k][...]
    left = iota((OVMAX, LANES), 1) < channels
    for start in range(0, total, OVMAX):
        rows = slot_scr[start : start + OVMAX, :]
        if start >= low:
            tail = next_scr[pl.ds(over_len + (start - low), OVMAX), :]
            rows = jnp.where(iota(rows.shape, 0) + start < own, rows, tail)
        win_scr[start : start + OVMAX, :] = jnp.where(left, rows, 0.0).astype(BF16)

    def twice(tokens):
        tokens = tokens.astype(F32)
        return tokens + pltpu.roll(tokens, channels, 1)

    def bend(tokens, doubled):
        bent = matmul(tokens[:, :channels], gram_ref[...])
        return (bent[:, :LANES] + bent[:, LANES:]) * doubled

    def variance(bent):
        return jnp.maximum(jnp.sum(bent, axis=-1, keepdims=True), 0.0) + 1e-05

    win = win_scr[...]
    mine = win_scr[pl.ds(pl.multiple_of(seq_pos * share, share), share), :]
    mine_twice = twice(mine)
    sum_ref[:share, full:] = mine_twice.astype(BF16)
    sum_ref[share:, full:] = mine_twice.astype(BF16)
    query_eps = variance(bend(mine, mine_twice)) * 1e-06
    doubled = twice(win)
    bent = bend(win, doubled)
    ones = jnp.ones((16, LANES), BF16)
    key_eps = (jnp.maximum(matmul_nt(ones, bent.astype(BF16))[:1], 0.0) + 1e-05) * 1e-06

    scaled = doubled * lax.rsqrt(variance(bent))
    counted = (iota((total, LANES), 0) >= jnp.minimum(own, total - 1)).astype(F32)
    left = iota((total, LANES), 1) < channels
    ext_scr[:, :LANES] = jnp.where(left, scaled, scaled * counted).astype(BF16)
    ext_scr[:, LANES:] = jnp.where(left, 1.0, counted).astype(BF16)

    tile = min(total, 256)
    win_right = jnp.where(left, 0.0, doubled).astype(BF16)
    for start in range(0, total, tile):
        keys = matmul_nt(map_scr[...], win_right[start : start + tile]).reshape(full // HDIM, HDIM, tile)
        norm = jnp.mean(keys * keys, axis=1, keepdims=True)
        keys = keys * lax.rsqrt(norm + key_eps[None, :, start : start + tile])
        key_scr[:, start : start + tile] = keys.reshape(full, tile).astype(BF16)

    one_head = iota((QUAD, QUAD), 0) // HDIM == iota((QUAD, QUAD), 1) // HDIM
    spread = jnp.where(one_head, 1.0 / HDIM, 0.0).astype(BF16)
    head_of = iota((share, QUAD), 1) // HDIM
    scale = HDIM ** (-0.5) * math.log2(math.e)
    left = iota((share, LANES), 1) < channels
    for quad in range(full // QUAD):
        span = slice(quad * QUAD, (quad + 1) * QUAD)
        queries = matmul_nt(mine, map_scr[span, :])
        norm = matmul((queries * queries).astype(BF16), spread)
        queries = (queries * lax.rsqrt(norm + query_eps)).astype(BF16)
        for head in range(4):
            query_scr[quad % 2, head * share : (head + 1) * share, :] = jnp.where(
                head_of == head, queries, jnp.zeros_like(queries)
            )
        for start in range(0, total, tile):
            scores = matmul(query_scr[quad % 2], key_scr[span, start : start + tile])
            p_scr[quad % 2, :, start : start + tile] = jnp.exp2(scores * scale).astype(BF16)
        summed = matmul(p_scr[quad % 2], ext_scr[...])
        summed = summed[:, :LANES] / summed[:, LANES:]
        for pair in range(2):
            even = summed[2 * pair * share : (2 * pair + 1) * share]
            odd = summed[(2 * pair + 1) * share : (2 * pair + 2) * share]
            at = slice(quad * QUAD + pair * LANES, quad * QUAD + (pair + 1) * LANES)
            sum_ref[:share, at] = jnp.where(left, even, pltpu.roll(odd, HDIM, 1)).astype(BF16)
            sum_ref[share:, at] = jnp.where(left, pltpu.roll(even, HDIM, 1), odd).astype(BF16)


def finish_kernel(count, shares, high, margin_ref, *refs):
    first_ref, second_ref, direct_ref, back_ref, far_ref, near_ref = refs[:6]
    rows_ref, packed_first, packed_second, all_scr, square_scr = refs[6:]
    width = back_ref.shape[0]
    depth = back_ref.shape[1] - LANES
    share = first_ref.shape[0] // 2
    full = width * count
    total = share * count
    part = width // shares
    channels = direct_ref.shape[0] // 2
    group_pos = lax.axis_index("group")
    seq_pos = lax.axis_index("seq")
    sub = lax.rem(group_pos, shares)
    all_scr[:width, :] = back_ref[...]
    all_scr[full:, :] = direct_ref[...]
    for i, m in enumerate(high):
        for near, ref in ((0, far_ref), (1, near_ref)):
            place = jnp.bitwise_xor(sub, m ^ near) * part
            for k in range(1, count):
                all_scr[pl.ds(pl.multiple_of(place + k * width, part), part), :] = ref[i, k - 1]
    tile = 2 * LANES
    known = jnp.concatenate([first_ref[...], second_ref[...]], axis=0)
    for start in range(0, depth, tile):
        mixed = matmul(known, all_scr[:, start : start + tile])
        squares = mixed * mixed
        squares = squares[:, :LANES] + squares[:, LANES:]
        square_scr[...] = squares if start == 0 else square_scr[...] + squares
    score = matmul(known, all_scr[:, depth:])
    variance = jnp.sum(square_scr[...], axis=-1, keepdims=True) * (1.0 / depth)
    score = (score + pltpu.roll(score, channels, 1)) * lax.rsqrt(variance + 1e-05)
    position = iota((share, LANES), 0) + seq_pos * share
    left = iota((share // 2, LANES), 1) < channels
    for window, packed_ref in enumerate((packed_first, packed_second)):
        at = 2 * share * window
        own = total - margin_at(margin_ref, 2 * group_pos + window)
        margin = jnp.where(position >= own, score[at + share : at + 2 * share], 0.0)
        signed = score[at : at + share] - margin
        rows_ref[window] = signed
        packed_ref[...] = jnp.where(left, signed[: share // 2], signed[share // 2 :]).astype(BF16)


def combine_kernel(count, deltas, margin_ref, latent_ref, rows_ref, *refs):
    out_ref, tail_scr = refs[2 * len(deltas) :]
    channels, share = latent_ref.shape[1:]
    total = share * count
    group_pos = lax.axis_index("group")
    seq_pos = lax.axis_index("seq")
    for slot in range(2):
        before = margin_at(margin_ref, 2 * group_pos + slot - 1)
        own = total - margin_at(margin_ref, 2 * group_pos + slot)
        tail_scr[...] = jnp.zeros_like(tail_scr)
        for delta, ref in zip(deltas, refs[slot * len(deltas) : (slot + 1) * len(deltas)]):
            row = (seq_pos + delta) * share - (total - OVMAX)
            for half in range(2):
                value = ref[...].astype(F32)
                value = pltpu.roll(value, channels, 1) if half else value
                at = pl.ds(pl.multiple_of(row + half * (share // 2), share // 2), share // 2)
                tail_scr[at, :] = value
        moved = tail_scr[pl.ds(OVMAX - before + seq_pos * share, share), :]
        score = (rows_ref[slot] + moved).T[:channels]
        keep = iota(score.shape, 1) + seq_pos * share < own
        out_ref[slot] = jnp.where(keep, latent_ref[slot] + STEP * score, 0.0)


def body(latent, margin_len, in_weight, norm_gain, qkv_weight, out_weight, final_gain, head_out):
    count = lax.axis_size("seq")
    groups = lax.axis_size("group")
    share, channels = latent.shape[1:]
    total = share * count
    width, depth = out_weight.shape
    full = width * count
    shares = min(groups, width // 16)
    high = range(0, shares, 2)

    def across(value, group_by, pairs):
        moves = [
            (g * count + i, (g + group_by) * count + j)
            for g in range(groups)
            for i, j in pairs
            if 0 <= g + group_by < groups
        ]
        return lax.ppermute(value, ("group", "seq"), moves)

    def swap(value, bits):
        return lax.ppermute(value, "group", [(g, g ^ bits) for g in range(groups)])

    def gathered(value):
        return [lax.ppermute(value, "seq", [(i, i ^ k) for i in range(count)]) for k in range(1, count)]

    turned = latent.transpose(0, 2, 1)
    packed = jnp.concatenate([latent[0], latent[1]], axis=1).astype(BF16)
    pieces = [packed] + gathered(packed)
    stacked = jnp.stack(pieces)
    following = across(stacked, -1, [(i, i) for i in range(count)])
    maps, back, part, direct, gram = pl.pallas_call(
        functools.partial(fold_kernel, shares),
        out_shape=(
            jax.ShapeDtypeStruct((width, LANES), BF16),
            jax.ShapeDtypeStruct((width, depth + LANES), BF16),
            jax.ShapeDtypeStruct((width // shares, depth + LANES), BF16),
            jax.ShapeDtypeStruct((2 * channels, depth + LANES), BF16),
            jax.ShapeDtypeStruct((channels, 2 * LANES), BF16),
        ),
        in_specs=[pl.BlockSpec(memory_space=pltpu.HBM)] * 6,
        compiler_params=limit(62),
        out_specs=(VMEM,) * 5,
        scratch_shapes=[
            pltpu.VMEM(in_weight.shape, BF16),
            pltpu.VMEM(norm_gain.shape, F32),
            pltpu.VMEM(qkv_weight.shape, BF16),
            pltpu.VMEM(out_weight.shape, BF16),
            pltpu.VMEM(final_gain.shape, F32),
            pltpu.VMEM(head_out.shape[::-1], BF16),
            pltpu.SemaphoreType.DMA((8,)),
        ],
        cost_estimate=pl.CostEstimate(flops=width * depth * 1200, bytes_accessed=8 * width * depth, transcendentals=0),
        name="fold",
    )(in_weight, norm_gain, qkv_weight, out_weight, final_gain, head_out.T)
    own_part = jnp.stack(gathered(part))
    map_pieces = [maps] + gathered(maps)

    def attend(window):
        rows = 4 * share
        extra = [following] if window else []
        return pl.pallas_call(
            functools.partial(attend_kernel, count, window),
            out_shape=jax.ShapeDtypeStruct((2 * share, full + LANES), BF16),
            in_specs=[SMEM] + [VMEM] * (2 * count + len(extra) + 1),
            compiler_params=limit(32),
            out_specs=VMEM,
            scratch_shapes=[
                pltpu.VMEM((total, LANES), F32),
                pltpu.VMEM((OVMAX + total, LANES), F32),
                pltpu.VMEM((total, LANES), BF16),
                pltpu.VMEM((full, LANES), BF16),
                pltpu.VMEM((full, total), BF16),
                pltpu.VMEM((2, rows, QUAD), BF16),
                pltpu.VMEM((2, rows, total), BF16),
                pltpu.VMEM((total, QUAD), BF16),
            ],
            cost_estimate=pl.CostEstimate(
                flops=16 * share * total * full,
                bytes_accessed=4 * full * share,
                transcendentals=share * total * full // HDIM,
            ),
            name="attend",
        )(margin_len, *pieces, *map_pieces, gram, *extra)

    first = attend(0)
    second = attend(1)
    planes = [swap(own_part, bits) for bits in high[1:]]
    far = jnp.stack([own_part] + planes)
    near = swap(far, 1)
    rows, *tails = pl.pallas_call(
        functools.partial(finish_kernel, count, shares, list(high)),
        out_shape=(
            jax.ShapeDtypeStruct((2, share, LANES), F32),
            jax.ShapeDtypeStruct((share // 2, LANES), BF16),
            jax.ShapeDtypeStruct((share // 2, LANES), BF16),
        ),
        in_specs=[SMEM] + [VMEM] * 6,
        compiler_params=limit(24),
        out_specs=(VMEM, VMEM, VMEM),
        scratch_shapes=[
            pltpu.VMEM((full + 2 * channels, depth + LANES), BF16),
            pltpu.VMEM((4 * share, LANES), F32),
        ],
        cost_estimate=pl.CostEstimate(
            flops=8 * share * full * depth, bytes_accessed=2 * full * depth, transcendentals=0
        ),
        name="finish",
    )(margin_len, first, second, direct, back, far, near)

    deltas = list(range((total - OVMAX) // share, count))
    received = []
    for window, group_by in ((1, 1), (0, 0)):
        received += [across(tails[window], group_by, [(i, i - d) for i in range(d, count)]) for d in deltas]
    turned = pl.pallas_call(
        functools.partial(combine_kernel, count, deltas),
        out_shape=jax.ShapeDtypeStruct(turned.shape, F32),
        in_specs=[SMEM] + [VMEM] * (2 + len(received)),
        compiler_params=limit(8),
        out_specs=VMEM,
        scratch_shapes=[pltpu.VMEM((OVMAX + total + share, LANES), F32)],
        name="combine",
    )(margin_len, turned, rows, *received)
    return turned.transpose(0, 2, 1)


def solution(mesh):
    in_specs = (
        P("group", "seq", None),
        P(),
        P(),
        P(),
        P(None, None, "seq"),
        P("seq", None),
        P(),
        P(),
    )
    out_specs = P("group", "seq", None)

    return jax.shard_map(body, mesh=mesh, in_specs=in_specs, out_specs=out_specs, check_vma=False)
```

```python
import functools
import math

import jax
import jax.numpy as jnp
from jax import lax
from jax.experimental import pallas as pl
from jax.experimental.pallas import tpu as pltpu
from jax.sharding import PartitionSpec as P

HDIM = 64
OVMAX = 512
LANES = 128
QUAD = 4 * HDIM
STEP = -0.5
F32 = jnp.float32
BF16 = jnp.bfloat16
VMEM = pl.BlockSpec(memory_space=pltpu.VMEM)
SMEM = pl.BlockSpec(memory_space=pltpu.SMEM)


def limit(mebibytes):
    return pltpu.CompilerParams(vmem_limit_bytes=mebibytes << 20)


def iota(shape, dim):
    return lax.broadcasted_iota(jnp.int32, shape, dim)


def matmul(lhs, rhs):
    return jnp.dot(lhs, rhs, preferred_element_type=F32)


def matmul_nt(lhs, rhs, precision=None):
    return lax.dot_general(lhs, rhs, (((1,), (1,)), ((), ())), precision=precision, preferred_element_type=F32)


def split(value):
    high = value.astype(BF16)
    return high, (value - high.astype(F32)).astype(BF16)


def margin_at(margin_ref, index):
    last = margin_ref.shape[0]
    length = margin_ref[jnp.clip(index, 0, last - 1)]
    return jnp.where((index >= 0) & (index < last), length, 0)


def started(pairs, sem):
    copies = [pltpu.make_async_copy(source, target, sem.at[i]) for i, (source, target) in enumerate(pairs)]
    for copy in copies:
        copy.start()
    return copies


def folded(both, weights, channels):
    product = matmul(both, weights)
    return product[:channels] + product[channels:]


def halves(value):
    channels = value.shape[1]
    value = jnp.concatenate([value, value], axis=1)
    high, low = split(value)
    left = iota(value.shape, 1) < channels
    return jnp.where(left, high.astype(F32), low.astype(F32)).astype(BF16)


def centered_rows(in_ref):
    weight = in_ref[...].astype(F32)
    return weight - jnp.mean(weight, axis=-1, keepdims=True)


def fold_back_kernel(shares, in_hbm, gain_hbm, qkv_hbm, out_hbm, final_hbm, head_hbm, *refs):
    back_ref, part_ref, in_ref, gain_ref, value_ref, out_ref, final_ref, head_ref, sem = refs
    pairs = [(in_hbm, in_ref), (gain_hbm, gain_ref), (qkv_hbm.at[2], value_ref), (out_hbm, out_ref)]
    copies = started(pairs + [(final_hbm, final_ref), (head_hbm, head_ref)], sem)
    copies[0].wait()
    copies[1].wait()
    centered = centered_rows(in_ref)
    channels, depth = centered.shape
    width = out_ref.shape[0]
    both = jnp.concatenate(split(centered * gain_ref[...][None, :]), axis=0)
    copies[2].wait()
    values = folded(both, value_ref[...], channels)
    copies[3].wait()
    tiled = jnp.concatenate([values] * (width // HDIM), axis=0)
    same = iota((width, width), 0) // channels == iota((width, width), 1) // HDIM
    high, low = split(jnp.where(same, tiled, 0.0))
    back = matmul(high, out_ref[...]) + matmul(low, out_ref[...])
    back = back - jnp.mean(back, axis=-1, keepdims=True)
    back_ref[:, :depth] = back.astype(BF16)
    copies[4].wait()
    copies[5].wait()
    scores = matmul_nt(jnp.concatenate(split(back * final_ref[...][None, :]), axis=0), head_ref[...])
    back_ref[:, depth:] = halves(scores[:width] + scores[width:])
    rows = width // shares
    sub = lax.rem(lax.axis_index("group"), shares)
    part_ref[...] = back_ref[pl.ds(pl.multiple_of(sub * rows, rows), rows), :]


def fold_maps_kernel(in_hbm, gain_hbm, qkv_hbm, final_hbm, head_hbm, *refs):
    map_ref, direct_ref, gram_ref, in_ref, gain_ref, query_ref, key_ref, final_ref, head_ref, sem = refs
    pairs = [(in_hbm, in_ref), (gain_hbm, gain_ref), (qkv_hbm.at[0], query_ref), (qkv_hbm.at[1], key_ref)]
    copies = started(pairs + [(final_hbm, final_ref), (head_hbm, head_ref)], sem)
    copies[0].wait()
    copies[1].wait()
    centered = centered_rows(in_ref)
    channels, depth = centered.shape
    both = jnp.concatenate(split(centered * gain_ref[...][None, :]), axis=0)

    high, low = split(centered)
    direct_ref[:channels, :depth] = high
    direct_ref[channels:, :depth] = low
    gram = matmul_nt(jnp.concatenate([high, low], axis=0), jnp.concatenate([high, low], axis=0))
    gram = (gram[:channels] + gram[channels:]) * (1.0 / depth)
    gram = gram + pltpu.roll(gram, channels, 1)
    first, _ = split(gram)
    second, third = split(gram - first.astype(F32))
    left = iota((channels, LANES), 1) < channels
    gram_ref[:, :LANES] = jnp.where(left, first.astype(F32), second.astype(F32)).astype(BF16)
    gram_ref[:, LANES:] = jnp.where(left, third.astype(F32), 0.0).astype(BF16)

    copies[2].wait()
    queries = folded(both, query_ref[...], channels)
    copies[3].wait()
    keys = folded(both, key_ref[...], channels)
    map_ref[...] = jnp.concatenate([queries, keys], axis=0).T.astype(BF16)

    copies[4].wait()
    copies[5].wait()
    scores = matmul_nt(jnp.concatenate(split(centered * final_ref[...][None, :]), axis=0), head_ref[...])
    direct_ref[:channels, depth:] = halves(scores[:channels] + scores[channels:])
    direct_ref[channels:, depth:] = jnp.zeros((channels, LANES), BF16)


def twice(tokens):
    tokens = tokens.astype(F32)
    return tokens + pltpu.roll(tokens, LANES // 2, 1)


def bend(tokens, doubled, gram_ref):
    bent = matmul(tokens[:, : gram_ref.shape[0]], gram_ref[...])
    return (bent[:, :LANES] + bent[:, LANES:]) * doubled


def variance(bent):
    return jnp.maximum(jnp.sum(bent, axis=-1, keepdims=True), 0.0) + 1e-05


def quads(maps, mine, query_eps, key_eps, right_ref, ext_ref, sum_ref, key_scr, query_scr, p_scr):
    heads_width = maps.shape[0]
    total = right_ref.shape[0]
    share = mine.shape[0]
    channels = LANES // 2
    tile = min(total, 256)
    for start in range(0, total, tile):
        keys = matmul_nt(maps, right_ref[start : start + tile]).reshape(heads_width // HDIM, HDIM, tile)
        norm = jnp.mean(keys * keys, axis=1, keepdims=True)
        keys = keys * lax.rsqrt(norm + key_eps[None, :, start : start + tile])
        key_scr[:, start : start + tile] = keys.reshape(heads_width, tile).astype(BF16)
    one_head = iota((QUAD, QUAD), 0) // HDIM == iota((QUAD, QUAD), 1) // HDIM
    spread = jnp.where(one_head, 1.0 / HDIM, 0.0).astype(BF16)
    head_of = iota((share, QUAD), 1) // HDIM
    scale = HDIM ** (-0.5) * math.log2(math.e)
    left = iota((share, LANES), 1) < channels
    for quad in range(heads_width // QUAD):
        span = slice(quad * QUAD, (quad + 1) * QUAD)
        queries = matmul_nt(mine, maps[span, :])
        norm = matmul((queries * queries).astype(BF16), spread)
        queries = (queries * lax.rsqrt(norm + query_eps)).astype(BF16)
        for head in range(4):
            query_scr[quad % 2, head * share : (head + 1) * share, :] = jnp.where(
                head_of == head, queries, jnp.zeros_like(queries)
            )
        for start in range(0, total, tile):
            scores = matmul(query_scr[quad % 2], key_scr[span, start : start + tile])
            p_scr[quad % 2, :, start : start + tile] = jnp.exp2(scores * scale).astype(BF16)
        summed = matmul(p_scr[quad % 2], ext_ref[...])
        summed = summed[:, :LANES] / summed[:, LANES:]
        for pair in range(2):
            even = summed[2 * pair * share : (2 * pair + 1) * share]
            odd = summed[(2 * pair + 1) * share : (2 * pair + 2) * share]
            at = slice(quad * QUAD + pair * LANES, quad * QUAD + (pair + 1) * LANES)
            sum_ref[:share, at] = jnp.where(left, even, pltpu.roll(odd, HDIM, 1)).astype(BF16)
            sum_ref[share:, at] = jnp.where(left, pltpu.roll(even, HDIM, 1), odd).astype(BF16)


def attend_own_kernel(count, window, own_width, margin_ref, *refs):
    piece_refs, refs = refs[:count], refs[count:]
    map_ref, gram_ref, refs = refs[0], refs[1], refs[2:]
    if window:
        next_ref, refs = refs[0], refs[1:]
    sum_ref, right_ref, mine_ref, ext_ref, eps_ref, slot_scr, next_scr, win_scr, key_scr, query_scr, p_scr = refs
    total = win_scr.shape[0]
    channels = gram_ref.shape[0]
    share = total // count
    low = total - OVMAX
    group_pos = lax.axis_index("group")
    seq_pos = lax.axis_index("seq")
    over_len = margin_at(margin_ref, 2 * group_pos + window)
    own = total - over_len

    next_scr[:OVMAX, :] = jnp.zeros((OVMAX, LANES), F32)
    for k in range(count):
        source = jnp.bitwise_xor(seq_pos, k) * share
        at = pl.ds(pl.multiple_of(source, share), share)
        after = pl.ds(pl.multiple_of(source + OVMAX, share), share)
        slot = piece_refs[k][...].astype(F32)
        slot_scr[at, :] = pltpu.roll(slot, channels, 1) if window else slot
        next_scr[after, :] = next_ref[k].astype(F32) if window else pltpu.roll(slot, channels, 1)
    left = iota((OVMAX, LANES), 1) < channels
    for start in range(0, total, OVMAX):
        rows = slot_scr[start : start + OVMAX, :]
        if start >= low:
            tail = next_scr[pl.ds(over_len + (start - low), OVMAX), :]
            rows = jnp.where(iota(rows.shape, 0) + start < own, rows, tail)
        win_scr[start : start + OVMAX, :] = jnp.where(left, rows, 0.0).astype(BF16)

    win = win_scr[...]
    mine = win_scr[pl.ds(pl.multiple_of(seq_pos * share, share), share), :]
    mine_ref[...] = mine
    mine_twice = twice(mine)
    sum_ref[:share, own_width:] = mine_twice.astype(BF16)
    sum_ref[share:, own_width:] = mine_twice.astype(BF16)
    query_eps = variance(bend(mine, mine_twice, gram_ref)) * 1e-06
    doubled = twice(win)
    bent = bend(win, doubled, gram_ref)
    ones = jnp.ones((16, LANES), BF16)
    key_eps = (jnp.maximum(matmul_nt(ones, bent.astype(BF16))[:8], 0.0) + 1e-05) * 1e-06
    eps_ref[...] = key_eps

    scaled = doubled * lax.rsqrt(variance(bent))
    counted = (iota((total, LANES), 0) >= jnp.minimum(own, total - 1)).astype(F32)
    left = iota((total, LANES), 1) < channels
    ext_ref[:, :LANES] = jnp.where(left, scaled, scaled * counted).astype(BF16)
    ext_ref[:, LANES:] = jnp.where(left, 1.0, counted).astype(BF16)
    right_ref[...] = jnp.where(left, 0.0, doubled).astype(BF16)
    if own_width:
        quads(map_ref[...], mine, query_eps, key_eps[:1], right_ref, ext_ref, sum_ref, key_scr, query_scr, p_scr)


def attend_rest_kernel(gram_ref, right_ref, mine_ref, ext_ref, eps_ref, *refs):
    map_refs, refs = refs[:-5], refs[-5:]
    sum_ref, map_scr, key_scr, query_scr, p_scr = refs
    width = map_refs[0].shape[0]
    for k, ref in enumerate(map_refs):
        map_scr[k * width : (k + 1) * width, :] = ref[...]
    mine = mine_ref[...]
    query_eps = variance(bend(mine, twice(mine), gram_ref)) * 1e-06
    maps = map_scr[...]
    quads(maps, mine, query_eps, eps_ref[:1, :], right_ref, ext_ref, sum_ref, key_scr, query_scr, p_scr)


def finish_kernel(count, shares, high, margin_ref, *refs):
    first_ref, first_rest, second_ref, second_rest, direct_ref, back_ref, far_ref, near_ref = refs[:8]
    rows_ref, packed_first, packed_second, all_scr, square_scr = refs[8:]
    width = back_ref.shape[0]
    depth = back_ref.shape[1] - LANES
    share = first_ref.shape[0] // 2
    full = width * count
    total = share * count
    part = width // shares
    channels = direct_ref.shape[0] // 2
    group_pos = lax.axis_index("group")
    seq_pos = lax.axis_index("seq")
    sub = lax.rem(group_pos, shares)
    all_scr[:width, :] = back_ref[...]
    all_scr[full:, :] = direct_ref[...]
    for i, m in enumerate(high):
        for near, ref in ((0, far_ref), (1, near_ref)):
            place = jnp.bitwise_xor(sub, m ^ near) * part
            for k in range(1, count):
                all_scr[pl.ds(pl.multiple_of(place + k * width, part), part), :] = ref[i, k - 1]
    tile = 2 * LANES
    own = first_ref.shape[1] - LANES
    windows = ((first_ref, first_rest), (second_ref, second_rest))
    known = jnp.concatenate(
        [jnp.concatenate([ref[:, :own], rest[...], ref[:, own:]][not own :], axis=1) for ref, rest in windows], axis=0
    )
    for start in range(0, depth, tile):
        mixed = matmul(known, all_scr[:, start : start + tile])
        squares = mixed * mixed
        squares = squares[:, :LANES] + squares[:, LANES:]
        square_scr[...] = squares if start == 0 else square_scr[...] + squares
    score = matmul(known, all_scr[:, depth:])
    variance = jnp.sum(square_scr[...], axis=-1, keepdims=True) * (1.0 / depth)
    score = (score + pltpu.roll(score, channels, 1)) * lax.rsqrt(variance + 1e-05)
    position = iota((share, LANES), 0) + seq_pos * share
    left = iota((share // 2, LANES), 1) < channels
    for window, packed_ref in enumerate((packed_first, packed_second)):
        at = 2 * share * window
        own = total - margin_at(margin_ref, 2 * group_pos + window)
        margin = jnp.where(position >= own, score[at + share : at + 2 * share], 0.0)
        signed = score[at : at + share] - margin
        rows_ref[window] = signed
        packed_ref[...] = jnp.where(left, signed[: share // 2], signed[share // 2 :]).astype(BF16)


def combine_kernel(count, deltas, margin_ref, latent_ref, rows_ref, *refs):
    out_ref, tail_scr = refs[2 * len(deltas) :]
    channels, share = latent_ref.shape[1:]
    total = share * count
    group_pos = lax.axis_index("group")
    seq_pos = lax.axis_index("seq")
    for slot in range(2):
        before = margin_at(margin_ref, 2 * group_pos + slot - 1)
        own = total - margin_at(margin_ref, 2 * group_pos + slot)
        tail_scr[...] = jnp.zeros_like(tail_scr)
        for delta, ref in zip(deltas, refs[slot * len(deltas) : (slot + 1) * len(deltas)]):
            row = (seq_pos + delta) * share - (total - OVMAX)
            for half in range(2):
                value = ref[...].astype(F32)
                value = pltpu.roll(value, channels, 1) if half else value
                at = pl.ds(pl.multiple_of(row + half * (share // 2), share // 2), share // 2)
                tail_scr[at, :] = value
        moved = tail_scr[pl.ds(OVMAX - before + seq_pos * share, share), :]
        score = (rows_ref[slot] + moved).T[:channels]
        keep = iota(score.shape, 1) + seq_pos * share < own
        out_ref[slot] = jnp.where(keep, latent_ref[slot] + STEP * score, 0.0)


def body(latent, margin_len, in_weight, norm_gain, qkv_weight, out_weight, final_gain, head_out):
    count = lax.axis_size("seq")
    groups = lax.axis_size("group")
    share, channels = latent.shape[1:]
    total = share * count
    width, depth = out_weight.shape
    full = width * count
    shares = min(groups, width // 16)
    high = range(0, shares, 2)

    def across(value, group_by, pairs):
        moves = [
            (g * count + i, (g + group_by) * count + j)
            for g in range(groups)
            for i, j in pairs
            if 0 <= g + group_by < groups
        ]
        return lax.ppermute(value, ("group", "seq"), moves)

    def swap(value, bits):
        return lax.ppermute(value, "group", [(g, g ^ bits) for g in range(groups)])

    def gathered(value):
        return [lax.ppermute(value, "seq", [(i, i ^ k) for i in range(count)]) for k in range(1, count)]

    turned = latent.transpose(0, 2, 1)
    packed = jnp.concatenate([latent[0], latent[1]], axis=1).astype(BF16)
    pieces = [packed] + gathered(packed)
    stacked = jnp.stack(pieces)
    following = across(stacked, -1, [(i, i) for i in range(count)])
    hbm = pl.BlockSpec(memory_space=pltpu.HBM)
    small = (pltpu.VMEM(final_gain.shape, F32), pltpu.VMEM(head_out.shape[::-1], BF16), pltpu.SemaphoreType.DMA((6,)))
    fronts = (pltpu.VMEM(in_weight.shape, BF16), pltpu.VMEM(norm_gain.shape, F32))
    matrix = pltpu.VMEM(qkv_weight.shape[1:], BF16)
    back, part = pl.pallas_call(
        functools.partial(fold_back_kernel, shares),
        out_shape=(
            jax.ShapeDtypeStruct((width, depth + LANES), BF16),
            jax.ShapeDtypeStruct((width // shares, depth + LANES), BF16),
        ),
        in_specs=[hbm] * 6,
        compiler_params=limit(62),
        out_specs=(VMEM,) * 2,
        scratch_shapes=[*fronts, matrix, pltpu.VMEM(out_weight.shape, BF16), *small],
        cost_estimate=pl.CostEstimate(flops=width * depth * 1000, bytes_accessed=5 * width * depth, transcendentals=0),
        name="fold_back",
    )(in_weight, norm_gain, qkv_weight, out_weight, final_gain, head_out.T)
    own_part = jnp.stack(gathered(part))
    maps, direct, gram = pl.pallas_call(
        fold_maps_kernel,
        out_shape=(
            jax.ShapeDtypeStruct((width, LANES), BF16),
            jax.ShapeDtypeStruct((2 * channels, depth + LANES), BF16),
            jax.ShapeDtypeStruct((channels, 2 * LANES), BF16),
        ),
        in_specs=[hbm] * 5,
        compiler_params=limit(62),
        out_specs=(VMEM,) * 3,
        scratch_shapes=[*fronts, matrix, matrix, *small],
        cost_estimate=pl.CostEstimate(flops=width * depth * 600, bytes_accessed=5 * width * depth, transcendentals=0),
        name="fold_maps",
    )(in_weight, norm_gain, qkv_weight, final_gain, head_out.T)
    far_maps = gathered(maps)
    own_width = width // QUAD * QUAD
    rest_maps = far_maps if own_width else [maps] + far_maps
    rest_width = full - own_width

    def attention(lanes):
        return pl.CostEstimate(
            flops=16 * share * total * lanes,
            bytes_accessed=4 * lanes * share,
            transcendentals=share * total * lanes // HDIM,
        )

    def scratch(lanes):
        return [
            pltpu.VMEM((lanes, total), BF16),
            pltpu.VMEM((2, 4 * share, QUAD), BF16),
            pltpu.VMEM((2, 4 * share, total), BF16),
        ]

    def attend_own(window):
        extra = [following] if window else []
        return pl.pallas_call(
            functools.partial(attend_own_kernel, count, window, own_width),
            out_shape=(
                jax.ShapeDtypeStruct((2 * share, own_width + LANES), BF16),
                jax.ShapeDtypeStruct((total, LANES), BF16),
                jax.ShapeDtypeStruct((share, LANES), BF16),
                jax.ShapeDtypeStruct((total, QUAD), BF16),
                jax.ShapeDtypeStruct((8, total), F32),
            ),
            in_specs=[SMEM] + [VMEM] * (count + len(extra) + 2),
            compiler_params=limit(24),
            out_specs=(VMEM,) * 5,
            scratch_shapes=[
                pltpu.VMEM((total, LANES), F32),
                pltpu.VMEM((OVMAX + total, LANES), F32),
                pltpu.VMEM((total, LANES), BF16),
                *scratch(max(own_width, QUAD)),
            ],
            cost_estimate=attention(max(own_width, QUAD)),
            name="attend_own",
        )(margin_len, *pieces, maps, gram, *extra)

    def attend_rest(state):
        return pl.pallas_call(
            attend_rest_kernel,
            out_shape=jax.ShapeDtypeStruct((2 * share, rest_width), BF16),
            in_specs=[VMEM] * (5 + len(rest_maps)),
            compiler_params=limit(28),
            out_specs=VMEM,
            scratch_shapes=[pltpu.VMEM((rest_width, LANES), BF16), *scratch(rest_width)],
            cost_estimate=attention(rest_width),
            name="attend_rest",
        )(gram, *state, *rest_maps)

    first, *first_state = attend_own(0)
    second, *second_state = attend_own(1)
    first_rest = attend_rest(first_state)
    second_rest = attend_rest(second_state)
    planes = [swap(own_part, bits) for bits in high[1:]]
    far = jnp.stack([own_part] + planes)
    near = swap(far, 1)
    rows, *tails = pl.pallas_call(
        functools.partial(finish_kernel, count, shares, list(high)),
        out_shape=(
            jax.ShapeDtypeStruct((2, share, LANES), F32),
            jax.ShapeDtypeStruct((share // 2, LANES), BF16),
            jax.ShapeDtypeStruct((share // 2, LANES), BF16),
        ),
        in_specs=[SMEM] + [VMEM] * 8,
        compiler_params=limit(24),
        out_specs=(VMEM, VMEM, VMEM),
        scratch_shapes=[
            pltpu.VMEM((full + 2 * channels, depth + LANES), BF16),
            pltpu.VMEM((4 * share, LANES), F32),
        ],
        cost_estimate=pl.CostEstimate(
            flops=8 * share * full * depth, bytes_accessed=2 * full * depth, transcendentals=0
        ),
        name="finish",
    )(margin_len, first, first_rest, second, second_rest, direct, back, far, near)

    deltas = list(range((total - OVMAX) // share, count))
    received = []
    for window, group_by in ((1, 1), (0, 0)):
        received += [across(tails[window], group_by, [(i, i - d) for i in range(d, count)]) for d in deltas]
    turned = pl.pallas_call(
        functools.partial(combine_kernel, count, deltas),
        out_shape=jax.ShapeDtypeStruct(turned.shape, F32),
        in_specs=[SMEM] + [VMEM] * (2 + len(received)),
        compiler_params=limit(8),
        out_specs=VMEM,
        scratch_shapes=[pltpu.VMEM((OVMAX + total + share, LANES), F32)],
        name="combine",
    )(margin_len, turned, rows, *received)
    return turned.transpose(0, 2, 1)


def solution(mesh):
    in_specs = (
        P("group", "seq", None),
        P(),
        P(),
        P(),
        P(None, None, "seq"),
        P("seq", None),
        P(),
        P(),
    )
    out_specs = P("group", "seq", None)

    return jax.shard_map(body, mesh=mesh, in_specs=in_specs, out_specs=out_specs, check_vma=False)
```

```python
import functools
import math

import jax
import jax.numpy as jnp
from jax import lax
from jax.experimental import pallas as pl
from jax.experimental.pallas import tpu as pltpu
from jax.sharding import PartitionSpec as P

HDIM = 64
OVMAX = 512
LANES = 128
QUAD = 4 * HDIM
STEP = -0.5
F32 = jnp.float32
BF16 = jnp.bfloat16
VMEM = pl.BlockSpec(memory_space=pltpu.VMEM)
SMEM = pl.BlockSpec(memory_space=pltpu.SMEM)


def limit(mebibytes):
    return pltpu.CompilerParams(vmem_limit_bytes=mebibytes << 20)


def iota(shape, dim):
    return lax.broadcasted_iota(jnp.int32, shape, dim)


def matmul(lhs, rhs):
    return jnp.dot(lhs, rhs, preferred_element_type=F32)


def matmul_nt(lhs, rhs, precision=None):
    return lax.dot_general(lhs, rhs, (((1,), (1,)), ((), ())), precision=precision, preferred_element_type=F32)


def split(value):
    high = value.astype(BF16)
    return high, (value - high.astype(F32)).astype(BF16)


def margin_at(margin_ref, index):
    last = margin_ref.shape[0]
    length = margin_ref[jnp.clip(index, 0, last - 1)]
    return jnp.where((index >= 0) & (index < last), length, 0)


def started(pairs, sem):
    copies = [pltpu.make_async_copy(source, target, sem.at[i]) for i, (source, target) in enumerate(pairs)]
    for copy in copies:
        copy.start()
    return copies


def folded(both, weights, channels):
    product = matmul(both, weights)
    return product[:channels] + product[channels:]


def halves(value):
    channels = value.shape[1]
    value = jnp.concatenate([value, value], axis=1)
    high, low = split(value)
    left = iota(value.shape, 1) < channels
    return jnp.where(left, high.astype(F32), low.astype(F32)).astype(BF16)


def centered_rows(in_ref):
    weight = in_ref[...].astype(F32)
    return weight - jnp.mean(weight, axis=-1, keepdims=True)


def fold_kernel(shares, in_hbm, gain_hbm, qkv_hbm, out_hbm, final_hbm, head_hbm, *refs):
    map_ref, back_ref, part_ref, direct_ref, gram_ref = refs[:5]
    in_ref, gain_ref, qkv_ref, out_ref, final_ref, head_ref, sem = refs[5:]
    pairs = [(in_hbm, in_ref), (gain_hbm, gain_ref), (qkv_hbm.at[2], qkv_ref.at[2]), (out_hbm, out_ref)]
    pairs += [(qkv_hbm.at[0], qkv_ref.at[0]), (qkv_hbm.at[1], qkv_ref.at[1])]
    copies = started(pairs + [(final_hbm, final_ref), (head_hbm, head_ref)], sem)
    copies[0].wait()
    copies[1].wait()
    centered = centered_rows(in_ref)
    channels, depth = centered.shape
    width = out_ref.shape[0]
    both = jnp.concatenate(split(centered * gain_ref[...][None, :]), axis=0)

    high, low = split(centered)
    direct_ref[:channels, :depth] = high
    direct_ref[channels:, :depth] = low
    gram = matmul_nt(jnp.concatenate([high, low], axis=0), jnp.concatenate([high, low], axis=0))
    gram = (gram[:channels] + gram[channels:]) * (1.0 / depth)
    gram = gram + pltpu.roll(gram, channels, 1)
    first, _ = split(gram)
    second, third = split(gram - first.astype(F32))
    left = iota((channels, LANES), 1) < channels
    gram_ref[:, :LANES] = jnp.where(left, first.astype(F32), second.astype(F32)).astype(BF16)
    gram_ref[:, LANES:] = jnp.where(left, third.astype(F32), 0.0).astype(BF16)

    copies[2].wait()
    values = folded(both, qkv_ref[2], channels)
    tiled = jnp.concatenate([values] * (width // HDIM), axis=0)
    same = iota((width, width), 0) // channels == iota((width, width), 1) // HDIM
    high, low = split(jnp.where(same, tiled, 0.0))
    copies[3].wait()
    back = matmul(high, out_ref[...]) + matmul(low, out_ref[...])
    back = back - jnp.mean(back, axis=-1, keepdims=True)
    back_ref[:, :depth] = back.astype(BF16)
    copies[4].wait()
    queries = folded(both, qkv_ref[0], channels)
    copies[5].wait()
    keys = folded(both, qkv_ref[1], channels)
    map_ref[...] = jnp.concatenate([queries, keys], axis=0).T.astype(BF16)

    copies[6].wait()
    copies[7].wait()
    pieces = split(back * final_ref[...][None, :]) + split(centered * final_ref[...][None, :])
    scores = matmul_nt(jnp.concatenate(pieces, axis=0), head_ref[...])
    back_ref[:, depth:] = halves(scores[:width] + scores[width : 2 * width])
    direct_ref[:channels, depth:] = halves(scores[2 * width : 2 * width + channels] + scores[2 * width + channels :])
    direct_ref[channels:, depth:] = jnp.zeros((channels, LANES), BF16)
    rows = width // shares
    sub = lax.rem(lax.axis_index("group"), shares)
    part_ref[...] = back_ref[pl.ds(pl.multiple_of(sub * rows, rows), rows), :]


def twice(tokens):
    tokens = tokens.astype(F32)
    return tokens + pltpu.roll(tokens, LANES // 2, 1)


def bend(tokens, doubled, gram_ref):
    bent = matmul(tokens[:, : gram_ref.shape[0]], gram_ref[...])
    return (bent[:, :LANES] + bent[:, LANES:]) * doubled


def variance(bent):
    return jnp.maximum(jnp.sum(bent, axis=-1, keepdims=True), 0.0) + 1e-05


def quads(maps, mine, query_eps, key_eps, right_ref, ext_ref, sum_ref, key_scr, query_scr, p_scr):
    heads_width = maps.shape[0]
    total = right_ref.shape[0]
    share = mine.shape[0]
    channels = LANES // 2
    tile = min(total, 256)
    for start in range(0, total, tile):
        keys = matmul_nt(maps, right_ref[start : start + tile]).reshape(heads_width // HDIM, HDIM, tile)
        norm = jnp.mean(keys * keys, axis=1, keepdims=True)
        keys = keys * lax.rsqrt(norm + key_eps[None, :, start : start + tile])
        key_scr[:, start : start + tile] = keys.reshape(heads_width, tile).astype(BF16)
    one_head = iota((QUAD, QUAD), 0) // HDIM == iota((QUAD, QUAD), 1) // HDIM
    spread = jnp.where(one_head, 1.0 / HDIM, 0.0).astype(BF16)
    head_of = iota((share, QUAD), 1) // HDIM
    scale = HDIM ** (-0.5) * math.log2(math.e)
    left = iota((share, LANES), 1) < channels
    for quad in range(heads_width // QUAD):
        span = slice(quad * QUAD, (quad + 1) * QUAD)
        queries = matmul_nt(mine, maps[span, :])
        norm = matmul((queries * queries).astype(BF16), spread)
        queries = (queries * lax.rsqrt(norm + query_eps)).astype(BF16)
        for head in range(4):
            query_scr[quad % 2, head * share : (head + 1) * share, :] = jnp.where(
                head_of == head, queries, jnp.zeros_like(queries)
            )
        for start in range(0, total, tile):
            scores = matmul(query_scr[quad % 2], key_scr[span, start : start + tile])
            p_scr[quad % 2, :, start : start + tile] = jnp.exp2(scores * scale).astype(BF16)
        summed = matmul(p_scr[quad % 2], ext_ref[...])
        summed = summed[:, :LANES] / summed[:, LANES:]
        for pair in range(2):
            even = summed[2 * pair * share : (2 * pair + 1) * share]
            odd = summed[(2 * pair + 1) * share : (2 * pair + 2) * share]
            at = slice(quad * QUAD + pair * LANES, quad * QUAD + (pair + 1) * LANES)
            sum_ref[:share, at] = jnp.where(left, even, pltpu.roll(odd, HDIM, 1)).astype(BF16)
            sum_ref[share:, at] = jnp.where(left, pltpu.roll(even, HDIM, 1), odd).astype(BF16)


def attend_own_kernel(count, window, own_width, margin_ref, *refs):
    piece_refs, refs = refs[:count], refs[count:]
    map_ref, gram_ref, refs = refs[0], refs[1], refs[2:]
    if window:
        next_ref, refs = refs[0], refs[1:]
    sum_ref, right_ref, mine_ref, ext_ref, eps_ref, slot_scr, next_scr, win_scr, key_scr, query_scr, p_scr = refs
    total = win_scr.shape[0]
    channels = gram_ref.shape[0]
    share = total // count
    low = total - OVMAX
    group_pos = lax.axis_index("group")
    seq_pos = lax.axis_index("seq")
    over_len = margin_at(margin_ref, 2 * group_pos + window)
    own = total - over_len

    next_scr[:OVMAX, :] = jnp.zeros((OVMAX, LANES), F32)
    for k in range(count):
        source = jnp.bitwise_xor(seq_pos, k) * share
        at = pl.ds(pl.multiple_of(source, share), share)
        after = pl.ds(pl.multiple_of(source + OVMAX, share), share)
        slot = piece_refs[k][...].astype(F32)
        slot_scr[at, :] = pltpu.roll(slot, channels, 1) if window else slot
        next_scr[after, :] = next_ref[k].astype(F32) if window else pltpu.roll(slot, channels, 1)
    left = iota((OVMAX, LANES), 1) < channels
    for start in range(0, total, OVMAX):
        rows = slot_scr[start : start + OVMAX, :]
        if start >= low:
            tail = next_scr[pl.ds(over_len + (start - low), OVMAX), :]
            rows = jnp.where(iota(rows.shape, 0) + start < own, rows, tail)
        win_scr[start : start + OVMAX, :] = jnp.where(left, rows, 0.0).astype(BF16)

    win = win_scr[...]
    mine = win_scr[pl.ds(pl.multiple_of(seq_pos * share, share), share), :]
    mine_ref[...] = mine
    mine_twice = twice(mine)
    sum_ref[:share, own_width:] = mine_twice.astype(BF16)
    sum_ref[share:, own_width:] = mine_twice.astype(BF16)
    query_eps = variance(bend(mine, mine_twice, gram_ref)) * 1e-06
    doubled = twice(win)
    bent = bend(win, doubled, gram_ref)
    ones = jnp.ones((16, LANES), BF16)
    key_eps = (jnp.maximum(matmul_nt(ones, bent.astype(BF16))[:8], 0.0) + 1e-05) * 1e-06
    eps_ref[...] = key_eps

    scaled = doubled * lax.rsqrt(variance(bent))
    counted = (iota((total, LANES), 0) >= jnp.minimum(own, total - 1)).astype(F32)
    left = iota((total, LANES), 1) < channels
    ext_ref[:, :LANES] = jnp.where(left, scaled, scaled * counted).astype(BF16)
    ext_ref[:, LANES:] = jnp.where(left, 1.0, counted).astype(BF16)
    right_ref[...] = jnp.where(left, 0.0, doubled).astype(BF16)
    if own_width:
        quads(map_ref[...], mine, query_eps, key_eps[:1], right_ref, ext_ref, sum_ref, key_scr, query_scr, p_scr)


def attend_rest_kernel(gram_ref, right_ref, mine_ref, ext_ref, eps_ref, *refs):
    map_refs, refs = refs[:-5], refs[-5:]
    sum_ref, map_scr, key_scr, query_scr, p_scr = refs
    width = map_refs[0].shape[0]
    for k, ref in enumerate(map_refs):
        map_scr[k * width : (k + 1) * width, :] = ref[...]
    mine = mine_ref[...]
    query_eps = variance(bend(mine, twice(mine), gram_ref)) * 1e-06
    maps = map_scr[...]
    quads(maps, mine, query_eps, eps_ref[:1, :], right_ref, ext_ref, sum_ref, key_scr, query_scr, p_scr)


def finish_kernel(count, shares, high, margin_ref, *refs):
    first_ref, first_rest, second_ref, second_rest, direct_ref, back_ref, far_ref, near_ref = refs[:8]
    rows_ref, packed_first, packed_second, all_scr, square_scr = refs[8:]
    width = back_ref.shape[0]
    depth = back_ref.shape[1] - LANES
    share = first_ref.shape[0] // 2
    full = width * count
    total = share * count
    part = width // shares
    channels = direct_ref.shape[0] // 2
    group_pos = lax.axis_index("group")
    seq_pos = lax.axis_index("seq")
    sub = lax.rem(group_pos, shares)
    all_scr[:width, :] = back_ref[...]
    all_scr[full:, :] = direct_ref[...]
    for i, m in enumerate(high):
        for near, ref in ((0, far_ref), (1, near_ref)):
            place = jnp.bitwise_xor(sub, m ^ near) * part
            for k in range(1, count):
                all_scr[pl.ds(pl.multiple_of(place + k * width, part), part), :] = ref[i, k - 1]
    tile = 2 * LANES
    own = first_ref.shape[1] - LANES
    windows = ((first_ref, first_rest), (second_ref, second_rest))
    known = jnp.concatenate(
        [jnp.concatenate([ref[:, :own], rest[...], ref[:, own:]][not own :], axis=1) for ref, rest in windows], axis=0
    )
    for start in range(0, depth, tile):
        mixed = matmul(known, all_scr[:, start : start + tile])
        squares = mixed * mixed
        squares = squares[:, :LANES] + squares[:, LANES:]
        square_scr[...] = squares if start == 0 else square_scr[...] + squares
    score = matmul(known, all_scr[:, depth:])
    variance = jnp.sum(square_scr[...], axis=-1, keepdims=True) * (1.0 / depth)
    score = (score + pltpu.roll(score, channels, 1)) * lax.rsqrt(variance + 1e-05)
    position = iota((share, LANES), 0) + seq_pos * share
    left = iota((share // 2, LANES), 1) < channels
    for window, packed_ref in enumerate((packed_first, packed_second)):
        at = 2 * share * window
        own = total - margin_at(margin_ref, 2 * group_pos + window)
        margin = jnp.where(position >= own, score[at + share : at + 2 * share], 0.0)
        signed = score[at : at + share] - margin
        rows_ref[window] = signed
        packed_ref[...] = jnp.where(left, signed[: share // 2], signed[share // 2 :]).astype(BF16)


def combine_kernel(count, deltas, margin_ref, latent_ref, rows_ref, *refs):
    out_ref, tail_scr = refs[2 * len(deltas) :]
    channels, share = latent_ref.shape[1:]
    total = share * count
    group_pos = lax.axis_index("group")
    seq_pos = lax.axis_index("seq")
    for slot in range(2):
        before = margin_at(margin_ref, 2 * group_pos + slot - 1)
        own = total - margin_at(margin_ref, 2 * group_pos + slot)
        tail_scr[...] = jnp.zeros_like(tail_scr)
        for delta, ref in zip(deltas, refs[slot * len(deltas) : (slot + 1) * len(deltas)]):
            row = (seq_pos + delta) * share - (total - OVMAX)
            for half in range(2):
                value = ref[...].astype(F32)
                value = pltpu.roll(value, channels, 1) if half else value
                at = pl.ds(pl.multiple_of(row + half * (share // 2), share // 2), share // 2)
                tail_scr[at, :] = value
        moved = tail_scr[pl.ds(OVMAX - before + seq_pos * share, share), :]
        score = (rows_ref[slot] + moved).T[:channels]
        keep = iota(score.shape, 1) + seq_pos * share < own
        out_ref[slot] = jnp.where(keep, latent_ref[slot] + STEP * score, 0.0)


def body(latent, margin_len, in_weight, norm_gain, qkv_weight, out_weight, final_gain, head_out):
    count = lax.axis_size("seq")
    groups = lax.axis_size("group")
    share, channels = latent.shape[1:]
    total = share * count
    width, depth = out_weight.shape
    full = width * count
    shares = min(groups, width // 16)
    high = range(0, shares, 2)

    def across(value, group_by, pairs):
        moves = [
            (g * count + i, (g + group_by) * count + j)
            for g in range(groups)
            for i, j in pairs
            if 0 <= g + group_by < groups
        ]
        return lax.ppermute(value, ("group", "seq"), moves)

    def swap(value, bits):
        return lax.ppermute(value, "group", [(g, g ^ bits) for g in range(groups)])

    def gathered(value):
        return [lax.ppermute(value, "seq", [(i, i ^ k) for i in range(count)]) for k in range(1, count)]

    turned = latent.transpose(0, 2, 1)
    packed = jnp.concatenate([latent[0], latent[1]], axis=1).astype(BF16)
    pieces = [packed] + gathered(packed)
    stacked = jnp.stack(pieces)
    following = across(stacked, -1, [(i, i) for i in range(count)])
    maps, back, part, direct, gram = pl.pallas_call(
        functools.partial(fold_kernel, shares),
        out_shape=(
            jax.ShapeDtypeStruct((width, LANES), BF16),
            jax.ShapeDtypeStruct((width, depth + LANES), BF16),
            jax.ShapeDtypeStruct((width // shares, depth + LANES), BF16),
            jax.ShapeDtypeStruct((2 * channels, depth + LANES), BF16),
            jax.ShapeDtypeStruct((channels, 2 * LANES), BF16),
        ),
        in_specs=[pl.BlockSpec(memory_space=pltpu.HBM)] * 6,
        compiler_params=limit(62),
        out_specs=(VMEM,) * 5,
        scratch_shapes=[
            pltpu.VMEM(in_weight.shape, BF16),
            pltpu.VMEM(norm_gain.shape, F32),
            pltpu.VMEM(qkv_weight.shape, BF16),
            pltpu.VMEM(out_weight.shape, BF16),
            pltpu.VMEM(final_gain.shape, F32),
            pltpu.VMEM(head_out.shape[::-1], BF16),
            pltpu.SemaphoreType.DMA((8,)),
        ],
        cost_estimate=pl.CostEstimate(flops=width * depth * 1200, bytes_accessed=8 * width * depth, transcendentals=0),
        name="fold",
    )(in_weight, norm_gain, qkv_weight, out_weight, final_gain, head_out.T)
    own_part = jnp.stack(gathered(part))
    far_maps = gathered(maps)
    own_width = width // QUAD * QUAD
    rest_maps = far_maps if own_width else [maps] + far_maps
    rest_width = full - own_width

    def attention(lanes):
        return pl.CostEstimate(
            flops=16 * share * total * lanes,
            bytes_accessed=4 * lanes * share,
            transcendentals=share * total * lanes // HDIM,
        )

    def scratch(lanes):
        return [
            pltpu.VMEM((lanes, total), BF16),
            pltpu.VMEM((2, 4 * share, QUAD), BF16),
            pltpu.VMEM((2, 4 * share, total), BF16),
        ]

    def attend_own(window):
        extra = [following] if window else []
        return pl.pallas_call(
            functools.partial(attend_own_kernel, count, window, own_width),
            out_shape=(
                jax.ShapeDtypeStruct((2 * share, own_width + LANES), BF16),
                jax.ShapeDtypeStruct((total, LANES), BF16),
                jax.ShapeDtypeStruct((share, LANES), BF16),
                jax.ShapeDtypeStruct((total, QUAD), BF16),
                jax.ShapeDtypeStruct((8, total), F32),
            ),
            in_specs=[SMEM] + [VMEM] * (count + len(extra) + 2),
            compiler_params=limit(24),
            out_specs=(VMEM,) * 5,
            scratch_shapes=[
                pltpu.VMEM((total, LANES), F32),
                pltpu.VMEM((OVMAX + total, LANES), F32),
                pltpu.VMEM((total, LANES), BF16),
                *scratch(max(own_width, QUAD)),
            ],
            cost_estimate=attention(max(own_width, QUAD)),
            name="attend_own",
        )(margin_len, *pieces, maps, gram, *extra)

    def attend_rest(state):
        return pl.pallas_call(
            attend_rest_kernel,
            out_shape=jax.ShapeDtypeStruct((2 * share, rest_width), BF16),
            in_specs=[VMEM] * (5 + len(rest_maps)),
            compiler_params=limit(28),
            out_specs=VMEM,
            scratch_shapes=[pltpu.VMEM((rest_width, LANES), BF16), *scratch(rest_width)],
            cost_estimate=attention(rest_width),
            name="attend_rest",
        )(gram, *state, *rest_maps)

    first, *first_state = attend_own(0)
    second, *second_state = attend_own(1)
    first_rest = attend_rest(first_state)
    second_rest = attend_rest(second_state)
    planes = [swap(own_part, bits) for bits in high[1:]]
    far = jnp.stack([own_part] + planes)
    near = swap(far, 1)
    rows, *tails = pl.pallas_call(
        functools.partial(finish_kernel, count, shares, list(high)),
        out_shape=(
            jax.ShapeDtypeStruct((2, share, LANES), F32),
            jax.ShapeDtypeStruct((share // 2, LANES), BF16),
            jax.ShapeDtypeStruct((share // 2, LANES), BF16),
        ),
        in_specs=[SMEM] + [VMEM] * 8,
        compiler_params=limit(24),
        out_specs=(VMEM, VMEM, VMEM),
        scratch_shapes=[
            pltpu.VMEM((full + 2 * channels, depth + LANES), BF16),
            pltpu.VMEM((4 * share, LANES), F32),
        ],
        cost_estimate=pl.CostEstimate(
            flops=8 * share * full * depth, bytes_accessed=2 * full * depth, transcendentals=0
        ),
        name="finish",
    )(margin_len, first, first_rest, second, second_rest, direct, back, far, near)

    deltas = list(range((total - OVMAX) // share, count))
    received = []
    for window, group_by in ((1, 1), (0, 0)):
        received += [across(tails[window], group_by, [(i, i - d) for i in range(d, count)]) for d in deltas]
    turned = pl.pallas_call(
        functools.partial(combine_kernel, count, deltas),
        out_shape=jax.ShapeDtypeStruct(turned.shape, F32),
        in_specs=[SMEM] + [VMEM] * (2 + len(received)),
        compiler_params=limit(8),
        out_specs=VMEM,
        scratch_shapes=[pltpu.VMEM((OVMAX + total + share, LANES), F32)],
        name="combine",
    )(margin_len, turned, rows, *received)
    return turned.transpose(0, 2, 1)


def solution(mesh):
    in_specs = (
        P("group", "seq", None),
        P(),
        P(),
        P(),
        P(None, None, "seq"),
        P("seq", None),
        P(),
        P(),
    )
    out_specs = P("group", "seq", None)

    return jax.shard_map(body, mesh=mesh, in_specs=in_specs, out_specs=out_specs, check_vma=False)
```

```python
import functools
import math

import jax
import jax.numpy as jnp
from jax import lax
from jax.experimental import pallas as pl
from jax.experimental.pallas import tpu as pltpu
from jax.sharding import PartitionSpec as P

HDIM = 64
OVMAX = 512
LANES = 128
QUAD = 4 * HDIM
STEP = -0.5
F32 = jnp.float32
BF16 = jnp.bfloat16
VMEM = pl.BlockSpec(memory_space=pltpu.VMEM)
SMEM = pl.BlockSpec(memory_space=pltpu.SMEM)


def limit(mebibytes):
    return pltpu.CompilerParams(vmem_limit_bytes=mebibytes << 20)


def iota(shape, dim):
    return lax.broadcasted_iota(jnp.int32, shape, dim)


def matmul(lhs, rhs):
    return jnp.dot(lhs, rhs, preferred_element_type=F32)


def matmul_nt(lhs, rhs, precision=None):
    return lax.dot_general(lhs, rhs, (((1,), (1,)), ((), ())), precision=precision, preferred_element_type=F32)


def split(value):
    high = value.astype(BF16)
    return high, (value - high.astype(F32)).astype(BF16)


def margin_at(margin_ref, index):
    last = margin_ref.shape[0]
    length = margin_ref[jnp.clip(index, 0, last - 1)]
    return jnp.where((index >= 0) & (index < last), length, 0)


def block_of(sub, shares):
    return lax.rem(sub, 2) * (shares // 2) + sub // 2


def started(pairs, sem):
    copies = [pltpu.make_async_copy(source, target, sem.at[i]) for i, (source, target) in enumerate(pairs)]
    for copy in copies:
        copy.start()
    return copies


def folded(both, weights, channels):
    product = matmul(both, weights)
    return product[:channels] + product[channels:]


def halves(value):
    channels = value.shape[1]
    value = jnp.concatenate([value, value], axis=1)
    high, low = split(value)
    left = iota(value.shape, 1) < channels
    return jnp.where(left, high.astype(F32), low.astype(F32)).astype(BF16)


def centered_rows(in_ref):
    weight = in_ref[...].astype(F32)
    return weight - jnp.mean(weight, axis=-1, keepdims=True)


def fold_kernel(shares, in_hbm, gain_hbm, qkv_hbm, out_hbm, final_hbm, head_hbm, *refs):
    map_ref, back_ref, part_ref, direct_ref, gram_ref = refs[:5]
    in_ref, gain_ref, qkv_ref, out_ref, final_ref, head_ref, sem = refs[5:]
    pairs = [(in_hbm, in_ref), (gain_hbm, gain_ref), (qkv_hbm.at[2], qkv_ref.at[2]), (out_hbm, out_ref)]
    pairs += [(qkv_hbm.at[0], qkv_ref.at[0]), (qkv_hbm.at[1], qkv_ref.at[1])]
    copies = started(pairs + [(final_hbm, final_ref), (head_hbm, head_ref)], sem)
    copies[0].wait()
    copies[1].wait()
    centered = centered_rows(in_ref)
    channels, depth = centered.shape
    width = out_ref.shape[0]
    both = jnp.concatenate(split(centered * gain_ref[...][None, :]), axis=0)

    high, low = split(centered)
    direct_ref[:channels, :depth] = high
    direct_ref[channels:, :depth] = low
    gram = matmul_nt(jnp.concatenate([high, low], axis=0), jnp.concatenate([high, low], axis=0))
    gram = (gram[:channels] + gram[channels:]) * (1.0 / depth)
    gram = gram + pltpu.roll(gram, channels, 1)
    first, _ = split(gram)
    second, third = split(gram - first.astype(F32))
    left = iota((channels, LANES), 1) < channels
    gram_ref[:, :LANES] = jnp.where(left, first.astype(F32), second.astype(F32)).astype(BF16)
    gram_ref[:, LANES:] = jnp.where(left, third.astype(F32), 0.0).astype(BF16)

    copies[2].wait()
    values = folded(both, qkv_ref[2], channels)
    tiled = jnp.concatenate([values] * (width // HDIM), axis=0)
    same = iota((width, width), 0) // channels == iota((width, width), 1) // HDIM
    high, low = split(jnp.where(same, tiled, 0.0))
    copies[3].wait()
    back = matmul(high, out_ref[...]) + matmul(low, out_ref[...])
    back = back - jnp.mean(back, axis=-1, keepdims=True)
    back_ref[:, :depth] = back.astype(BF16)
    copies[4].wait()
    queries = folded(both, qkv_ref[0], channels)
    copies[5].wait()
    keys = folded(both, qkv_ref[1], channels)
    map_ref[...] = jnp.concatenate([queries, keys], axis=0).T.astype(BF16)

    copies[6].wait()
    copies[7].wait()
    pieces = split(back * final_ref[...][None, :]) + split(centered * final_ref[...][None, :])
    scores = matmul_nt(jnp.concatenate(pieces, axis=0), head_ref[...])
    back_ref[:, depth:] = halves(scores[:width] + scores[width : 2 * width])
    direct_ref[:channels, depth:] = halves(scores[2 * width : 2 * width + channels] + scores[2 * width + channels :])
    direct_ref[channels:, depth:] = jnp.zeros((channels, LANES), BF16)
    rows = width // shares
    sub = lax.rem(lax.axis_index("group"), shares)
    part_ref[...] = back_ref[pl.ds(pl.multiple_of(block_of(sub, shares) * rows, rows), rows), :]


def twice(tokens):
    tokens = tokens.astype(F32)
    return tokens + pltpu.roll(tokens, LANES // 2, 1)


def bend(tokens, doubled, gram_ref):
    bent = matmul(tokens[:, : gram_ref.shape[0]], gram_ref[...])
    return (bent[:, :LANES] + bent[:, LANES:]) * doubled


def variance(bent):
    return jnp.maximum(jnp.sum(bent, axis=-1, keepdims=True), 0.0) + 1e-05


def quads(maps, mine, query_eps, key_eps, right_ref, ext_ref, sum_ref, key_scr, query_scr, p_scr):
    heads_width = maps.shape[0]
    total = right_ref.shape[0]
    share = mine.shape[0]
    channels = LANES // 2
    tile = min(total, 256)
    for start in range(0, total, tile):
        keys = matmul_nt(maps, right_ref[start : start + tile]).reshape(heads_width // HDIM, HDIM, tile)
        norm = jnp.mean(keys * keys, axis=1, keepdims=True)
        keys = keys * lax.rsqrt(norm + key_eps[None, :, start : start + tile])
        key_scr[:, start : start + tile] = keys.reshape(heads_width, tile).astype(BF16)
    one_head = iota((QUAD, QUAD), 0) // HDIM == iota((QUAD, QUAD), 1) // HDIM
    spread = jnp.where(one_head, 1.0 / HDIM, 0.0).astype(BF16)
    head_of = iota((share, QUAD), 1) // HDIM
    scale = HDIM ** (-0.5) * math.log2(math.e)
    left = iota((share, LANES), 1) < channels
    for quad in range(heads_width // QUAD):
        span = slice(quad * QUAD, (quad + 1) * QUAD)
        queries = matmul_nt(mine, maps[span, :])
        norm = matmul((queries * queries).astype(BF16), spread)
        queries = (queries * lax.rsqrt(norm + query_eps)).astype(BF16)
        for head in range(4):
            query_scr[quad % 2, head * share : (head + 1) * share, :] = jnp.where(
                head_of == head, queries, jnp.zeros_like(queries)
            )
        for start in range(0, total, tile):
            scores = matmul(query_scr[quad % 2], key_scr[span, start : start + tile])
            p_scr[quad % 2, :, start : start + tile] = jnp.exp2(scores * scale).astype(BF16)
        summed = matmul(p_scr[quad % 2], ext_ref[...])
        summed = summed[:, :LANES] / summed[:, LANES:]
        for pair in range(2):
            even = summed[2 * pair * share : (2 * pair + 1) * share]
            odd = summed[(2 * pair + 1) * share : (2 * pair + 2) * share]
            at = slice(quad * QUAD + pair * LANES, quad * QUAD + (pair + 1) * LANES)
            sum_ref[:share, at] = jnp.where(left, even, pltpu.roll(odd, HDIM, 1)).astype(BF16)
            sum_ref[share:, at] = jnp.where(left, pltpu.roll(even, HDIM, 1), odd).astype(BF16)


def attend_own_kernel(count, window, own_width, margin_ref, *refs):
    piece_refs, refs = refs[:count], refs[count:]
    map_ref, gram_ref, refs = refs[0], refs[1], refs[2:]
    if window:
        next_ref, refs = refs[0], refs[1:]
    sum_ref, right_ref, mine_ref, ext_ref, eps_ref, slot_scr, next_scr, win_scr, key_scr, query_scr, p_scr = refs
    total = win_scr.shape[0]
    channels = gram_ref.shape[0]
    share = total // count
    low = total - OVMAX
    group_pos = lax.axis_index("group")
    seq_pos = lax.axis_index("seq")
    over_len = margin_at(margin_ref, 2 * group_pos + window)
    own = total - over_len

    next_scr[:OVMAX, :] = jnp.zeros((OVMAX, LANES), F32)
    for k in range(count):
        source = jnp.bitwise_xor(seq_pos, k) * share
        at = pl.ds(pl.multiple_of(source, share), share)
        after = pl.ds(pl.multiple_of(source + OVMAX, share), share)
        slot = piece_refs[k][...].astype(F32)
        slot_scr[at, :] = pltpu.roll(slot, channels, 1) if window else slot
        next_scr[after, :] = next_ref[k].astype(F32) if window else pltpu.roll(slot, channels, 1)
    left = iota((OVMAX, LANES), 1) < channels
    for start in range(0, total, OVMAX):
        rows = slot_scr[start : start + OVMAX, :]
        if start >= low:
            tail = next_scr[pl.ds(over_len + (start - low), OVMAX), :]
            rows = jnp.where(iota(rows.shape, 0) + start < own, rows, tail)
        win_scr[start : start + OVMAX, :] = jnp.where(left, rows, 0.0).astype(BF16)

    win = win_scr[...]
    mine = win_scr[pl.ds(pl.multiple_of(seq_pos * share, share), share), :]
    mine_ref[...] = mine
    mine_twice = twice(mine)
    sum_ref[:share, own_width:] = mine_twice.astype(BF16)
    sum_ref[share:, own_width:] = mine_twice.astype(BF16)
    query_eps = variance(bend(mine, mine_twice, gram_ref)) * 1e-06
    doubled = twice(win)
    bent = bend(win, doubled, gram_ref)
    ones = jnp.ones((16, LANES), BF16)
    key_eps = (jnp.maximum(matmul_nt(ones, bent.astype(BF16))[:8], 0.0) + 1e-05) * 1e-06
    eps_ref[...] = key_eps

    scaled = doubled * lax.rsqrt(variance(bent))
    counted = (iota((total, LANES), 0) >= jnp.minimum(own, total - 1)).astype(F32)
    left = iota((total, LANES), 1) < channels
    ext_ref[:, :LANES] = jnp.where(left, scaled, scaled * counted).astype(BF16)
    ext_ref[:, LANES:] = jnp.where(left, 1.0, counted).astype(BF16)
    right_ref[...] = jnp.where(left, 0.0, doubled).astype(BF16)
    if own_width:
        quads(map_ref[...], mine, query_eps, key_eps[:1], right_ref, ext_ref, sum_ref, key_scr, query_scr, p_scr)


def attend_rest_kernel(gram_ref, right_ref, mine_ref, ext_ref, eps_ref, *refs):
    map_refs, refs = refs[:-5], refs[-5:]
    sum_ref, map_scr, key_scr, query_scr, p_scr = refs
    width = map_refs[0].shape[0]
    for k, ref in enumerate(map_refs):
        map_scr[k * width : (k + 1) * width, :] = ref[...]
    mine = mine_ref[...]
    query_eps = variance(bend(mine, twice(mine), gram_ref)) * 1e-06
    maps = map_scr[...]
    quads(maps, mine, query_eps, eps_ref[:1, :], right_ref, ext_ref, sum_ref, key_scr, query_scr, p_scr)


def signed_rows(count, score, margin_ref, rows_ref, packed_first, packed_second):
    share = rows_ref.shape[1]
    total = share * count
    channels = LANES // 2
    group_pos = lax.axis_index("group")
    seq_pos = lax.axis_index("seq")
    position = iota((share, LANES), 0) + seq_pos * share
    left = iota((share // 2, LANES), 1) < channels
    for window, packed_ref in enumerate((packed_first, packed_second)):
        at = 2 * share * window
        own = total - margin_at(margin_ref, 2 * group_pos + window)
        margin = jnp.where(position >= own, score[at + share : at + 2 * share], 0.0)
        signed = score[at : at + share] - margin
        rows_ref[window] = signed
        packed_ref[...] = jnp.where(left, signed[: share // 2], signed[share // 2 :]).astype(BF16)


def finish_kernel(count, shares, high, margin_ref, *refs):
    first_ref, first_rest, second_ref, second_rest, direct_ref, back_ref, far_ref, near_ref = refs[:8]
    rows_ref, packed_first, packed_second, all_scr, square_scr = refs[8:]
    width = back_ref.shape[0]
    depth = back_ref.shape[1] - LANES
    full = width * count
    part = width // shares
    channels = direct_ref.shape[0] // 2
    group_pos = lax.axis_index("group")
    sub = lax.rem(group_pos, shares)
    all_scr[:width, :] = back_ref[...]
    all_scr[full:, :] = direct_ref[...]
    for i, m in enumerate(high):
        for near, ref in ((0, far_ref), (1, near_ref)):
            place = block_of(jnp.bitwise_xor(sub, m ^ near), shares) * part
            for k in range(1, count):
                all_scr[pl.ds(pl.multiple_of(place + k * width, part), part), :] = ref[i, k - 1]
    tile = 2 * LANES
    own = first_ref.shape[1] - LANES
    windows = ((first_ref, first_rest), (second_ref, second_rest))
    known = jnp.concatenate(
        [jnp.concatenate([ref[:, :own], rest[...], ref[:, own:]][not own :], axis=1) for ref, rest in windows], axis=0
    )
    for start in range(0, depth, tile):
        mixed = matmul(known, all_scr[:, start : start + tile])
        squares = mixed * mixed
        squares = squares[:, :LANES] + squares[:, LANES:]
        square_scr[...] = squares if start == 0 else square_scr[...] + squares
    score = matmul(known, all_scr[:, depth:])
    variance = jnp.sum(square_scr[...], axis=-1, keepdims=True) * (1.0 / depth)
    score = (score + pltpu.roll(score, channels, 1)) * lax.rsqrt(variance + 1e-05)
    signed_rows(count, score, margin_ref, rows_ref, packed_first, packed_second)


def half_known(rest_ref, count, core):
    width = rest_ref.shape[1] // (count - 1)
    half = width // 2
    starts = [pl.multiple_of(k * width + core * half, half) for k in range(count - 1)]
    return [rest_ref[:, pl.ds(start, half)] for start in starts]


def fill_half(all_scr, base, gathered_ref, sub, high, half, count):
    part = gathered_ref.shape[2]
    for i, m in enumerate(high):
        place = jnp.bitwise_xor(sub, m) // 2 * part
        for k in range(count - 1):
            all_scr[pl.ds(pl.multiple_of(base + k * half + place, part), part), :] = gathered_ref[i, k]


def finish_far_kernel(count, shares, high, *refs):
    first_ref, first_rest, second_ref, second_rest, direct_ref, back_ref, far_ref, sum_ref, all_scr = refs
    width = back_ref.shape[0]
    half = width // 2
    sub = lax.rem(lax.axis_index("group"), shares)
    core = lax.rem(sub, 2)
    all_scr[:width, :] = back_ref[...]
    fill_half(all_scr, width, far_ref, sub, high, half, count)
    all_scr[width + (count - 1) * half :, :] = direct_ref[...]
    windows = ((first_ref, first_rest), (second_ref, second_rest))
    known = jnp.concatenate(
        [
            jnp.concatenate([ref[:, :width], *half_known(rest, count, core), ref[:, width:]], axis=1)
            for ref, rest in windows
        ],
        axis=0,
    )
    columns = sum_ref.shape[1]
    for start in range(0, columns, 2 * LANES):
        at = slice(start, min(start + 2 * LANES, columns))
        sum_ref[:, at] = matmul(known, all_scr[:, at])


def finish_near_kernel(count, shares, high, margin_ref, *refs):
    first_rest, second_rest, near_ref, sum_ref, rows_ref, packed_first, packed_second, all_scr, square_scr = refs
    depth = sum_ref.shape[1] - LANES
    half = first_rest.shape[1] // (count - 1) // 2
    sub = jnp.bitwise_xor(lax.rem(lax.axis_index("group"), shares), 1)
    fill_half(all_scr, 0, near_ref, sub, high, half, count)
    core = lax.rem(sub, 2)
    known = jnp.concatenate(
        [jnp.concatenate(half_known(rest, count, core), axis=1) for rest in (first_rest, second_rest)], axis=0
    )
    for start in range(0, depth, 2 * LANES):
        at = slice(start, start + 2 * LANES)
        mixed = sum_ref[:, at] + matmul(known, all_scr[:, at])
        squares = mixed * mixed
        squares = squares[:, :LANES] + squares[:, LANES:]
        square_scr[...] = squares if start == 0 else square_scr[...] + squares
    score = sum_ref[:, depth:] + matmul(known, all_scr[:, depth:])
    variance_out = jnp.sum(square_scr[...], axis=-1, keepdims=True) * (1.0 / depth)
    score = (score + pltpu.roll(score, LANES // 2, 1)) * lax.rsqrt(variance_out + 1e-05)
    signed_rows(count, score, margin_ref, rows_ref, packed_first, packed_second)


def combine_kernel(count, deltas, margin_ref, latent_ref, rows_ref, *refs):
    out_ref, tail_scr = refs[2 * len(deltas) :]
    channels, share = latent_ref.shape[1:]
    total = share * count
    group_pos = lax.axis_index("group")
    seq_pos = lax.axis_index("seq")
    for slot in range(2):
        before = margin_at(margin_ref, 2 * group_pos + slot - 1)
        own = total - margin_at(margin_ref, 2 * group_pos + slot)
        tail_scr[...] = jnp.zeros_like(tail_scr)
        for delta, ref in zip(deltas, refs[slot * len(deltas) : (slot + 1) * len(deltas)]):
            row = (seq_pos + delta) * share - (total - OVMAX)
            for half in range(2):
                value = ref[...].astype(F32)
                value = pltpu.roll(value, channels, 1) if half else value
                at = pl.ds(pl.multiple_of(row + half * (share // 2), share // 2), share // 2)
                tail_scr[at, :] = value
        moved = tail_scr[pl.ds(OVMAX - before + seq_pos * share, share), :]
        score = (rows_ref[slot] + moved).T[:channels]
        keep = iota(score.shape, 1) + seq_pos * share < own
        out_ref[slot] = jnp.where(keep, latent_ref[slot] + STEP * score, 0.0)


def body(latent, margin_len, in_weight, norm_gain, qkv_weight, out_weight, final_gain, head_out):
    count = lax.axis_size("seq")
    groups = lax.axis_size("group")
    share, channels = latent.shape[1:]
    total = share * count
    width, depth = out_weight.shape
    full = width * count
    shares = min(groups, width // 16)
    high = range(0, shares, 2)

    def across(value, group_by, pairs):
        moves = [
            (g * count + i, (g + group_by) * count + j)
            for g in range(groups)
            for i, j in pairs
            if 0 <= g + group_by < groups
        ]
        return lax.ppermute(value, ("group", "seq"), moves)

    def swap(value, bits):
        return lax.ppermute(value, "group", [(g, g ^ bits) for g in range(groups)])

    def gathered(value):
        return [lax.ppermute(value, "seq", [(i, i ^ k) for i in range(count)]) for k in range(1, count)]

    turned = latent.transpose(0, 2, 1)
    packed = jnp.concatenate([latent[0], latent[1]], axis=1).astype(BF16)
    pieces = [packed] + gathered(packed)
    stacked = jnp.stack(pieces)
    following = across(stacked, -1, [(i, i) for i in range(count)])
    maps, back, part, direct, gram = pl.pallas_call(
        functools.partial(fold_kernel, shares),
        out_shape=(
            jax.ShapeDtypeStruct((width, LANES), BF16),
            jax.ShapeDtypeStruct((width, depth + LANES), BF16),
            jax.ShapeDtypeStruct((width // shares, depth + LANES), BF16),
            jax.ShapeDtypeStruct((2 * channels, depth + LANES), BF16),
            jax.ShapeDtypeStruct((channels, 2 * LANES), BF16),
        ),
        in_specs=[pl.BlockSpec(memory_space=pltpu.HBM)] * 6,
        compiler_params=limit(20),
        out_specs=(VMEM,) * 5,
        scratch_shapes=[
            pltpu.VMEM(in_weight.shape, BF16),
            pltpu.VMEM(norm_gain.shape, F32),
            pltpu.VMEM(qkv_weight.shape, BF16),
            pltpu.VMEM(out_weight.shape, BF16),
            pltpu.VMEM(final_gain.shape, F32),
            pltpu.VMEM(head_out.shape[::-1], BF16),
            pltpu.SemaphoreType.DMA((8,)),
        ],
        cost_estimate=pl.CostEstimate(flops=width * depth * 1200, bytes_accessed=8 * width * depth, transcendentals=0),
        name="fold",
    )(*[pltpu.with_memory_space_constraint(x, pltpu.HBM) for x in (in_weight, norm_gain, qkv_weight, out_weight, final_gain, head_out.T)])
    own_part = jnp.stack(gathered(part))
    far_maps = gathered(maps)
    own_width = width // QUAD * QUAD
    rest_maps = far_maps if own_width else [maps] + far_maps
    rest_width = full - own_width

    def attention(lanes):
        return pl.CostEstimate(
            flops=16 * share * total * lanes,
            bytes_accessed=4 * lanes * share,
            transcendentals=share * total * lanes // HDIM,
        )

    def scratch(lanes):
        return [
            pltpu.VMEM((lanes, total), BF16),
            pltpu.VMEM((2, 4 * share, QUAD), BF16),
            pltpu.VMEM((2, 4 * share, total), BF16),
        ]

    def attend_own(window):
        extra = [following] if window else []
        return pl.pallas_call(
            functools.partial(attend_own_kernel, count, window, own_width),
            out_shape=(
                jax.ShapeDtypeStruct((2 * share, own_width + LANES), BF16),
                jax.ShapeDtypeStruct((total, LANES), BF16),
                jax.ShapeDtypeStruct((share, LANES), BF16),
                jax.ShapeDtypeStruct((total, QUAD), BF16),
                jax.ShapeDtypeStruct((8, total), F32),
            ),
            in_specs=[SMEM] + [VMEM] * (count + len(extra) + 2),
            compiler_params=limit(24),
            out_specs=(VMEM,) * 5,
            scratch_shapes=[
                pltpu.VMEM((total, LANES), F32),
                pltpu.VMEM((OVMAX + total, LANES), F32),
                pltpu.VMEM((total, LANES), BF16),
                *scratch(max(own_width, QUAD)),
            ],
            cost_estimate=attention(max(own_width, QUAD)),
            name="attend_own",
        )(margin_len, *pieces, maps, gram, *extra)

    def attend_rest(state):
        return pl.pallas_call(
            attend_rest_kernel,
            out_shape=jax.ShapeDtypeStruct((2 * share, rest_width), BF16),
            in_specs=[VMEM] * (5 + len(rest_maps)),
            compiler_params=limit(28),
            out_specs=VMEM,
            scratch_shapes=[pltpu.VMEM((rest_width, LANES), BF16), *scratch(rest_width)],
            cost_estimate=attention(rest_width),
            name="attend_rest",
        )(gram, *state, *rest_maps)

    first, *first_state = attend_own(0)
    second, *second_state = attend_own(1)
    first_rest = attend_rest(first_state)
    second_rest = attend_rest(second_state)
    planes = [swap(own_part, bits) for bits in high[1:]]
    far = jnp.stack([own_part] + planes)
    near = swap(far, 1)
    scored = (
        jax.ShapeDtypeStruct((2, share, LANES), F32),
        jax.ShapeDtypeStruct((share // 2, LANES), BF16),
        jax.ShapeDtypeStruct((share // 2, LANES), BF16),
    )
    half = width // 2
    columns = depth + LANES
    if own_width == width and half % LANES == 0:
        near_rows = (count - 1) * half
        far_rows = width + near_rows + 2 * channels
        partial_sums = pl.pallas_call(
            functools.partial(finish_far_kernel, count, shares, list(high)),
            out_shape=jax.ShapeDtypeStruct((4 * share, columns), F32),
            in_specs=[VMEM] * 7,
            compiler_params=limit(24),
            out_specs=VMEM,
            scratch_shapes=[pltpu.VMEM((far_rows, columns), BF16)],
            cost_estimate=pl.CostEstimate(
                flops=8 * share * far_rows * columns, bytes_accessed=4 * columns * far_rows, transcendentals=0
            ),
            name="finish_far",
        )(first, first_rest, second, second_rest, direct, back, far)
        rows, *tails = pl.pallas_call(
            functools.partial(finish_near_kernel, count, shares, list(high)),
            out_shape=scored,
            in_specs=[SMEM] + [VMEM] * 4,
            compiler_params=limit(24),
            out_specs=(VMEM, VMEM, VMEM),
            scratch_shapes=[pltpu.VMEM((near_rows, columns), BF16), pltpu.VMEM((4 * share, LANES), F32)],
            cost_estimate=pl.CostEstimate(
                flops=8 * share * near_rows * columns, bytes_accessed=4 * columns * near_rows, transcendentals=0
            ),
            name="finish_near",
        )(margin_len, first_rest, second_rest, near, partial_sums)
    else:
        rows, *tails = pl.pallas_call(
            functools.partial(finish_kernel, count, shares, list(high)),
            out_shape=(
                jax.ShapeDtypeStruct((2, share, LANES), F32),
                jax.ShapeDtypeStruct((share // 2, LANES), BF16),
                jax.ShapeDtypeStruct((share // 2, LANES), BF16),
            ),
            in_specs=[SMEM] + [VMEM] * 8,
            compiler_params=limit(24),
            out_specs=(VMEM, VMEM, VMEM),
            scratch_shapes=[
                pltpu.VMEM((full + 2 * channels, depth + LANES), BF16),
                pltpu.VMEM((4 * share, LANES), F32),
            ],
            cost_estimate=pl.CostEstimate(
                flops=8 * share * full * depth, bytes_accessed=2 * full * depth, transcendentals=0
            ),
            name="finish",
        )(margin_len, first, first_rest, second, second_rest, direct, back, far, near)

    deltas = list(range((total - OVMAX) // share, count))
    received = []
    for window, group_by in ((1, 1), (0, 0)):
        received += [across(tails[window], group_by, [(i, i - d) for i in range(d, count)]) for d in deltas]
    turned = pl.pallas_call(
        functools.partial(combine_kernel, count, deltas),
        out_shape=jax.ShapeDtypeStruct(turned.shape, F32),
        in_specs=[SMEM] + [VMEM] * (2 + len(received)),
        compiler_params=limit(8),
        out_specs=VMEM,
        scratch_shapes=[pltpu.VMEM((OVMAX + total + share, LANES), F32)],
        name="combine",
    )(margin_len, turned, rows, *received)
    return turned.transpose(0, 2, 1)


def solution(mesh):
    in_specs = (
        P("group", "seq", None),
        P(),
        P(),
        P(),
        P(None, None, "seq"),
        P("seq", None),
        P(),
        P(),
    )
    out_specs = P("group", "seq", None)

    return jax.shard_map(body, mesh=mesh, in_specs=in_specs, out_specs=out_specs, check_vma=False)
```

```python
import functools
import math

import jax
import jax.numpy as jnp
from jax import lax
from jax.experimental import pallas as pl
from jax.experimental.pallas import tpu as pltpu
from jax.sharding import PartitionSpec as P

HDIM = 64
OVMAX = 512
LANES = 128
QUAD = 4 * HDIM
STEP = -0.5
F32 = jnp.float32
BF16 = jnp.bfloat16
VMEM = pl.BlockSpec(memory_space=pltpu.VMEM)
SMEM = pl.BlockSpec(memory_space=pltpu.SMEM)


def limit(mebibytes):
    return pltpu.CompilerParams(vmem_limit_bytes=mebibytes << 20)


def iota(shape, dim):
    return lax.broadcasted_iota(jnp.int32, shape, dim)


def matmul(lhs, rhs):
    return jnp.dot(lhs, rhs, preferred_element_type=F32)


def matmul_nt(lhs, rhs, precision=None):
    return lax.dot_general(lhs, rhs, (((1,), (1,)), ((), ())), precision=precision, preferred_element_type=F32)


def split(value):
    high = value.astype(BF16)
    return high, (value - high.astype(F32)).astype(BF16)


def margin_at(margin_ref, index):
    last = margin_ref.shape[0]
    length = margin_ref[jnp.clip(index, 0, last - 1)]
    return jnp.where((index >= 0) & (index < last), length, 0)


def block_of(sub, shares):
    return lax.rem(sub, 2) * (shares // 2) + sub // 2


def started(pairs, sem):
    copies = [pltpu.make_async_copy(source, target, sem.at[i]) for i, (source, target) in enumerate(pairs)]
    for copy in copies:
        copy.start()
    return copies


def folded(both, weights, channels):
    product = matmul(both, weights)
    return product[:channels] + product[channels:]


def halves(value):
    channels = value.shape[1]
    value = jnp.concatenate([value, value], axis=1)
    high, low = split(value)
    left = iota(value.shape, 1) < channels
    return jnp.where(left, high.astype(F32), low.astype(F32)).astype(BF16)


def centered_rows(in_ref):
    weight = in_ref[...].astype(F32)
    return weight - jnp.mean(weight, axis=-1, keepdims=True)


def fold_kernel(shares, in_hbm, gain_hbm, qkv_hbm, out_hbm, final_hbm, head_hbm, *refs):
    map_ref, back_ref, part_ref, direct_ref, gram_ref = refs[:5]
    in_ref, gain_ref, qkv_ref, out_ref, final_ref, head_ref, sem = refs[5:]
    pairs = [(in_hbm, in_ref), (gain_hbm, gain_ref), (qkv_hbm.at[2], qkv_ref.at[2]), (out_hbm, out_ref)]
    pairs += [(qkv_hbm.at[0], qkv_ref.at[0]), (qkv_hbm.at[1], qkv_ref.at[1])]
    copies = started(pairs + [(final_hbm, final_ref), (head_hbm, head_ref)], sem)
    copies[0].wait()
    copies[1].wait()
    centered = centered_rows(in_ref)
    channels, depth = centered.shape
    width = out_ref.shape[0]
    both = jnp.concatenate(split(centered * gain_ref[...][None, :]), axis=0)

    high, low = split(centered)
    direct_ref[:channels, :depth] = high
    direct_ref[channels:, :depth] = low
    gram = matmul_nt(jnp.concatenate([high, low], axis=0), jnp.concatenate([high, low], axis=0))
    gram = (gram[:channels] + gram[channels:]) * (1.0 / depth)
    gram = gram + pltpu.roll(gram, channels, 1)
    first, _ = split(gram)
    second, third = split(gram - first.astype(F32))
    left = iota((channels, LANES), 1) < channels
    gram_ref[:, :LANES] = jnp.where(left, first.astype(F32), second.astype(F32)).astype(BF16)
    gram_ref[:, LANES:] = jnp.where(left, third.astype(F32), 0.0).astype(BF16)

    copies[2].wait()
    values = folded(both, qkv_ref[2], channels)
    tiled = jnp.concatenate([values] * (width // HDIM), axis=0)
    same = iota((width, width), 0) // channels == iota((width, width), 1) // HDIM
    high, low = split(jnp.where(same, tiled, 0.0))
    copies[3].wait()
    back = matmul(high, out_ref[...]) + matmul(low, out_ref[...])
    back = back - jnp.mean(back, axis=-1, keepdims=True)
    back_ref[:, :depth] = back.astype(BF16)
    copies[4].wait()
    queries = folded(both, qkv_ref[0], channels)
    copies[5].wait()
    keys = folded(both, qkv_ref[1], channels)
    map_ref[...] = jnp.concatenate([queries, keys], axis=0).T.astype(BF16)

    copies[6].wait()
    copies[7].wait()
    pieces = split(back * final_ref[...][None, :]) + split(centered * final_ref[...][None, :])
    scores = matmul_nt(jnp.concatenate(pieces, axis=0), head_ref[...])
    back_ref[:, depth:] = halves(scores[:width] + scores[width : 2 * width])
    direct_ref[:channels, depth:] = halves(scores[2 * width : 2 * width + channels] + scores[2 * width + channels :])
    direct_ref[channels:, depth:] = jnp.zeros((channels, LANES), BF16)
    rows = width // shares
    sub = lax.rem(lax.axis_index("group"), shares)
    part_ref[...] = back_ref[pl.ds(pl.multiple_of(block_of(sub, shares) * rows, rows), rows), :]


def twice(tokens):
    tokens = tokens.astype(F32)
    return tokens + pltpu.roll(tokens, LANES // 2, 1)


def bend(tokens, doubled, gram_ref):
    bent = matmul(tokens[:, : gram_ref.shape[0]], gram_ref[...])
    return (bent[:, :LANES] + bent[:, LANES:]) * doubled


def variance(bent):
    return jnp.maximum(jnp.sum(bent, axis=-1, keepdims=True), 0.0) + 1e-05


def quads(maps, mine, query_eps, key_eps, right_ref, ext_ref, sum_ref, key_scr, query_scr, p_scr):
    heads_width = maps.shape[0]
    total = right_ref.shape[0]
    share = mine.shape[0]
    channels = LANES // 2
    tile = min(total, 256)
    for start in range(0, total, tile):
        keys = matmul_nt(maps, right_ref[start : start + tile]).reshape(heads_width // HDIM, HDIM, tile)
        norm = jnp.mean(keys * keys, axis=1, keepdims=True)
        keys = keys * lax.rsqrt(norm + key_eps[None, :, start : start + tile])
        key_scr[:, start : start + tile] = keys.reshape(heads_width, tile).astype(BF16)
    one_head = iota((QUAD, QUAD), 0) // HDIM == iota((QUAD, QUAD), 1) // HDIM
    spread = jnp.where(one_head, 1.0 / HDIM, 0.0).astype(BF16)
    head_of = iota((share, QUAD), 1) // HDIM
    scale = HDIM ** (-0.5) * math.log2(math.e)
    left = iota((share, LANES), 1) < channels
    for quad in range(heads_width // QUAD):
        span = slice(quad * QUAD, (quad + 1) * QUAD)
        queries = matmul_nt(mine, maps[span, :])
        norm = matmul((queries * queries).astype(BF16), spread)
        queries = (queries * lax.rsqrt(norm + query_eps)).astype(BF16)
        for head in range(4):
            query_scr[quad % 2, head * share : (head + 1) * share, :] = jnp.where(
                head_of == head, queries, jnp.zeros_like(queries)
            )
        for start in range(0, total, tile):
            scores = matmul(query_scr[quad % 2], key_scr[span, start : start + tile])
            p_scr[quad % 2, :, start : start + tile] = jnp.exp2(scores * scale).astype(BF16)
        summed = matmul(p_scr[quad % 2], ext_ref[...])
        summed = summed[:, :LANES] / summed[:, LANES:]
        for pair in range(2):
            even = summed[2 * pair * share : (2 * pair + 1) * share]
            odd = summed[(2 * pair + 1) * share : (2 * pair + 2) * share]
            at = slice(quad * QUAD + pair * LANES, quad * QUAD + (pair + 1) * LANES)
            sum_ref[:share, at] = jnp.where(left, even, pltpu.roll(odd, HDIM, 1)).astype(BF16)
            sum_ref[share:, at] = jnp.where(left, pltpu.roll(even, HDIM, 1), odd).astype(BF16)


def attend_own_kernel(count, window, own_width, margin_ref, *refs):
    piece_refs, refs = refs[:count], refs[count:]
    map_ref, gram_ref, refs = refs[0], refs[1], refs[2:]
    if window:
        next_ref, refs = refs[0], refs[1:]
    sum_ref, right_ref, mine_ref, ext_ref, eps_ref, slot_scr, next_scr, win_scr, key_scr, query_scr, p_scr = refs
    total = win_scr.shape[0]
    channels = gram_ref.shape[0]
    share = total // count
    low = total - OVMAX
    group_pos = lax.axis_index("group")
    seq_pos = lax.axis_index("seq")
    over_len = margin_at(margin_ref, 2 * group_pos + window)
    own = total - over_len

    next_scr[:OVMAX, :] = jnp.zeros((OVMAX, LANES), F32)
    for k in range(count):
        source = jnp.bitwise_xor(seq_pos, k) * share
        at = pl.ds(pl.multiple_of(source, share), share)
        after = pl.ds(pl.multiple_of(source + OVMAX, share), share)
        slot = piece_refs[k][...].astype(F32)
        slot_scr[at, :] = pltpu.roll(slot, channels, 1) if window else slot
        next_scr[after, :] = next_ref[k].astype(F32) if window else pltpu.roll(slot, channels, 1)
    left = iota((OVMAX, LANES), 1) < channels
    for start in range(0, total, OVMAX):
        rows = slot_scr[start : start + OVMAX, :]
        if start >= low:
            tail = next_scr[pl.ds(over_len + (start - low), OVMAX), :]
            rows = jnp.where(iota(rows.shape, 0) + start < own, rows, tail)
        win_scr[start : start + OVMAX, :] = jnp.where(left, rows, 0.0).astype(BF16)

    win = win_scr[...]
    mine = win_scr[pl.ds(pl.multiple_of(seq_pos * share, share), share), :]
    mine_ref[...] = mine
    mine_twice = twice(mine)
    sum_ref[:share, own_width:] = mine_twice.astype(BF16)
    sum_ref[share:, own_width:] = mine_twice.astype(BF16)
    query_eps = variance(bend(mine, mine_twice, gram_ref)) * 1e-06
    doubled = twice(win)
    bent = bend(win, doubled, gram_ref)
    ones = jnp.ones((16, LANES), BF16)
    key_eps = (jnp.maximum(matmul_nt(ones, bent.astype(BF16))[:8], 0.0) + 1e-05) * 1e-06
    eps_ref[...] = key_eps

    scaled = doubled * lax.rsqrt(variance(bent))
    counted = (iota((total, LANES), 0) >= jnp.minimum(own, total - 1)).astype(F32)
    left = iota((total, LANES), 1) < channels
    ext_ref[:, :LANES] = jnp.where(left, scaled, scaled * counted).astype(BF16)
    ext_ref[:, LANES:] = jnp.where(left, 1.0, counted).astype(BF16)
    right_ref[...] = jnp.where(left, 0.0, doubled).astype(BF16)
    if own_width:
        quads(map_ref[...], mine, query_eps, key_eps[:1], right_ref, ext_ref, sum_ref, key_scr, query_scr, p_scr)


def attend_rest_kernel(gram_ref, right_ref, mine_ref, ext_ref, eps_ref, *refs):
    map_refs, refs = refs[:-5], refs[-5:]
    sum_ref, map_scr, key_scr, query_scr, p_scr = refs
    width = map_refs[0].shape[0]
    for k, ref in enumerate(map_refs):
        map_scr[k * width : (k + 1) * width, :] = ref[...]
    mine = mine_ref[...]
    query_eps = variance(bend(mine, twice(mine), gram_ref)) * 1e-06
    maps = map_scr[...]
    quads(maps, mine, query_eps, eps_ref[:1, :], right_ref, ext_ref, sum_ref, key_scr, query_scr, p_scr)


def signed_rows(count, score, margin_ref, rows_ref, packed_first, packed_second):
    share = rows_ref.shape[1]
    total = share * count
    channels = LANES // 2
    group_pos = lax.axis_index("group")
    seq_pos = lax.axis_index("seq")
    position = iota((share, LANES), 0) + seq_pos * share
    left = iota((share // 2, LANES), 1) < channels
    for window, packed_ref in enumerate((packed_first, packed_second)):
        at = 2 * share * window
        own = total - margin_at(margin_ref, 2 * group_pos + window)
        margin = jnp.where(position >= own, score[at + share : at + 2 * share], 0.0)
        signed = score[at : at + share] - margin
        rows_ref[window] = signed
        packed_ref[...] = jnp.where(left, signed[: share // 2], signed[share // 2 :]).astype(BF16)


def finish_kernel(count, shares, high, margin_ref, *refs):
    first_ref, first_rest, second_ref, second_rest, direct_ref, back_ref, far_ref, near_ref = refs[:8]
    rows_ref, packed_first, packed_second, all_scr, square_scr = refs[8:]
    width = back_ref.shape[0]
    depth = back_ref.shape[1] - LANES
    full = width * count
    part = width // shares
    channels = direct_ref.shape[0] // 2
    group_pos = lax.axis_index("group")
    sub = lax.rem(group_pos, shares)
    all_scr[:width, :] = back_ref[...]
    all_scr[full:, :] = direct_ref[...]
    for i, m in enumerate(high):
        for near, ref in ((0, far_ref), (1, near_ref)):
            place = block_of(jnp.bitwise_xor(sub, m ^ near), shares) * part
            for k in range(1, count):
                all_scr[pl.ds(pl.multiple_of(place + k * width, part), part), :] = ref[i, k - 1]
    tile = 2 * LANES
    own = first_ref.shape[1] - LANES
    windows = ((first_ref, first_rest), (second_ref, second_rest))
    known = jnp.concatenate(
        [jnp.concatenate([ref[:, :own], rest[...], ref[:, own:]][not own :], axis=1) for ref, rest in windows], axis=0
    )
    for start in range(0, depth, tile):
        mixed = matmul(known, all_scr[:, start : start + tile])
        squares = mixed * mixed
        squares = squares[:, :LANES] + squares[:, LANES:]
        square_scr[...] = squares if start == 0 else square_scr[...] + squares
    score = matmul(known, all_scr[:, depth:])
    variance = jnp.sum(square_scr[...], axis=-1, keepdims=True) * (1.0 / depth)
    score = (score + pltpu.roll(score, channels, 1)) * lax.rsqrt(variance + 1e-05)
    signed_rows(count, score, margin_ref, rows_ref, packed_first, packed_second)


def half_known(rest_ref, count, core):
    width = rest_ref.shape[1] // (count - 1)
    half = width // 2
    starts = [pl.multiple_of(k * width + core * half, half) for k in range(count - 1)]
    return [rest_ref[:, pl.ds(start, half)] for start in starts]


def fill_half(all_scr, base, gathered_ref, sub, high, half, count):
    part = gathered_ref.shape[2]
    for i, m in enumerate(high):
        place = jnp.bitwise_xor(sub, m) // 2 * part
        for k in range(count - 1):
            all_scr[pl.ds(pl.multiple_of(base + k * half + place, part), part), :] = gathered_ref[i, k]


def finish_far_kernel(count, shares, high, *refs):
    first_ref, first_rest, second_ref, second_rest, direct_ref, back_ref, far_ref, sum_ref, all_scr = refs
    width = back_ref.shape[0]
    half = width // 2
    sub = lax.rem(lax.axis_index("group"), shares)
    core = lax.rem(sub, 2)
    all_scr[:width, :] = back_ref[...]
    fill_half(all_scr, width, far_ref, sub, high, half, count)
    all_scr[width + (count - 1) * half :, :] = direct_ref[...]
    windows = ((first_ref, first_rest), (second_ref, second_rest))
    known = jnp.concatenate(
        [
            jnp.concatenate([ref[:, :width], *half_known(rest, count, core), ref[:, width:]], axis=1)
            for ref, rest in windows
        ],
        axis=0,
    )
    columns = sum_ref.shape[1]
    for start in range(0, columns, 2 * LANES):
        at = slice(start, min(start + 2 * LANES, columns))
        sum_ref[:, at] = matmul(known, all_scr[:, at])


def finish_near_kernel(count, shares, high, margin_ref, *refs):
    first_rest, second_rest, near_ref, sum_ref, rows_ref, packed_first, packed_second, all_scr, square_scr = refs
    depth = sum_ref.shape[1] - LANES
    half = first_rest.shape[1] // (count - 1) // 2
    sub = jnp.bitwise_xor(lax.rem(lax.axis_index("group"), shares), 1)
    fill_half(all_scr, 0, near_ref, sub, high, half, count)
    core = lax.rem(sub, 2)
    known = jnp.concatenate(
        [jnp.concatenate(half_known(rest, count, core), axis=1) for rest in (first_rest, second_rest)], axis=0
    )
    for start in range(0, depth, 2 * LANES):
        at = slice(start, start + 2 * LANES)
        mixed = sum_ref[:, at] + matmul(known, all_scr[:, at])
        squares = mixed * mixed
        squares = squares[:, :LANES] + squares[:, LANES:]
        square_scr[...] = squares if start == 0 else square_scr[...] + squares
    score = sum_ref[:, depth:] + matmul(known, all_scr[:, depth:])
    variance_out = jnp.sum(square_scr[...], axis=-1, keepdims=True) * (1.0 / depth)
    score = (score + pltpu.roll(score, LANES // 2, 1)) * lax.rsqrt(variance_out + 1e-05)
    signed_rows(count, score, margin_ref, rows_ref, packed_first, packed_second)


def combine_kernel(count, deltas, margin_ref, latent_ref, rows_ref, *refs):
    out_ref, tail_scr = refs[2 * len(deltas) :]
    channels, share = latent_ref.shape[1:]
    total = share * count
    group_pos = lax.axis_index("group")
    seq_pos = lax.axis_index("seq")
    for slot in range(2):
        before = margin_at(margin_ref, 2 * group_pos + slot - 1)
        own = total - margin_at(margin_ref, 2 * group_pos + slot)
        tail_scr[...] = jnp.zeros_like(tail_scr)
        for delta, ref in zip(deltas, refs[slot * len(deltas) : (slot + 1) * len(deltas)]):
            row = (seq_pos + delta) * share - (total - OVMAX)
            for half in range(2):
                value = ref[...].astype(F32)
                value = pltpu.roll(value, channels, 1) if half else value
                at = pl.ds(pl.multiple_of(row + half * (share // 2), share // 2), share // 2)
                tail_scr[at, :] = value
        moved = tail_scr[pl.ds(OVMAX - before + seq_pos * share, share), :]
        score = (rows_ref[slot] + moved).T[:channels]
        keep = iota(score.shape, 1) + seq_pos * share < own
        out_ref[slot] = jnp.where(keep, latent_ref[slot] + STEP * score, 0.0)


def body(latent, margin_len, in_weight, norm_gain, qkv_weight, out_weight, final_gain, head_out):
    count = lax.axis_size("seq")
    groups = lax.axis_size("group")
    share, channels = latent.shape[1:]
    total = share * count
    width, depth = out_weight.shape
    full = width * count
    shares = min(groups, width // 16)
    high = range(0, shares, 2)

    def across(value, group_by, pairs):
        moves = [
            (g * count + i, (g + group_by) * count + j)
            for g in range(groups)
            for i, j in pairs
            if 0 <= g + group_by < groups
        ]
        return lax.ppermute(value, ("group", "seq"), moves)

    def swap(value, bits):
        return lax.ppermute(value, "group", [(g, g ^ bits) for g in range(groups)])

    def gathered(value):
        return [lax.ppermute(value, "seq", [(i, i ^ k) for i in range(count)]) for k in range(1, count)]

    turned = latent.transpose(0, 2, 1)
    packed = jnp.concatenate([latent[0], latent[1]], axis=1).astype(BF16)
    pieces = [packed] + gathered(packed)
    stacked = jnp.stack(pieces)
    following = across(stacked, -1, [(i, i) for i in range(count)])
    maps, back, part, direct, gram = pl.pallas_call(
        functools.partial(fold_kernel, shares),
        out_shape=(
            jax.ShapeDtypeStruct((width, LANES), BF16),
            jax.ShapeDtypeStruct((width, depth + LANES), BF16),
            jax.ShapeDtypeStruct((width // shares, depth + LANES), BF16),
            jax.ShapeDtypeStruct((2 * channels, depth + LANES), BF16),
            jax.ShapeDtypeStruct((channels, 2 * LANES), BF16),
        ),
        in_specs=[pl.BlockSpec(memory_space=pltpu.HBM)] * 6,
        compiler_params=limit(20),
        out_specs=(VMEM,) * 5,
        scratch_shapes=[
            pltpu.VMEM(in_weight.shape, BF16),
            pltpu.VMEM(norm_gain.shape, F32),
            pltpu.VMEM(qkv_weight.shape, BF16),
            pltpu.VMEM(out_weight.shape, BF16),
            pltpu.VMEM(final_gain.shape, F32),
            pltpu.VMEM(head_out.shape[::-1], BF16),
            pltpu.SemaphoreType.DMA((8,)),
        ],
        cost_estimate=pl.CostEstimate(flops=width * depth * 1200, bytes_accessed=8 * width * depth, transcendentals=0),
        name="fold",
    )(*[pltpu.with_memory_space_constraint(x, pltpu.HBM) for x in (in_weight, norm_gain, qkv_weight, out_weight, final_gain, head_out.T)])
    own_part = jnp.stack(gathered(part))
    far_maps = gathered(maps)
    own_width = width // QUAD * QUAD
    rest_maps = far_maps if own_width else [maps] + far_maps
    rest_width = full - own_width

    def attention(lanes):
        return pl.CostEstimate(
            flops=16 * share * total * lanes,
            bytes_accessed=4 * lanes * share,
            transcendentals=share * total * lanes // HDIM,
        )

    def scratch(lanes):
        return [
            pltpu.VMEM((lanes, total), BF16),
            pltpu.VMEM((2, 4 * share, QUAD), BF16),
            pltpu.VMEM((2, 4 * share, total), BF16),
        ]

    def attend_own(window):
        extra = [following] if window else []
        return pl.pallas_call(
            functools.partial(attend_own_kernel, count, window, own_width),
            out_shape=(
                jax.ShapeDtypeStruct((2 * share, own_width + LANES), BF16),
                jax.ShapeDtypeStruct((total, LANES), BF16),
                jax.ShapeDtypeStruct((share, LANES), BF16),
                jax.ShapeDtypeStruct((total, QUAD), BF16),
                jax.ShapeDtypeStruct((8, total), F32),
            ),
            in_specs=[SMEM] + [VMEM] * (count + len(extra) + 2),
            compiler_params=limit(24),
            out_specs=(VMEM,) * 5,
            scratch_shapes=[
                pltpu.VMEM((total, LANES), F32),
                pltpu.VMEM((OVMAX + total, LANES), F32),
                pltpu.VMEM((total, LANES), BF16),
                *scratch(max(own_width, QUAD)),
            ],
            cost_estimate=attention(max(own_width, QUAD)),
            name="attend_own",
        )(margin_len, *pieces, maps, gram, *extra)

    def attend_rest(state):
        return pl.pallas_call(
            attend_rest_kernel,
            out_shape=jax.ShapeDtypeStruct((2 * share, rest_width), BF16),
            in_specs=[VMEM] * (5 + len(rest_maps)),
            compiler_params=limit(28),
            out_specs=VMEM,
            scratch_shapes=[pltpu.VMEM((rest_width, LANES), BF16), *scratch(rest_width)],
            cost_estimate=attention(rest_width),
            name="attend_rest",
        )(gram, *state, *rest_maps)

    first, *first_state = attend_own(0)
    second, *second_state = attend_own(1)
    first_rest = attend_rest(first_state)
    second_rest = attend_rest(second_state)
    planes = []
    for bits in high[1:]:
        planes.append(swap(own_part, bits))
    far = jnp.stack([own_part] + planes)
    near = swap(far, 1)
    scored = (
        jax.ShapeDtypeStruct((2, share, LANES), F32),
        jax.ShapeDtypeStruct((share // 2, LANES), BF16),
        jax.ShapeDtypeStruct((share // 2, LANES), BF16),
    )
    half = width // 2
    columns = depth + LANES
    if own_width == width and half % LANES == 0:
        near_rows = (count - 1) * half
        far_rows = width + near_rows + 2 * channels
        partial_sums = pl.pallas_call(
            functools.partial(finish_far_kernel, count, shares, list(high)),
            out_shape=jax.ShapeDtypeStruct((4 * share, columns), F32),
            in_specs=[VMEM] * 7,
            compiler_params=limit(24),
            out_specs=VMEM,
            scratch_shapes=[pltpu.VMEM((far_rows, columns), BF16)],
            cost_estimate=pl.CostEstimate(
                flops=8 * share * far_rows * columns, bytes_accessed=4 * columns * far_rows, transcendentals=0
            ),
            name="finish_far",
        )(first, first_rest, second, second_rest, direct, back, far)
        rows, *tails = pl.pallas_call(
            functools.partial(finish_near_kernel, count, shares, list(high)),
            out_shape=scored,
            in_specs=[SMEM] + [VMEM] * 4,
            compiler_params=limit(24),
            out_specs=(VMEM, VMEM, VMEM),
            scratch_shapes=[pltpu.VMEM((near_rows, columns), BF16), pltpu.VMEM((4 * share, LANES), F32)],
            cost_estimate=pl.CostEstimate(
                flops=8 * share * near_rows * columns, bytes_accessed=4 * columns * near_rows, transcendentals=0
            ),
            name="finish_near",
        )(margin_len, first_rest, second_rest, near, partial_sums)
    else:
        rows, *tails = pl.pallas_call(
            functools.partial(finish_kernel, count, shares, list(high)),
            out_shape=(
                jax.ShapeDtypeStruct((2, share, LANES), F32),
                jax.ShapeDtypeStruct((share // 2, LANES), BF16),
                jax.ShapeDtypeStruct((share // 2, LANES), BF16),
            ),
            in_specs=[SMEM] + [VMEM] * 8,
            compiler_params=limit(24),
            out_specs=(VMEM, VMEM, VMEM),
            scratch_shapes=[
                pltpu.VMEM((full + 2 * channels, depth + LANES), BF16),
                pltpu.VMEM((4 * share, LANES), F32),
            ],
            cost_estimate=pl.CostEstimate(
                flops=8 * share * full * depth, bytes_accessed=2 * full * depth, transcendentals=0
            ),
            name="finish",
        )(margin_len, first, first_rest, second, second_rest, direct, back, far, near)

    deltas = list(range((total - OVMAX) // share, count))
    received = []
    for window, group_by in ((1, 1), (0, 0)):
        for d in deltas:
            received.append(across(tails[window], group_by, [(i, i - d) for i in range(d, count)]))
    turned = pl.pallas_call(
        functools.partial(combine_kernel, count, deltas),
        out_shape=jax.ShapeDtypeStruct(turned.shape, F32),
        in_specs=[SMEM] + [VMEM] * (2 + len(received)),
        compiler_params=limit(8),
        out_specs=VMEM,
        scratch_shapes=[pltpu.VMEM((OVMAX + total + share, LANES), F32)],
        name="combine",
    )(margin_len, turned, rows, *received)
    return turned.transpose(0, 2, 1)


def solution(mesh):
    in_specs = (
        P("group", "seq", None),
        P(),
        P(),
        P(),
        P(None, None, "seq"),
        P("seq", None),
        P(),
        P(),
    )
    out_specs = P("group", "seq", None)

    return jax.shard_map(body, mesh=mesh, in_specs=in_specs, out_specs=out_specs, check_vma=False)
```
